32 devices in a mesh: pa: 4 (over x, core), pb: 8 (over z, y).
Axes of the slice: x: 2, y: 2, z: 4, core: 2. Of those that a mesh axis runs over, the one named last changes fastest.
Arguments:
- point_keys: bfloat16 [4096, 768], P(('pa', 'pb')), may hold values from -7 to 7
- point_values: bfloat16 [4096, 768], P(('pa', 'pb')), may hold values from -40 to 40
- out_grad: bfloat16 [4096, 768], P(('pa', 'pb')), may hold values from -512 to 512
- decoder_norm: float32 [12, 4096], P(None, ('pa', 'pb')), as said below
- latent_query: bfloat16 [1024, 768], P(('pa', 'pb')), may hold values from -4 to 4
- latent_out: bfloat16 [1024, 768], P(('pa', 'pb')), may hold values from -5 to 5
- encoder_norm: float32 [12, 1024], replicated, as said below
Outputs:
- keys_grad: bfloat16 [4096, 768], P(('pa', 'pb'))
- values_grad: bfloat16 [4096, 768], P(('pa', 'pb'))
- latent_grad: float32 [1024, 768], P(('pa', 'pb'))
The draws below stay inside these ranges and needn't reach their ends.
Inputs may be any that keep to these rules, and one draw needn't show every extreme that they name: `decoder_norm`: each entry lies between log(1024) - 0.3 and log(1024) + 1.3. `encoder_norm`: each entry lies between log(4096) - 0.3 and log(4096) + 1.3.
All inputs are finite; a program needn't handle non-finite values.
Results may differ from the reference program's by a relative error of at most 0.004.
The reference program's roundings to bfloat16 on the way count: a program that leaves them out, or rounds other values in their place, can miss the bound.
Values may be sent and summed in bfloat16 or wider, within the bound.
No kernel may reach another device: no remote copies, remote signals or barrier semaphores. Data moves between devices by JAX's collectives and lax.ppermute only.
A program may use at most 64 MiB of HBM per device.

```python
import math
import jax
import jax.numpy as jnp
from jax import lax

HEADS = 12
HEAD_DIM = 64
LATENTS = 1024
TOK_DEV = 128
D = 768
POINTS = 4096


def shared_queries(key):
    raw = jnp.clip(jax.random.normal(jax.random.fold_in(key, 51), (LATENTS, D), jnp.float32), -3.5, 3.5)
    raw = raw.reshape(LATENTS, HEADS, HEAD_DIM)
    length = jnp.sqrt(jnp.sum(raw * raw, axis=2, keepdims=True)) + 1e-06
    unit = raw * (math.sqrt(HEAD_DIM) / length)
    return jnp.clip(unit.reshape(LATENTS, D), -4.0, 4.0)


def draw_latent_query(key, part):
    return shared_queries(key).astype(jnp.bfloat16)


def draw_point_keys(key, part):
    groups = POINTS // TOK_DEV
    per_owner = LATENTS // groups
    queries = shared_queries(key)
    positions = jnp.arange(POINTS, dtype=jnp.int32)
    device = positions // TOK_DEV
    local = positions % TOK_DEV
    offsets = jax.random.randint(jax.random.fold_in(key, 52), (groups,), 1, groups, dtype=jnp.int32)
    far_owner = (device + groups // 2) % groups
    other_owner = (device + offsets[device]) % groups
    owner = jnp.where(local % 2 == 0, far_owner, other_owner)
    pick = jax.random.randint(jax.random.fold_in(key, 53), (POINTS,), 0, per_owner, dtype=jnp.int32)
    target = (owner * per_owner + pick).astype(jnp.int32)
    aligned = queries[target]
    noise = jnp.clip(jax.random.normal(jax.random.fold_in(key, 54), (POINTS, D), jnp.float32), -4.0, 4.0)
    mixed = 0.6 * noise + 0.8 * aligned
    return jnp.clip(mixed, -7.0, 7.0).astype(jnp.bfloat16)


def draw_point_values(key, part):
    base = jnp.clip(jax.random.normal(jax.random.fold_in(key, 11), (POINTS, D), jnp.float32), -4.0, 4.0)
    rising = 1.0 + 2.0 * jnp.arange(POINTS, dtype=jnp.float32)[:, None] / POINTS
    row_scale = jnp.exp(jax.random.uniform(jax.random.fold_in(key, 12), (POINTS, 1), jnp.float32, 0.0, math.log(10.0))) / 3.0
    return jnp.clip(base * rising * row_scale, -40.0, 40.0).astype(jnp.bfloat16)


def draw_out_grad(key, part):
    scale_factor = LATENTS // 8
    base = jnp.clip(jax.random.normal(jax.random.fold_in(key, 23), (POINTS, D), jnp.float32), -4.0, 4.0)
    return (base * scale_factor).astype(jnp.bfloat16)


def draw_decoder_norm(key, part):
    spread = jax.random.uniform(jax.random.fold_in(key, 32), (HEADS, POINTS), jnp.float32, 0.0, 1.0)
    return (math.log(LATENTS) + spread).astype(jnp.float32)


def draw_encoder_norm(key, part):
    spread = jax.random.uniform(jax.random.fold_in(key, 42), (HEADS, LATENTS), jnp.float32, 0.0, 1.0)
    return (math.log(POINTS) + spread).astype(jnp.float32)


def levels(key, extent, shards, smallest, top_value):
    factor_of = 1.0
    for position, parts in shards:
        steps = jax.random.uniform(jax.random.fold_in(jax.random.fold_in(key, 6), position), (parts,), jnp.float32, smallest / len(shards), top_value / len(shards))
        factor_of = factor_of * jnp.repeat(jnp.exp(steps), extent[position] // parts).reshape((-1,) + (1,) * (len(extent) - 1 - position))
    return factor_of


def centred(own_key, dims, width, bound, split=(), kind=jnp.bfloat16):
    array = width * jax.random.normal(own_key, dims, jnp.float32)
    if split:
        array = array * levels(own_key, dims, split, -0.22, 0.18)
    return jnp.clip(array, -bound, bound).astype(kind)


def setup_inputs(seed: int = 0) -> dict:
    keys = jax.random.split(jax.random.key(seed), 8)
    point_keys = draw_point_keys(jax.random.fold_in(keys[7], 71), 0)
    point_values = draw_point_values(jax.random.fold_in(keys[7], 71), 0)
    out_grad = draw_out_grad(jax.random.fold_in(keys[7], 71), 0)
    decoder_norm = draw_decoder_norm(jax.random.fold_in(keys[7], 71), 0)
    latent_query = draw_latent_query(jax.random.fold_in(keys[7], 71), 0)
    latent_out = centred(keys[5], (LATENTS, D), 1.0, 5.0, ((0, 32),))
    encoder_norm = draw_encoder_norm(jax.random.fold_in(keys[7], 71), 0)
    return {"point_keys": point_keys, "point_values": point_values, "out_grad": out_grad, "decoder_norm": decoder_norm, "latent_query": latent_query, "latent_out": latent_out, "encoder_norm": encoder_norm}


PRECISION_MAXIMUM = lax.Precision.HIGHEST


def divide_heads(block):
    return block.astype(jnp.float32).reshape(block.shape[0], HEADS, HEAD_DIM)


def rounded_portion(block):
    return lax.optimization_barrier(block.astype(jnp.bfloat16)).astype(jnp.float32)


def reference(point_keys, point_values, out_grad, decoder_norm, latent_query, latent_out, encoder_norm):
    scale_factor = HEAD_DIM ** -0.5
    latent_head_rows = divide_heads(latent_query)
    output_heads = divide_heads(latent_out)
    blocks = POINTS // TOK_DEV
    key_blocks = point_keys.reshape(blocks, TOK_DEV, D)
    value_blocks = point_values.reshape(blocks, TOK_DEV, D)
    grad_blocks = out_grad.reshape(blocks, TOK_DEV, D)
    norm_blocks = decoder_norm.reshape(HEADS, blocks, TOK_DEV).transpose(1, 0, 2)

    def scores_of(key_tile_block):
        return jnp.einsum("cxt,ext->xce", divide_heads(key_tile_block), latent_head_rows, precision=PRECISION_MAXIMUM) * scale_factor

    def pass_one(state, inputs):
        key_tile_block, grad_block, norm_block = inputs
        key_head_rows = divide_heads(key_tile_block)
        gradient_heads = divide_heads(grad_block)
        decoder_weights = jnp.exp(scores_of(key_tile_block) - norm_block[:, :, None])
        decoder_gradient = jnp.einsum("cxt,ext->xce", gradient_heads, output_heads, precision=PRECISION_MAXIMUM)
        row_total = jnp.sum(decoder_weights * decoder_gradient, axis=2, keepdims=True)
        decoder_scores_grad = rounded_portion(decoder_weights * (decoder_gradient - row_total))
        mixing_piece = jnp.einsum("lzb,zly->bly", rounded_portion(decoder_weights), gradient_heads, precision=PRECISION_MAXIMUM)
        query_portion = jnp.einsum("lzb,zly->bly", decoder_scores_grad, key_head_rows, precision=PRECISION_MAXIMUM) * scale_factor
        key_portion = jnp.einsum("qjx,xqi->jqi", decoder_scores_grad, latent_head_rows, precision=PRECISION_MAXIMUM) * scale_factor
        return (state[0] + mixing_piece, state[1] + query_portion), key_portion

    blank = jnp.zeros((LATENTS, HEADS, HEAD_DIM), jnp.float32)
    (mix_grad, query_grad), key_decoder = lax.scan(pass_one, (blank, blank), (key_blocks, grad_blocks, norm_blocks))
    mixing_portion = rounded_portion(mix_grad)

    def encoder_of(key_tile_block, value_tile_block):
        encoder = jnp.exp(scores_of(key_tile_block) - encoder_norm[:, None, :])
        encoder_gradient = jnp.einsum("cxt,ext->xce", divide_heads(value_tile_block), mixing_portion, precision=PRECISION_MAXIMUM)
        return encoder, encoder_gradient

    def pass_two(state, inputs):
        key_tile_block, value_tile_block = inputs
        encoder, encoder_gradient = encoder_of(key_tile_block, value_tile_block)
        encoder_portion = rounded_portion(encoder)
        value_portion = jnp.einsum("qjx,xqi->jqi", encoder_portion, mixing_portion, precision=PRECISION_MAXIMUM)
        return state + jnp.sum(encoder_portion * encoder_gradient, axis=1), value_portion.astype(jnp.bfloat16)

    column_total, value_grad = lax.scan(pass_two, jnp.zeros((HEADS, LATENTS), jnp.float32), (key_blocks, value_blocks))

    def pass_three(state, inputs):
        key_tile_block, value_tile_block, key_before = inputs
        encoder, encoder_gradient = encoder_of(key_tile_block, value_tile_block)
        encoder_scores_grad = rounded_portion(encoder * (encoder_gradient - column_total[:, None, :]))
        query_portion = jnp.einsum("lzb,zly->bly", encoder_scores_grad, divide_heads(key_tile_block), precision=PRECISION_MAXIMUM) * scale_factor
        key_portion = jnp.einsum("qjx,xqi->jqi", encoder_scores_grad, latent_head_rows, precision=PRECISION_MAXIMUM) * scale_factor
        return state + query_portion, (key_before + key_portion).astype(jnp.bfloat16)

    query_grad, key_grad = lax.scan(pass_three, query_grad, (key_blocks, value_blocks, key_decoder))
    return key_grad.reshape(POINTS, D), value_grad.reshape(POINTS, D), query_grad.reshape(LATENTS, D)
```

```python
import math

import jax
import jax.numpy as jnp
from jax import lax
from jax.experimental import pallas as pl
from jax.experimental.pallas import tpu as pltpu
from jax.sharding import PartitionSpec as P


HEADS = 12
HEAD_DIM = 64
LANES = 128
AXES = ("pa", "pb")
MOST_IN_PLANE = 16
GROUPS = 4
VMEM_BYTES = 20 * 2**20
LOG2E = math.log2(math.e)


class Plan:
    def __init__(self, npa, npb, rows, lat_rows, width):
        self.npa, self.npb = npa, npb
        self.fast = npb // GROUPS
        self.plane = npa * self.fast
        self.rows, self.lat_rows, self.width = rows, lat_rows, width
        self.heads = HEADS // GROUPS
        self.cols = self.heads * HEAD_DIM
        self.points = rows * GROUPS
        self.block = lat_rows * GROUPS
        self.latents = self.block * self.plane
        self.pts_cols = 3 * self.cols + HEAD_DIM
        self.ct_rows = self.cols + 16

    @staticmethod
    def fits(npa, npb, rows, lat_rows, width):
        def power(v):
            return v > 0 and v & (v - 1) == 0

        return (
            power(npa)
            and power(npb)
            and npb % GROUPS == 0
            and npa * npb // GROUPS <= MOST_IN_PLANE
            and lat_rows * GROUPS == LANES
            and rows % LANES == 0
            and width == HEADS * HEAD_DIM
        )

    def exchange(self, value, over_group, step):
        pairs = []
        for a in range(self.npa):
            for b in range(self.npb):
                z, f = divmod(b, self.fast)
                if over_group:
                    a2, z2, f2 = a, z ^ step, f
                else:
                    a2, z2, f2 = a ^ (step // self.fast), z, f ^ (step % self.fast)
                pairs.append((a * self.npb + b, a2 * self.npb + z2 * self.fast + f2))
        return lax.ppermute(value, AXES, pairs)


def vmem():
    return pl.BlockSpec(memory_space=pltpu.VMEM)


def call(kernel, outs, args, scratch=(), flops=0):
    nbytes = sum(a.size * a.dtype.itemsize for a in args)
    nbytes += sum(math.prod(o.shape) * o.dtype.itemsize for o in outs)
    return pl.pallas_call(
        kernel,
        out_shape=tuple(outs),
        in_specs=[vmem()] * len(args),
        out_specs=tuple(vmem() for _ in outs),
        scratch_shapes=list(scratch),
        cost_estimate=pl.CostEstimate(flops=flops, bytes_accessed=nbytes, transcendentals=flops // 256),
        compiler_params=pltpu.CompilerParams(vmem_limit_bytes=VMEM_BYTES),
    )(*args)


def shaped(shape, dtype):
    return jax.ShapeDtypeStruct(shape, dtype)


def by_group(pieces, z):
    out = list(pieces)
    bit = 1
    while bit < len(out):
        on = (z & bit) != 0
        out = [jnp.where(on, out[g ^ bit], out[g]) for g in range(len(out))]
        bit *= 2
    return out


def group_index(plan):
    return lax.axis_index("pb") // plan.fast


def split3(value):
    hi = value.astype(jnp.bfloat16).astype(jnp.float32)
    rest = value - hi
    mid = rest.astype(jnp.bfloat16).astype(jnp.float32)
    return hi, mid, rest - mid


def nn(a, b):
    return lax.dot_general(a, b, (((1,), (0,)), ((), ())), preferred_element_type=jnp.float32)


def nt(a, b):
    return lax.dot_general(a, b, (((1,), (1,)), ((), ())), preferred_element_type=jnp.float32)


def turned(block):
    return block.astype(jnp.float32).T.astype(block.dtype)


def pack_latents(plan, query, out):
    def kernel(q_ref, o_ref, *outs):
        z = group_index(plan)
        q, o = q_ref[...].astype(jnp.float32), o_ref[...].astype(jnp.float32)
        c = plan.cols
        pieces = by_group(
            [
                jnp.concatenate([q[:, g * c : (g + 1) * c], o[:, g * c : (g + 1) * c]], axis=1)
                for g in range(GROUPS)
            ],
            z,
        )
        for ref, piece in zip(outs, pieces, strict=True):
            ref[...] = piece.astype(jnp.bfloat16)

    outs = [shaped((plan.lat_rows, 2 * plan.cols), jnp.bfloat16)] * GROUPS
    return call(kernel, outs, (query, out))


def pack_points(plan, keys, grads, values, norm):
    def kernel(k_ref, g_ref, v_ref, n_ref, *outs):
        z = group_index(plan)
        c, hs = plan.cols, plan.heads
        for first, ref in ((0, k_ref), (1, g_ref), (2, v_ref)):
            whole = ref[...].astype(jnp.float32)
            pieces = by_group([whole[:, g * c : (g + 1) * c] for g in range(GROUPS)], z)
            for out, piece in zip(outs, pieces, strict=True):
                out[:, first * c : (first + 1) * c] = piece.astype(jnp.bfloat16)
        norms = by_group([n_ref[g * hs : (g + 1) * hs, :] for g in range(GROUPS)], z)
        for out, norm_rows in zip(outs, norms, strict=True):
            fill = jnp.zeros((HEAD_DIM - 3 * hs, plan.rows), jnp.float32)
            stack = jnp.concatenate([*split3(norm_rows), fill], axis=0)
            out[:, 3 * c :] = stack.T.astype(jnp.bfloat16)

    outs = [shaped((plan.rows, plan.pts_cols), jnp.bfloat16)] * GROUPS
    return call(kernel, outs, (keys, grads, values, norm))


def order_norm(plan, norm):
    def kernel(n_ref, out_ref):
        z = group_index(plan)
        member = lax.axis_index("pa") * plan.npb + lax.axis_index("pb")
        hs, m = plan.heads, plan.latents
        rows = by_group([n_ref[g * hs : (g + 1) * hs, :] for g in range(GROUPS)], z)[0]
        fill = jnp.zeros((16 - 3 * hs, m), jnp.float32)
        stack = jnp.concatenate([*split3(rows), fill], axis=0).astype(jnp.bfloat16)
        lane = lax.broadcasted_iota(jnp.int32, (1, m), 1)
        inner, j, k = lane % plan.lat_rows, (lane // plan.lat_rows) % GROUPS, lane // plan.block
        owner = (k // plan.fast) * plan.npb + j * plan.fast + k % plan.fast
        source = (owner ^ member) * plan.lat_rows + inner
        total = jnp.zeros((16, m), jnp.float32)
        step = 256
        for start in range(0, m, step):
            row = lax.broadcasted_iota(jnp.int32, (step, m), 0) + start
            chosen = jnp.where(row == source, 1.0, 0.0).astype(jnp.bfloat16)
            total = total + nn(stack[:, start : start + step], chosen)
        out_ref[0:hs, :] = (total[:hs] + total[hs : 2 * hs]) + total[2 * hs : 3 * hs]

    return call(kernel, [shaped((plan.heads, plan.latents), jnp.float32)], (norm,))[0]


def turn_latents(plan, slots):
    def kernel(*refs):
        *ins, out = refs
        out[...] = turned(jnp.concatenate([r[...] for r in ins], axis=0))

    outs = [shaped((2 * plan.cols, plan.block), jnp.bfloat16)]
    return call(kernel, outs, slots)[0]


def norm_column(plan, pts, head):
    base, hs = 3 * plan.cols, plan.heads
    parts = [
        pts[:, base + i * hs + head : base + i * hs + head + 1].astype(jnp.float32) for i in range(3)
    ]
    return (parts[0] + parts[1]) + parts[2]


def first_pass(plan, lats, pts, norm):
    n_lat, n_pts = len(lats), len(pts)
    c, m = plan.cols, plan.latents

    def kernel(*refs):
        lat_refs, pts_refs, norm_ref = refs[:n_lat], refs[n_lat : n_lat + n_pts], refs[n_lat + n_pts]
        outs = refs[n_lat + n_pts + 1 : -4]
        query, sides, dec, enc = refs[-4:]
        for k, ref in enumerate(lat_refs):
            query[:, k * plan.block : (k + 1) * plan.block] = ref[:c, :]
        for j, ref in enumerate(pts_refs):
            sides[:, j * plan.rows : (j + 1) * plan.rows] = turned(ref[:, c : 3 * c])
        for h in range(plan.heads):
            mine = slice(h * HEAD_DIM, (h + 1) * HEAD_DIM)
            enc_norm = norm_ref[h : h + 1, :] * LOG2E
            for j, ref in enumerate(pts_refs):
                scores = nn(ref[:, mine], query[mine, :]) * (HEAD_DIM**-0.5 * LOG2E)
                rows = slice(j * plan.rows, (j + 1) * plan.rows)
                dec_norm = norm_column(plan, ref, h) * LOG2E
                dec[rows, :] = jnp.exp2(scores - dec_norm).astype(jnp.bfloat16)
                enc[rows, :] = jnp.exp2(scores - enc_norm).astype(jnp.bfloat16)
            below = slice(c + h * HEAD_DIM, c + (h + 1) * HEAD_DIM)
            mix = nn(sides[mine, :], dec[...])
            weighted = nn(sides[below, :], enc[...])
            for k, out in enumerate(outs):
                lanes = slice(k * plan.block, (k + 1) * plan.block)
                out[mine, :] = mix[:, lanes]
                out[below, :] = weighted[:, lanes]

    outs = [shaped((2 * c, plan.block), jnp.float32)] * plan.plane
    scratch = [
        pltpu.VMEM((c, m), jnp.bfloat16),
        pltpu.VMEM((2 * c, plan.points), jnp.bfloat16),
        pltpu.VMEM((plan.points, m), jnp.bfloat16),
        pltpu.VMEM((plan.points, m), jnp.bfloat16),
    ]
    flops = 6 * plan.points * m * c
    return call(kernel, outs, (*lats, *pts, norm), scratch, flops)


def decoder_pass(plan, lats, pts, heads):
    n_lat = len(lats)
    c, m = plan.cols, plan.latents

    def kernel(*refs):
        lat_refs, pts_refs = refs[:n_lat], refs[n_lat:-5]
        key_ref, lat_ref = refs[-5:-3]
        both, keys_t, ds = refs[-3:]
        for k, ref in enumerate(lat_refs):
            both[:, k * plan.block : (k + 1) * plan.block] = ref[...]
        for j, ref in enumerate(pts_refs):
            keys_t[:, j * plan.rows : (j + 1) * plan.rows] = turned(ref[:, :c])
        for at, h in enumerate(heads):
            mine = slice(h * HEAD_DIM, (h + 1) * HEAD_DIM)
            put = slice(at * HEAD_DIM, (at + 1) * HEAD_DIM)
            other = slice(c + h * HEAD_DIM, c + (h + 1) * HEAD_DIM)
            for j, ref in enumerate(pts_refs):
                rows = slice(j * plan.rows, (j + 1) * plan.rows)
                scores = nn(ref[:, mine], both[mine, :]) * (HEAD_DIM**-0.5 * LOG2E)
                dec = jnp.exp2(scores - norm_column(plan, ref, h) * LOG2E)
                grad = nn(ref[:, other], both[other, :])
                total = jnp.sum(dec * grad, axis=1, keepdims=True)
                tile = (dec * (grad - total)).astype(jnp.bfloat16)
                ds[rows, :] = tile
                key_ref[rows, put] = nt(tile, both[mine, :])
            lat_ref[put, :] = nn(keys_t[mine, :], ds[...])

    width = len(heads) * HEAD_DIM
    outs = [shaped((plan.points, width), jnp.float32), shaped((width, m), jnp.float32)]
    scratch = [
        pltpu.VMEM((2 * c, m), jnp.bfloat16),
        pltpu.VMEM((c, plan.points), jnp.bfloat16),
        pltpu.VMEM((plan.points, m), jnp.bfloat16),
    ]
    flops = 8 * plan.points * m * width
    return call(kernel, outs, (*lats, *pts), scratch, flops)


def reduce_mix(plan, parts):
    c, hs = plan.cols, plan.heads

    def kernel(*refs):
        *ins, out = refs
        total = ins[0][...]
        for ref in ins[1:]:
            total = total + ref[...]
        half = total[:c].astype(jnp.bfloat16)
        out[:c, :] = half
        product = half.astype(jnp.float32) * total[c:]
        sums = [
            jnp.sum(product[h * HEAD_DIM : (h + 1) * HEAD_DIM], axis=0, keepdims=True) for h in range(hs)
        ]
        fill = jnp.zeros((16 - 3 * hs, plan.block), jnp.float32)
        stack = jnp.concatenate([*split3(jnp.concatenate(sums, axis=0)), fill], axis=0)
        out[c:, :] = stack.astype(jnp.bfloat16)

    outs = [shaped((plan.ct_rows, plan.block), jnp.bfloat16)]
    return call(kernel, outs, parts)[0]


def encoder_pass(plan, lats, pts, norm, mixes, before):
    places = [(part, at) for part, (heads, _) in enumerate(before) for at in range(len(heads))]
    n_lat, n_pts, n_mix = len(lats), len(pts), len(mixes)
    c, m, hs = plan.cols, plan.latents, plan.heads

    def kernel(*refs):
        refs = list(refs)

        def take(n):
            got = refs[:n]
            del refs[:n]
            return got

        lat_refs, pts_refs = take(n_lat), take(n_pts)
        (norm_ref,) = take(1)
        mix_refs = take(n_mix)
        parts_in = [take(2) for _ in before]
        pts_outs, lat_outs = take(n_pts), take(n_lat)
        query, mix, keys_t, ds = refs
        for k, ref in enumerate(lat_refs):
            query[:, k * plan.block : (k + 1) * plan.block] = ref[:c, :]
        for k, ref in enumerate(mix_refs):
            mix[:, k * plan.block : (k + 1) * plan.block] = ref[...]
        for j, ref in enumerate(pts_refs):
            keys_t[:, j * plan.rows : (j + 1) * plan.rows] = turned(ref[:, :c])
        tail = mix[c:, :].astype(jnp.float32)
        columns = (tail[:hs] + tail[hs : 2 * hs]) + tail[2 * hs : 3 * hs]
        for h in range(plan.heads):
            mine = slice(h * HEAD_DIM, (h + 1) * HEAD_DIM)
            third = slice(2 * c + h * HEAD_DIM, 2 * c + (h + 1) * HEAD_DIM)
            enc_norm = norm_ref[h : h + 1, :] * LOG2E
            column = columns[h : h + 1, :]
            part, at = places[h]
            key_in, lat_in = parts_in[part]
            put = slice(at * HEAD_DIM, (at + 1) * HEAD_DIM)
            for j, ref in enumerate(pts_refs):
                rows = slice(j * plan.rows, (j + 1) * plan.rows)
                scores = nn(ref[:, mine], query[mine, :]) * (HEAD_DIM**-0.5 * LOG2E)
                enc = jnp.exp2(scores - enc_norm)
                grad = nn(ref[:, third], mix[mine, :])
                tile = (enc * (grad - column)).astype(jnp.bfloat16)
                ds[rows, :] = tile
                key = (key_in[rows, put] + nt(tile, query[mine, :])) * HEAD_DIM**-0.5
                pts_outs[j][:, mine] = key.astype(jnp.bfloat16)
                value = nt(enc.astype(jnp.bfloat16), mix[mine, :])
                pts_outs[j][:, c + h * HEAD_DIM : c + (h + 1) * HEAD_DIM] = value.astype(jnp.bfloat16)
            lat = (lat_in[put, :] + nn(keys_t[mine, :], ds[...])) * HEAD_DIM**-0.5
            for k, out in enumerate(lat_outs):
                out[mine, :] = lat[:, k * plan.block : (k + 1) * plan.block]

    outs = [shaped((plan.rows, 2 * c), jnp.bfloat16)] * n_pts
    outs += [shaped((c, plan.block), jnp.float32)] * n_lat
    scratch = [
        pltpu.VMEM((c, m), jnp.bfloat16),
        pltpu.VMEM((plan.ct_rows, m), jnp.bfloat16),
        pltpu.VMEM((c, plan.points), jnp.bfloat16),
        pltpu.VMEM((plan.points, m), jnp.bfloat16),
    ]
    flops = 10 * plan.points * m * c
    args = (*lats, *pts, norm, *mixes, *(a for _, part in before for a in part))
    got = call(kernel, outs, args, scratch, flops)
    return got[:n_pts], got[n_pts:]


def add_pairs(mine, theirs):
    def kernel(*refs):
        n = len(mine)
        for a, b, out in zip(refs[:n], refs[n : 2 * n], refs[2 * n :], strict=True):
            out[...] = a[...] + b[...]

    outs = [shaped(a.shape, a.dtype) for a in mine]
    return call(kernel, outs, (*mine, *theirs))


def reduce_latents(plan, parts):
    def kernel(*refs):
        ins, outs = refs[: len(parts)], refs[len(parts) :]
        total = ins[0][...]
        for ref in ins[1:]:
            total = total + ref[...]
        total = total.T
        for j, out in enumerate(outs):
            out[...] = total[j * plan.lat_rows : (j + 1) * plan.lat_rows]

    outs = [shaped((plan.lat_rows, plan.cols), jnp.float32)] * GROUPS
    return call(kernel, outs, parts)


def place_points(plan, slots):
    def kernel(*refs):
        ins, (key_out, value_out) = refs[:GROUPS], refs[GROUPS:]
        z = group_index(plan)
        c = plan.cols
        pieces = by_group([r[...].astype(jnp.float32) for r in ins], z)
        for g, piece in enumerate(pieces):
            key_out[:, g * c : (g + 1) * c] = piece[:, :c].astype(jnp.bfloat16)
            value_out[:, g * c : (g + 1) * c] = piece[:, c:].astype(jnp.bfloat16)

    outs = [shaped((plan.rows, plan.width), jnp.bfloat16)] * 2
    return call(kernel, outs, slots)


def place_latents(plan, slots):
    def kernel(*refs):
        *ins, out = refs
        pieces = by_group([r[...] for r in ins], group_index(plan))
        for g, piece in enumerate(pieces):
            out[:, g * plan.cols : (g + 1) * plan.cols] = piece

    outs = [shaped((plan.lat_rows, plan.width), jnp.float32)]
    return call(kernel, outs, slots)[0]


def grouped(
    plan, point_keys, point_values, out_grad, decoder_norm, latent_query, latent_out, encoder_norm
):
    def over_group(slots):
        return (slots[0], *(plan.exchange(s, True, j) for j, s in enumerate(slots) if j))

    def sum_cores(blocks):
        near = [k for k in range(plan.plane) if not k & plan.fast]
        theirs = [plan.exchange(blocks[k | plan.fast], False, plan.fast) for k in near]
        return near, add_pairs([blocks[k] for k in near], theirs)

    def from_chips(near, blocks):
        return [b if k == 0 else plan.exchange(b, False, k) for k, b in zip(near, blocks, strict=True)]

    def to_plane(block):
        got = {0: block}
        for k in range(1, plan.plane):
            if not k & plan.fast:
                got[k] = plan.exchange(block, False, k)
        for k in range(plan.plane):
            if k & plan.fast:
                got[k] = plan.exchange(got[k ^ plan.fast], False, plan.fast)
        return tuple(got[k] for k in range(plan.plane))

    lat_slots = over_group(pack_latents(plan, latent_query, latent_out))
    pts = pack_points(plan, point_keys, out_grad, point_values, decoder_norm)
    pts = over_group(pts)
    norm = order_norm(plan, encoder_norm)
    lats = to_plane(turn_latents(plan, lat_slots))
    cores = sum_cores(first_pass(plan, lats, pts, norm))
    early, late = tuple(range(plan.heads))[:-1], tuple(range(plan.heads))[-1:]
    before = [(early, decoder_pass(plan, lats, pts, early))]
    sums = from_chips(*cores)
    before.append((late, decoder_pass(plan, lats, pts, late)))
    mixes = to_plane(reduce_mix(plan, sums))
    pts_out, lat_out = encoder_pass(plan, lats, pts, norm, mixes, before)
    lat_out = from_chips(*sum_cores(lat_out))
    pts_out = over_group(pts_out)
    lat_rows = over_group(reduce_latents(plan, lat_out))
    keys_grad, values_grad = place_points(plan, pts_out)
    return keys_grad, values_grad, place_latents(plan, lat_rows)


def column(block, current):
    return lax.dynamic_slice_in_dim(block, current * HEAD_DIM, HEAD_DIM, 1)


def put_head(total, piece, current):
    return lax.dynamic_update_slice_in_dim(total, piece, current * HEAD_DIM, 1)


def add_head(total, piece, current):
    return put_head(total, column(total, current) + piece, current)


def across(left, right):
    return lax.dot_general(
        left, right, (((1,), (1,)), ((), ())), preferred_element_type=jnp.float32
    )


def down_rows(left, right):
    return lax.dot_general(
        left, right, (((0,), (0,)), ((), ())), preferred_element_type=jnp.float32
    )


def gathered(
    point_keys, point_values, out_grad, decoder_norm, latent_query, latent_out, encoder_norm
):
    scale_factor = HEAD_DIM ** (-0.5)
    lat_all, out_all = (
        lax.all_gather(latent_query, ("pa", "pb"), axis=0, tiled=True),
        lax.all_gather(latent_out, ("pa", "pb"), axis=0, tiled=True),
    )
    point_rows = point_keys.shape[0]
    latent_rows = lat_all.shape[0]
    width = point_keys.shape[1]

    def encoder_row(current):
        return lax.dynamic_slice_in_dim(encoder_norm, current, 1, 0)

    def pass_one(current, state):
        mix_acc, query_acc, key_acc, weighted_acc = state
        key_head = column(point_keys, current)
        grad_head = column(out_grad, current)
        lat_head = column(lat_all, current)
        scores = across(key_head, lat_head) * scale_factor
        decoder_weights = jnp.exp(scores - lax.dynamic_slice_in_dim(decoder_norm, current, 1, 0).T)
        decoder_gradient = across(grad_head, column(out_all, current))
        row_total = jnp.sum(decoder_weights * decoder_gradient, axis=1, keepdims=True)
        decoder_scores_grad = (decoder_weights * (decoder_gradient - row_total)).astype(
            jnp.bfloat16
        )
        mix_acc = put_head(
            mix_acc, down_rows(decoder_weights.astype(jnp.bfloat16), grad_head), current
        )
        query_acc = put_head(
            query_acc, down_rows(decoder_scores_grad, key_head) * scale_factor, current
        )
        key_acc = put_head(
            key_acc,
            jnp.dot(decoder_scores_grad, lat_head, preferred_element_type=jnp.float32)
            * scale_factor,
            current,
        )
        return (mix_acc, query_acc, key_acc, weighted_acc)

    weighted_blank = jnp.zeros((1, 1), jnp.float32)
    latent_blank = jnp.zeros((latent_rows, width), jnp.float32)
    begin = (
        latent_blank,
        latent_blank,
        jnp.zeros((point_rows, width), jnp.float32),
        weighted_blank,
    )
    mix_acc, query_acc, key_acc, _ = lax.fori_loop(0, HEADS, pass_one, begin)
    mix_grad = lax.psum(mix_acc, ("pa", "pb"))
    mixing_portion = mix_grad.astype(jnp.bfloat16)

    def pass_two(current, state):
        partial_rows, value_acc = state
        scores = across(column(point_keys, current), column(lat_all, current)) * scale_factor
        encoder_portion = jnp.exp(scores - encoder_row(current)).astype(jnp.bfloat16)
        mix_head = column(mixing_portion, current)
        encoder_gradient = across(column(point_values, current), mix_head)
        sums = jnp.sum(encoder_portion.astype(jnp.float32) * encoder_gradient, axis=0)[None, :]
        partial_rows = lax.dynamic_update_slice_in_dim(partial_rows, sums, current, 0)
        value_acc = put_head(
            value_acc,
            jnp.dot(encoder_portion, mix_head, preferred_element_type=jnp.float32),
            current,
        )
        return (partial_rows, value_acc)

    partial_rows, value_acc = lax.fori_loop(
        0,
        HEADS,
        pass_two,
        (jnp.zeros((HEADS, latent_rows), jnp.float32), jnp.zeros((point_rows, width), jnp.float32)),
    )
    column_total = lax.psum(partial_rows, ("pa", "pb"))

    def pass_three(current, state):
        query_acc, key_acc, value_acc = state
        key_head = column(point_keys, current)
        lat_head = column(lat_all, current)
        mix_head = column(mixing_portion, current)
        scores = across(key_head, lat_head) * scale_factor
        encoder = jnp.exp(scores - encoder_row(current))
        encoder_gradient = across(column(point_values, current), mix_head)
        encoder_scores_grad = (
            encoder * (encoder_gradient - lax.dynamic_slice_in_dim(column_total, current, 1, 0))
        ).astype(jnp.bfloat16)
        query_acc = add_head(
            query_acc, down_rows(encoder_scores_grad, key_head) * scale_factor, current
        )
        key_acc = add_head(
            key_acc,
            jnp.dot(encoder_scores_grad, lat_head, preferred_element_type=jnp.float32)
            * scale_factor,
            current,
        )
        return (query_acc, key_acc, value_acc)

    query_acc, key_acc, value_acc = lax.fori_loop(
        0, HEADS, pass_three, (query_acc, key_acc, value_acc)
    )
    latent_grad = lax.psum_scatter(query_acc, ("pa", "pb"), scatter_dimension=0, tiled=True)
    return (key_acc.astype(jnp.bfloat16), value_acc.astype(jnp.bfloat16), latent_grad)


def solution(mesh):
    in_specs = (
        P(("pa", "pb"), None),
        P(("pa", "pb"), None),
        P(("pa", "pb"), None),
        P(None, ("pa", "pb")),
        P(("pa", "pb"), None),
        P(("pa", "pb"), None),
        P(),
    )
    out_specs = (P(("pa", "pb"), None), P(("pa", "pb"), None), P(("pa", "pb"), None))
    npa, npb = mesh.shape["pa"], mesh.shape["pb"]

    def shards(*args):
        plan_of = (npa, npb, args[0].shape[0], args[4].shape[0], args[0].shape[1])
        if Plan.fits(*plan_of):
            return grouped(Plan(*plan_of), *args)
        return gathered(*args)

    return jax.shard_map(shards, mesh=mesh, in_specs=in_specs, out_specs=out_specs, check_vma=False)
```

```python
import math

import jax
import jax.numpy as jnp
from jax import lax
from jax.experimental import pallas as pl
from jax.experimental.pallas import tpu as pltpu
from jax.sharding import PartitionSpec as P


HEADS = 12
HEAD_DIM = 64
LANES = 128
AXES = ("pa", "pb")
MOST_IN_PLANE = 16
GROUPS = 4
VMEM_BYTES = 20 * 2**20
WHOLE_VMEM_BYTES = 60 * 2**20
LOG2E = math.log2(math.e)


class Plan:
    def __init__(self, npa, npb, rows, lat_rows, width):
        self.npa, self.npb = npa, npb
        self.fast = npb // GROUPS
        self.plane = npa * self.fast
        self.rows, self.lat_rows, self.width = rows, lat_rows, width
        self.heads = HEADS // GROUPS
        self.cols = self.heads * HEAD_DIM
        self.points = rows * GROUPS
        self.block = lat_rows * GROUPS
        self.latents = self.block * self.plane
        self.slot = lat_rows + 16
        self.ct_rows = self.cols + 16

    @staticmethod
    def fits(npa, npb, rows, lat_rows, width):
        def power(v):
            return v > 0 and v & (v - 1) == 0

        return (
            power(npa)
            and power(npb)
            and npb % GROUPS == 0
            and npa * npb // GROUPS <= MOST_IN_PLANE
            and lat_rows * GROUPS == LANES
            and rows == LANES
            and HEADS % GROUPS == 0
            and HEADS // GROUPS * rows == 2 * HEADS // GROUPS * HEAD_DIM
            and width == HEADS * HEAD_DIM
            and 2 * width // GROUPS == 3 * LANES
        )

    def exchange(self, value, over_group, step):
        pairs = []
        for a in range(self.npa):
            for b in range(self.npb):
                z, f = divmod(b, self.fast)
                if over_group:
                    a2, z2, f2 = a, z ^ step, f
                else:
                    a2, z2, f2 = a ^ (step // self.fast), z, f ^ (step % self.fast)
                pairs.append((a * self.npb + b, a2 * self.npb + z2 * self.fast + f2))
        return lax.ppermute(value, AXES, pairs)


def vmem():
    return pl.BlockSpec(memory_space=pltpu.VMEM)


def call(kernel, outs, args, scratch=(), flops=0, from_hbm=False):
    limit = WHOLE_VMEM_BYTES if from_hbm else VMEM_BYTES
    nbytes = sum(a.size * a.dtype.itemsize for a in args)
    nbytes += sum(math.prod(o.shape) * o.dtype.itemsize for o in outs)
    return pl.pallas_call(
        kernel,
        out_shape=tuple(outs),
        in_specs=[pl.BlockSpec(memory_space=pltpu.HBM) if from_hbm else vmem()] * len(args),
        out_specs=tuple(vmem() for _ in outs),
        scratch_shapes=list(scratch),
        cost_estimate=pl.CostEstimate(flops=flops, bytes_accessed=nbytes, transcendentals=flops // 256),
        compiler_params=pltpu.CompilerParams(vmem_limit_bytes=limit),
    )(*args)


def fetched(kernel, args):
    n = len(args)

    def body(*refs):
        held, sems = refs[-n - 1 : -1], refs[-1]
        copies = [
            pltpu.make_async_copy(src, dst, sems.at[i])
            for i, (src, dst) in enumerate(zip(refs[:n], held, strict=True))
        ]
        for copy in copies:
            copy.start()
        for copy in copies:
            copy.wait()
        kernel(*held, *refs[n : -n - 1])

    scratch = [pltpu.VMEM(a.shape, a.dtype) for a in args] + [pltpu.SemaphoreType.DMA((n,))]
    return body, scratch


def shaped(shape, dtype):
    return jax.ShapeDtypeStruct(shape, dtype)


def by_group(pieces, z):
    out = list(pieces)
    bit = 1
    while bit < len(out):
        on = (z & bit) != 0
        out = [jnp.where(on, out[g ^ bit], out[g]) for g in range(len(out))]
        bit *= 2
    return out


def group_index(plan):
    return lax.axis_index("pb") // plan.fast


def split3(value):
    hi = value.astype(jnp.bfloat16).astype(jnp.float32)
    rest = value - hi
    mid = rest.astype(jnp.bfloat16).astype(jnp.float32)
    return hi, mid, rest - mid


def nn(a, b):
    return lax.dot_general(a, b, (((1,), (0,)), ((), ())), preferred_element_type=jnp.float32)


def nt(a, b):
    return lax.dot_general(a, b, (((1,), (1,)), ((), ())), preferred_element_type=jnp.float32)


def turned(block):
    return block.astype(jnp.float32).T.astype(block.dtype)


def pack_latents(plan, query, out, norm):
    def kernel(q_ref, o_ref, n_ref, *outs):
        z = group_index(plan)
        c, hs = plan.cols, plan.heads
        q, o = q_ref[...].astype(jnp.float32), o_ref[...].astype(jnp.float32)
        parts = split3(n_ref[...])
        fill = jnp.zeros((plan.slot - plan.lat_rows - 3, hs * plan.rows), jnp.float32)
        pieces = []
        for g in range(GROUPS):
            top = jnp.concatenate([q[:, g * c : (g + 1) * c], o[:, g * c : (g + 1) * c]], axis=1)
            lines = [
                jnp.concatenate([p[h : h + 1, :] for h in range(g * hs, (g + 1) * hs)], axis=1) for p in parts
            ]
            pieces.append(jnp.concatenate([top, *lines, fill], axis=0))
        for ref, piece in zip(outs, by_group(pieces, z), strict=True):
            ref[...] = piece.astype(jnp.bfloat16)

    outs = [shaped((plan.slot, 2 * plan.cols), jnp.bfloat16)] * GROUPS
    args = (query, out, norm)
    body, scratch = fetched(kernel, args)
    return call(body, outs, args, scratch, from_hbm=True)


def pack_points(plan, keys, grads, values):
    def kernel(k_ref, g_ref, v_ref, *outs):
        z = group_index(plan)
        c = plan.cols
        for first, ref in ((0, k_ref), (1, g_ref)):
            whole = ref[...].astype(jnp.float32)
            pieces = by_group([whole[:, g * c : (g + 1) * c] for g in range(GROUPS)], z)
            for out, piece in zip(outs, pieces, strict=True):
                out[: plan.rows, first * c : (first + 1) * c] = piece.astype(jnp.bfloat16)
        across = v_ref[...].astype(jnp.float32).T.astype(jnp.bfloat16)
        pieces = by_group([across[g * c : (g + 1) * c] for g in range(GROUPS)], z)
        for out, piece in zip(outs, pieces, strict=True):
            for h in range(plan.heads):
                lanes = slice(h * plan.rows, (h + 1) * plan.rows)
                out[plan.rows :, lanes] = piece[h * HEAD_DIM : (h + 1) * HEAD_DIM]

    outs = [shaped((plan.rows + HEAD_DIM, 2 * plan.cols), jnp.bfloat16)] * GROUPS
    args = (keys, grads, values)
    body, scratch = fetched(kernel, args)
    return call(body, outs, args, scratch, from_hbm=True)


def order_norm(plan, norm):
    def kernel(n_ref, out_ref):
        z = group_index(plan)
        member = lax.axis_index("pa") * plan.npb + lax.axis_index("pb")
        hs, m = plan.heads, plan.latents
        rows = by_group([n_ref[g * hs : (g + 1) * hs, :] for g in range(GROUPS)], z)[0]
        fill = jnp.zeros((16 - 3 * hs, m), jnp.float32)
        stack = jnp.concatenate([*split3(rows), fill], axis=0).astype(jnp.bfloat16)
        lane = lax.broadcasted_iota(jnp.int32, (1, m), 1)
        inner, j, k = lane % plan.lat_rows, (lane // plan.lat_rows) % GROUPS, lane // plan.block
        owner = (k // plan.fast) * plan.npb + j * plan.fast + k % plan.fast
        source = (owner ^ member) * plan.lat_rows + inner
        total = jnp.zeros((16, m), jnp.float32)
        step = 256
        for start in range(0, m, step):
            row = lax.broadcasted_iota(jnp.int32, (step, m), 0) + start
            chosen = jnp.where(row == source, 1.0, 0.0).astype(jnp.bfloat16)
            total = total + nn(stack[:, start : start + step], chosen)
        out_ref[0:hs, :] = (total[:hs] + total[hs : 2 * hs]) + total[2 * hs : 3 * hs]

    return call(kernel, [shaped((plan.heads, plan.latents), jnp.float32)], (norm,))[0]


def turn_latents(plan, slots):
    def kernel(*refs):
        *slots, out, norm_out = refs
        n, rows = plan.lat_rows, plan.rows
        slots = [s[...] for s in slots]
        out[...] = turned(jnp.concatenate([s[:n] for s in slots], axis=0))
        for j, slot in enumerate(slots):
            parts = slot[n : n + 3].astype(jnp.float32)
            line = (parts[0:1] + parts[1:2]) + parts[2:3]
            lines = [line[:, h * rows : (h + 1) * rows] for h in range(plan.heads)]
            fill = jnp.zeros((LANES - plan.heads, rows), jnp.float32)
            norm_out[j * rows : (j + 1) * rows, :] = jnp.concatenate([*lines, fill], axis=0).T

    outs = [
        shaped((2 * plan.cols, plan.block), jnp.bfloat16),
        shaped((plan.points, LANES), jnp.float32),
    ]
    return call(kernel, outs, slots)


def lane_tiles(plan):
    width = min(2 * plan.block, plan.latents)
    return [slice(at, at + width) for at in range(0, plan.latents, width)]


def store_blocks(plan, outs, rows, lanes, value):
    for at in range(lanes.start, lanes.stop, plan.block):
        outs[at // plan.block][rows, :] = value[:, at - lanes.start : at - lanes.start + plan.block]


def first_pass(plan, lats, pts, dec_norm, enc_norm):
    n_lat = len(lats)
    c, m = plan.cols, plan.latents

    def kernel(*refs):
        lat_refs, pts_refs, (dec_ref, enc_ref) = refs[:n_lat], refs[n_lat:-5 - n_lat], refs[-5 - n_lat : -3 - n_lat]
        outs = refs[-3 - n_lat : -3]
        query, sides, keys = refs[-3:]
        for k, ref in enumerate(lat_refs):
            query[:, k * plan.block : (k + 1) * plan.block] = ref[:c, :]
        for j, ref in enumerate(pts_refs):
            rows = slice(j * plan.rows, (j + 1) * plan.rows)
            keys[rows, :] = ref[: plan.rows, :c]
            sides[:c, rows] = turned(ref[: plan.rows, c:])
            for h in range(plan.heads):
                below = slice(c + h * HEAD_DIM, c + (h + 1) * HEAD_DIM)
                sides[below, rows] = ref[plan.rows :, h * plan.rows : (h + 1) * plan.rows]
        for h in range(plan.heads):
            mine = slice(h * HEAD_DIM, (h + 1) * HEAD_DIM)
            below = slice(c + h * HEAD_DIM, c + (h + 1) * HEAD_DIM)
            key = keys[:, mine]
            row_norm = dec_ref[:, h : h + 1] * LOG2E
            for lanes in lane_tiles(plan):
                scores = nn(key, query[mine, lanes]) * (HEAD_DIM**-0.5 * LOG2E)
                dec = jnp.exp2(scores - row_norm).astype(jnp.bfloat16)
                enc = jnp.exp2(scores - enc_ref[h : h + 1, lanes] * LOG2E).astype(jnp.bfloat16)
                store_blocks(plan, outs, mine, lanes, nn(sides[mine, :], dec))
                store_blocks(plan, outs, below, lanes, nn(sides[below, :], enc))

    outs = [shaped((2 * c, plan.block), jnp.float32)] * plan.plane
    scratch = [
        pltpu.VMEM((c, m), jnp.bfloat16),
        pltpu.VMEM((2 * c, plan.points), jnp.bfloat16),
        pltpu.VMEM((plan.points, c), jnp.bfloat16),
    ]
    flops = 6 * plan.points * m * c
    return call(kernel, outs, (*lats, *pts, dec_norm, enc_norm), scratch, flops)


def decoder_pass(plan, lats, pts, dec_norm, heads):
    n_lat = len(lats)
    c, m = plan.cols, plan.latents

    def kernel(*refs):
        lat_refs, pts_refs, dec_ref = refs[:n_lat], refs[n_lat:-6], refs[-6]
        key_ref, lat_ref = refs[-5:-3]
        both, keys_t, ds = refs[-3:]
        for k, ref in enumerate(lat_refs):
            both[:, k * plan.block : (k + 1) * plan.block] = ref[...]
        for j, ref in enumerate(pts_refs):
            keys_t[:, j * plan.rows : (j + 1) * plan.rows] = turned(ref[: plan.rows, :c])
        for at, h in enumerate(heads):
            mine = slice(h * HEAD_DIM, (h + 1) * HEAD_DIM)
            put = slice(at * HEAD_DIM, (at + 1) * HEAD_DIM)
            other = slice(c + h * HEAD_DIM, c + (h + 1) * HEAD_DIM)
            for j, ref in enumerate(pts_refs):
                rows = slice(j * plan.rows, (j + 1) * plan.rows)
                scores = nn(ref[: plan.rows, mine], both[mine, :]) * (HEAD_DIM**-0.5 * LOG2E)
                dec = jnp.exp2(scores - dec_ref[rows, h : h + 1] * LOG2E)
                grad = nn(ref[: plan.rows, other], both[other, :])
                total = jnp.sum(dec * grad, axis=1, keepdims=True)
                tile = (dec * (grad - total)).astype(jnp.bfloat16)
                ds[rows, :] = tile
                key_ref[rows, put] = nt(tile, both[mine, :])
            lat_ref[put, :] = nn(keys_t[mine, :], ds[...])

    width = len(heads) * HEAD_DIM
    outs = [shaped((plan.points, width), jnp.float32), shaped((width, m), jnp.float32)]
    scratch = [
        pltpu.VMEM((2 * c, m), jnp.bfloat16),
        pltpu.VMEM((c, plan.points), jnp.bfloat16),
        pltpu.VMEM((plan.points, m), jnp.bfloat16),
    ]
    flops = 8 * plan.points * m * width
    return call(kernel, outs, (*lats, *pts, dec_norm), scratch, flops)


def reduce_mix(plan, parts):
    c, hs = plan.cols, plan.heads

    def kernel(*refs):
        *ins, out = refs
        total = ins[0][...]
        for ref in ins[1:]:
            total = total + ref[...]
        half = total[:c].astype(jnp.bfloat16)
        out[:c, :] = half
        product = half.astype(jnp.float32) * total[c:]
        sums = [
            jnp.sum(product[h * HEAD_DIM : (h + 1) * HEAD_DIM], axis=0, keepdims=True) for h in range(hs)
        ]
        fill = jnp.zeros((16 - 3 * hs, plan.block), jnp.float32)
        stack = jnp.concatenate([*split3(jnp.concatenate(sums, axis=0)), fill], axis=0)
        out[c:, :] = stack.astype(jnp.bfloat16)

    outs = [shaped((plan.ct_rows, plan.block), jnp.bfloat16)]
    return call(kernel, outs, parts)[0]


def encoder_pass(plan, lats, pts, norm, mixes, before):
    places = [(part, at) for part, (heads, _) in enumerate(before) for at in range(len(heads))]
    n_lat, n_pts, n_mix = len(lats), len(pts), len(mixes)
    c, m, hs = plan.cols, plan.latents, plan.heads

    def kernel(*refs):
        refs = list(refs)

        def take(n):
            got = refs[:n]
            del refs[:n]
            return got

        lat_refs, pts_refs = take(n_lat), take(n_pts)
        (norm_ref,) = take(1)
        mix_refs = take(n_mix)
        parts_in = [take(2) for _ in before]
        pts_outs, lat_outs = take(n_pts), take(n_lat)
        query, mix, keys, keys_t, values = refs
        for k, ref in enumerate(lat_refs):
            query[:, k * plan.block : (k + 1) * plan.block] = ref[:c, :]
        for k, ref in enumerate(mix_refs):
            mix[:, k * plan.block : (k + 1) * plan.block] = ref[...]
        for j, ref in enumerate(pts_refs):
            rows = slice(j * plan.rows, (j + 1) * plan.rows)
            keys[rows, :] = ref[: plan.rows, :c]
            keys_t[:, rows] = turned(ref[: plan.rows, :c])
            across = [ref[plan.rows :, h * plan.rows : (h + 1) * plan.rows] for h in range(hs)]
            values[rows, :] = turned(jnp.concatenate(across, axis=0))
        tail = mix[c:, :].astype(jnp.float32)
        columns = (tail[:hs] + tail[hs : 2 * hs]) + tail[2 * hs : 3 * hs]
        for h in range(hs):
            mine = slice(h * HEAD_DIM, (h + 1) * HEAD_DIM)
            part, at = places[h]
            key_in, lat_in = parts_in[part]
            put = slice(at * HEAD_DIM, (at + 1) * HEAD_DIM)
            key, value = keys[:, mine], values[:, mine]
            key_sum = key_in[:, put]
            value_sum = None
            for lanes in lane_tiles(plan):
                scores = nn(key, query[mine, lanes]) * (HEAD_DIM**-0.5 * LOG2E)
                enc = jnp.exp2(scores - norm_ref[h : h + 1, lanes] * LOG2E)
                grad = nn(value, mix[mine, lanes])
                ds = (enc * (grad - columns[h : h + 1, lanes])).astype(jnp.bfloat16)
                key_sum = key_sum + nt(ds, query[mine, lanes])
                more = nt(enc.astype(jnp.bfloat16), mix[mine, lanes])
                value_sum = more if value_sum is None else value_sum + more
                lat = (lat_in[put, lanes] + nn(keys_t[mine, :], ds)) * HEAD_DIM**-0.5
                store_blocks(plan, lat_outs, mine, lanes, lat)
            key_sum = (key_sum * HEAD_DIM**-0.5).astype(jnp.bfloat16)
            value_sum = value_sum.astype(jnp.bfloat16)
            for j, out in enumerate(pts_outs):
                rows = slice(j * plan.rows, (j + 1) * plan.rows)
                out[:, mine] = key_sum[rows]
                out[:, c + h * HEAD_DIM : c + (h + 1) * HEAD_DIM] = value_sum[rows]

    outs = [shaped((plan.rows, 2 * c), jnp.bfloat16)] * n_pts
    outs += [shaped((c, plan.block), jnp.float32)] * n_lat
    scratch = [
        pltpu.VMEM((c, m), jnp.bfloat16),
        pltpu.VMEM((plan.ct_rows, m), jnp.bfloat16),
        pltpu.VMEM((plan.points, c), jnp.bfloat16),
        pltpu.VMEM((c, plan.points), jnp.bfloat16),
        pltpu.VMEM((plan.points, c), jnp.bfloat16),
    ]
    flops = 10 * plan.points * m * c
    args = (*lats, *pts, norm, *mixes, *(a for _, part in before for a in part))
    got = call(kernel, outs, args, scratch, flops)
    return got[:n_pts], got[n_pts:]


def add_pairs(mine, theirs):
    def kernel(*refs):
        n = len(mine)
        for a, b, out in zip(refs[:n], refs[n : 2 * n], refs[2 * n :], strict=True):
            out[...] = a[...] + b[...]

    outs = [shaped(a.shape, a.dtype) for a in mine]
    return call(kernel, outs, (*mine, *theirs))


def reduce_latents(plan, parts):
    def kernel(*refs):
        ins, outs = refs[: len(parts)], refs[len(parts) :]
        total = ins[0][...]
        for ref in ins[1:]:
            total = total + ref[...]
        total = total.T
        for j, out in enumerate(outs):
            rows = total[j * plan.lat_rows : (j + 1) * plan.lat_rows]
            n, half = plan.lat_rows, plan.lat_rows // 2
            out[:n, :] = rows[:, :LANES]
            out[n:, :] = jnp.concatenate([rows[:half, LANES:], rows[half:, LANES:]], axis=1)

    outs = [shaped((3 * plan.lat_rows // 2, LANES), jnp.float32)] * GROUPS
    return call(kernel, outs, parts)


def place_points(plan, slots):
    def kernel(*refs):
        ins, (key_out, value_out) = refs[:GROUPS], refs[GROUPS:]
        z = group_index(plan)
        c = plan.cols
        pieces = by_group([r[...].astype(jnp.float32) for r in ins], z)
        for g, piece in enumerate(pieces):
            key_out[:, g * c : (g + 1) * c] = piece[:, :c].astype(jnp.bfloat16)
            value_out[:, g * c : (g + 1) * c] = piece[:, c:].astype(jnp.bfloat16)

    outs = [shaped((plan.rows, plan.width), jnp.bfloat16)] * 2
    return call(kernel, outs, slots)


def place_latents(plan, slots):
    def kernel(*refs):
        *ins, out = refs
        n, at = plan.lat_rows, plan.cols - LANES
        for g, piece in enumerate(by_group([r[...] for r in ins], group_index(plan))):
            rest = jnp.concatenate([piece[n:, :at], piece[n:, at:]], axis=0)
            out[:, g * plan.cols : (g + 1) * plan.cols] = jnp.concatenate([piece[:n], rest], axis=1)

    outs = [shaped((plan.lat_rows, plan.width), jnp.float32)]
    return call(kernel, outs, slots)[0]


def grouped(
    plan, point_keys, point_values, out_grad, decoder_norm, latent_query, latent_out, encoder_norm
):
    def over_group(slots):
        got = [slots[0]]
        for j in range(1, GROUPS):
            got.append(plan.exchange(slots[j], True, j))
        return got

    def chip_steps():
        return [k for k in range(plan.plane) if not k & plan.fast]

    def from_chips(blocks):
        got = []
        for k, block in zip(chip_steps(), blocks, strict=True):
            got.append(plan.exchange(block, False, k) if k else block)
        return got

    def sum_cores(blocks):
        near = chip_steps()
        theirs = [plan.exchange(blocks[k | plan.fast], False, plan.fast) for k in near]
        return add_pairs([blocks[k] for k in near], theirs)

    def to_plane(block):
        got = dict(zip(chip_steps(), from_chips([block] * len(chip_steps())), strict=True))
        for k in chip_steps():
            got[k | plan.fast] = plan.exchange(got[k], False, plan.fast)
        return tuple(got[k] for k in range(plan.plane))

    lat_slots = over_group(pack_latents(plan, latent_query, latent_out, decoder_norm))
    pts = pack_points(plan, point_keys, out_grad, point_values)
    pts = over_group(pts)
    norm = order_norm(plan, encoder_norm)
    block, dec_norm = turn_latents(plan, lat_slots)
    lats = to_plane(block)
    cores = sum_cores(first_pass(plan, lats, pts, dec_norm, norm))
    early, late = tuple(range(plan.heads))[:1], tuple(range(plan.heads))[1:]
    before = [(early, decoder_pass(plan, lats, pts, dec_norm, early))]
    sums = from_chips(cores)
    before.append((late, decoder_pass(plan, lats, pts, dec_norm, late)))
    mixes = to_plane(reduce_mix(plan, sums))
    pts_out, lat_out = encoder_pass(plan, lats, pts, norm, mixes, before)
    lat_out = from_chips(sum_cores(lat_out))
    pts_out = over_group(pts_out)
    lat_rows = over_group(reduce_latents(plan, lat_out))
    keys_grad, values_grad = place_points(plan, pts_out)
    return keys_grad, values_grad, place_latents(plan, lat_rows)


def column(block, current):
    return lax.dynamic_slice_in_dim(block, current * HEAD_DIM, HEAD_DIM, 1)


def put_head(total, piece, current):
    return lax.dynamic_update_slice_in_dim(total, piece, current * HEAD_DIM, 1)


def add_head(total, piece, current):
    return put_head(total, column(total, current) + piece, current)


def across(left, right):
    return lax.dot_general(
        left, right, (((1,), (1,)), ((), ())), preferred_element_type=jnp.float32
    )


def down_rows(left, right):
    return lax.dot_general(
        left, right, (((0,), (0,)), ((), ())), preferred_element_type=jnp.float32
    )


def gathered(
    point_keys, point_values, out_grad, decoder_norm, latent_query, latent_out, encoder_norm
):
    scale_factor = HEAD_DIM ** (-0.5)
    lat_all, out_all = (
        lax.all_gather(latent_query, ("pa", "pb"), axis=0, tiled=True),
        lax.all_gather(latent_out, ("pa", "pb"), axis=0, tiled=True),
    )
    point_rows = point_keys.shape[0]
    latent_rows = lat_all.shape[0]
    width = point_keys.shape[1]

    def encoder_row(current):
        return lax.dynamic_slice_in_dim(encoder_norm, current, 1, 0)

    def pass_one(current, state):
        mix_acc, query_acc, key_acc, weighted_acc = state
        key_head = column(point_keys, current)
        grad_head = column(out_grad, current)
        lat_head = column(lat_all, current)
        scores = across(key_head, lat_head) * scale_factor
        decoder_weights = jnp.exp(scores - lax.dynamic_slice_in_dim(decoder_norm, current, 1, 0).T)
        decoder_gradient = across(grad_head, column(out_all, current))
        row_total = jnp.sum(decoder_weights * decoder_gradient, axis=1, keepdims=True)
        decoder_scores_grad = (decoder_weights * (decoder_gradient - row_total)).astype(
            jnp.bfloat16
        )
        mix_acc = put_head(
            mix_acc, down_rows(decoder_weights.astype(jnp.bfloat16), grad_head), current
        )
        query_acc = put_head(
            query_acc, down_rows(decoder_scores_grad, key_head) * scale_factor, current
        )
        key_acc = put_head(
            key_acc,
            jnp.dot(decoder_scores_grad, lat_head, preferred_element_type=jnp.float32)
            * scale_factor,
            current,
        )
        return (mix_acc, query_acc, key_acc, weighted_acc)

    weighted_blank = jnp.zeros((1, 1), jnp.float32)
    latent_blank = jnp.zeros((latent_rows, width), jnp.float32)
    begin = (
        latent_blank,
        latent_blank,
        jnp.zeros((point_rows, width), jnp.float32),
        weighted_blank,
    )
    mix_acc, query_acc, key_acc, _ = lax.fori_loop(0, HEADS, pass_one, begin)
    mix_grad = lax.psum(mix_acc, ("pa", "pb"))
    mixing_portion = mix_grad.astype(jnp.bfloat16)

    def pass_two(current, state):
        partial_rows, value_acc = state
        scores = across(column(point_keys, current), column(lat_all, current)) * scale_factor
        encoder_portion = jnp.exp(scores - encoder_row(current)).astype(jnp.bfloat16)
        mix_head = column(mixing_portion, current)
        encoder_gradient = across(column(point_values, current), mix_head)
        sums = jnp.sum(encoder_portion.astype(jnp.float32) * encoder_gradient, axis=0)[None, :]
        partial_rows = lax.dynamic_update_slice_in_dim(partial_rows, sums, current, 0)
        value_acc = put_head(
            value_acc,
            jnp.dot(encoder_portion, mix_head, preferred_element_type=jnp.float32),
            current,
        )
        return (partial_rows, value_acc)

    partial_rows, value_acc = lax.fori_loop(
        0,
        HEADS,
        pass_two,
        (jnp.zeros((HEADS, latent_rows), jnp.float32), jnp.zeros((point_rows, width), jnp.float32)),
    )
    column_total = lax.psum(partial_rows, ("pa", "pb"))

    def pass_three(current, state):
        query_acc, key_acc, value_acc = state
        key_head = column(point_keys, current)
        lat_head = column(lat_all, current)
        mix_head = column(mixing_portion, current)
        scores = across(key_head, lat_head) * scale_factor
        encoder = jnp.exp(scores - encoder_row(current))
        encoder_gradient = across(column(point_values, current), mix_head)
        encoder_scores_grad = (
            encoder * (encoder_gradient - lax.dynamic_slice_in_dim(column_total, current, 1, 0))
        ).astype(jnp.bfloat16)
        query_acc = add_head(
            query_acc, down_rows(encoder_scores_grad, key_head) * scale_factor, current
        )
        key_acc = add_head(
            key_acc,
            jnp.dot(encoder_scores_grad, lat_head, preferred_element_type=jnp.float32)
            * scale_factor,
            current,
        )
        return (query_acc, key_acc, value_acc)

    query_acc, key_acc, value_acc = lax.fori_loop(
        0, HEADS, pass_three, (query_acc, key_acc, value_acc)
    )
    latent_grad = lax.psum_scatter(query_acc, ("pa", "pb"), scatter_dimension=0, tiled=True)
    return (key_acc.astype(jnp.bfloat16), value_acc.astype(jnp.bfloat16), latent_grad)


def solution(mesh):
    in_specs = (
        P(("pa", "pb"), None),
        P(("pa", "pb"), None),
        P(("pa", "pb"), None),
        P(None, ("pa", "pb")),
        P(("pa", "pb"), None),
        P(("pa", "pb"), None),
        P(),
    )
    out_specs = (P(("pa", "pb"), None), P(("pa", "pb"), None), P(("pa", "pb"), None))
    npa, npb = mesh.shape["pa"], mesh.shape["pb"]

    def shards(*args):
        plan_of = (npa, npb, args[0].shape[0], args[4].shape[0], args[0].shape[1])
        if Plan.fits(*plan_of):
            return grouped(Plan(*plan_of), *args)
        return gathered(*args)

    return jax.shard_map(shards, mesh=mesh, in_specs=in_specs, out_specs=out_specs, check_vma=False)
```

```python
import math

import jax
import jax.numpy as jnp
from jax import lax
from jax.experimental import pallas as pl
from jax.experimental.pallas import tpu as pltpu
from jax.sharding import PartitionSpec as P


HEADS = 12
HEAD_DIM = 64
LANES = 128
AXES = ("pa", "pb")
MOST_IN_PLANE = 16
LAG, SLOTS = 1, 3
GROUPS = 4
VMEM_BYTES = 20 * 2**20
WHOLE_VMEM_BYTES = 60 * 2**20
LOG2E = math.log2(math.e)


class Plan:
    def __init__(self, npa, npb, rows, lat_rows, width):
        self.npa, self.npb = npa, npb
        self.fast = npb // GROUPS
        self.plane = npa * self.fast
        self.rows, self.lat_rows, self.width = rows, lat_rows, width
        self.heads = HEADS // GROUPS
        self.cols = self.heads * HEAD_DIM
        self.points = rows * GROUPS
        self.block = lat_rows * GROUPS
        self.latents = self.block * self.plane
        self.slot = lat_rows + 16
        self.ct_rows = self.cols + 16

    @staticmethod
    def fits(npa, npb, rows, lat_rows, width):
        def power(v):
            return v > 0 and v & (v - 1) == 0

        return (
            power(npa)
            and power(npb)
            and npb % GROUPS == 0
            and npa * npb // GROUPS <= MOST_IN_PLANE
            and lat_rows * GROUPS == LANES
            and rows == LANES
            and HEADS % GROUPS == 0
            and HEADS // GROUPS * rows == 2 * HEADS // GROUPS * HEAD_DIM
            and width == HEADS * HEAD_DIM
            and 2 * width // GROUPS == 3 * LANES
        )

    def exchange(self, value, over_group, step):
        pairs = []
        for a in range(self.npa):
            for b in range(self.npb):
                z, f = divmod(b, self.fast)
                if over_group:
                    a2, z2, f2 = a, z ^ step, f
                else:
                    a2, z2, f2 = a ^ (step // self.fast), z, f ^ (step % self.fast)
                pairs.append((a * self.npb + b, a2 * self.npb + z2 * self.fast + f2))
        return lax.ppermute(value, AXES, pairs)


def vmem():
    return pl.BlockSpec(memory_space=pltpu.VMEM)


def call(kernel, outs, args, scratch=(), flops=0, from_hbm=False):
    limit = WHOLE_VMEM_BYTES if from_hbm else VMEM_BYTES
    nbytes = sum(a.size * a.dtype.itemsize for a in args)
    nbytes += sum(math.prod(o.shape) * o.dtype.itemsize for o in outs)
    return pl.pallas_call(
        kernel,
        out_shape=tuple(outs),
        in_specs=[pl.BlockSpec(memory_space=pltpu.HBM) if from_hbm else vmem()] * len(args),
        out_specs=tuple(vmem() for _ in outs),
        scratch_shapes=list(scratch),
        cost_estimate=pl.CostEstimate(flops=flops, bytes_accessed=nbytes, transcendentals=flops // 256),
        compiler_params=pltpu.CompilerParams(vmem_limit_bytes=limit),
    )(*args)


def fetched(kernel, args):
    n = len(args)

    def body(*refs):
        held, sems = refs[-n - 1 : -1], refs[-1]
        copies = [
            pltpu.make_async_copy(src, dst, sems.at[i])
            for i, (src, dst) in enumerate(zip(refs[:n], held, strict=True))
        ]
        for copy in copies:
            copy.start()
        for copy in copies:
            copy.wait()
        kernel(*held, *refs[n : -n - 1])

    scratch = [pltpu.VMEM(a.shape, a.dtype) for a in args] + [pltpu.SemaphoreType.DMA((n,))]
    return body, scratch


def shaped(shape, dtype):
    return jax.ShapeDtypeStruct(shape, dtype)


def by_group(pieces, z):
    out = list(pieces)
    bit = 1
    while bit < len(out):
        on = (z & bit) != 0
        out = [jnp.where(on, out[g ^ bit], out[g]) for g in range(len(out))]
        bit *= 2
    return out


def group_index(plan):
    return lax.axis_index("pb") // plan.fast


def split3(value):
    hi = value.astype(jnp.bfloat16).astype(jnp.float32)
    rest = value - hi
    mid = rest.astype(jnp.bfloat16).astype(jnp.float32)
    return hi, mid, rest - mid


def nn(a, b):
    return lax.dot_general(a, b, (((1,), (0,)), ((), ())), preferred_element_type=jnp.float32)


def nt(a, b):
    return lax.dot_general(a, b, (((1,), (1,)), ((), ())), preferred_element_type=jnp.float32)


def turned(block):
    return block.astype(jnp.float32).T.astype(block.dtype)


def pack(plan, query, out, norm, keys, grads, values):
    def kernel(q_ref, o_ref, n_ref, k_ref, g_ref, v_ref, *outs):
        z = group_index(plan)
        c, hs = plan.cols, plan.heads
        q, o = q_ref[...].astype(jnp.float32), o_ref[...].astype(jnp.float32)
        parts = split3(n_ref[...])
        fill = jnp.zeros((plan.slot - plan.lat_rows - 3, hs * plan.rows), jnp.float32)
        pieces = []
        for g in range(GROUPS):
            top = jnp.concatenate([q[:, g * c : (g + 1) * c], o[:, g * c : (g + 1) * c]], axis=1)
            lines = [
                jnp.concatenate([p[h : h + 1, :] for h in range(g * hs, (g + 1) * hs)], axis=1) for p in parts
            ]
            pieces.append(jnp.concatenate([top, *lines, fill], axis=0).astype(jnp.bfloat16))
        for ref, piece in zip(outs[:GROUPS], by_group(pieces, z), strict=True):
            ref[...] = piece
        outs = outs[GROUPS:]
        for first, ref in ((0, k_ref), (1, g_ref)):
            pieces = by_group([ref[:, g * c : (g + 1) * c] for g in range(GROUPS)], z)
            for out, piece in zip(outs, pieces, strict=True):
                out[: plan.rows, first * c : (first + 1) * c] = piece
        across = v_ref[...].T
        pieces = by_group([across[g * c : (g + 1) * c] for g in range(GROUPS)], z)
        for out, piece in zip(outs, pieces, strict=True):
            for h in range(hs):
                lanes = slice(h * plan.rows, (h + 1) * plan.rows)
                out[plan.rows :, lanes] = piece[h * HEAD_DIM : (h + 1) * HEAD_DIM]

    outs = [shaped((plan.slot, 2 * plan.cols), jnp.bfloat16)] * GROUPS
    outs += [shaped((plan.rows + HEAD_DIM, 2 * plan.cols), jnp.bfloat16)] * GROUPS
    args = (query, out, norm, keys, grads, values)
    body, scratch = fetched(kernel, args)
    got = call(body, outs, args, scratch, from_hbm=True)
    return got[:GROUPS], got[GROUPS:]


def order_norm(plan, norm):
    def kernel(n_ref, out_ref):
        z = group_index(plan)
        member = lax.axis_index("pa") * plan.npb + lax.axis_index("pb")
        hs, m = plan.heads, plan.latents
        rows = by_group([n_ref[g * hs : (g + 1) * hs, :] for g in range(GROUPS)], z)[0]
        fill = jnp.zeros((16 - 3 * hs, m), jnp.float32)
        stack = jnp.concatenate([*split3(rows), fill], axis=0).astype(jnp.bfloat16)
        lane = lax.broadcasted_iota(jnp.int32, (1, m), 1)
        inner, j, k = lane % plan.lat_rows, (lane // plan.lat_rows) % GROUPS, lane // plan.block
        owner = (k // plan.fast) * plan.npb + j * plan.fast + k % plan.fast
        source = (owner ^ member) * plan.lat_rows + inner
        total = jnp.zeros((16, m), jnp.float32)
        step = 256
        for start in range(0, m, step):
            row = lax.broadcasted_iota(jnp.int32, (step, m), 0) + start
            chosen = jnp.where(row == source, 1.0, 0.0).astype(jnp.bfloat16)
            total = total + nn(stack[:, start : start + step], chosen)
        out_ref[0:hs, :] = (total[:hs] + total[hs : 2 * hs]) + total[2 * hs : 3 * hs]

    return call(kernel, [shaped((plan.heads, plan.latents), jnp.float32)], (norm,))[0]


def turn_latents(plan, slots):
    def kernel(*refs):
        *slots, out, norm_out = refs
        n, rows = plan.lat_rows, plan.rows
        slots = [s[...] for s in slots]
        out[...] = turned(jnp.concatenate([s[:n] for s in slots], axis=0))
        for j, slot in enumerate(slots):
            parts = slot[n : n + 3].astype(jnp.float32)
            line = (parts[0:1] + parts[1:2]) + parts[2:3]
            lines = [line[:, h * rows : (h + 1) * rows] for h in range(plan.heads)]
            fill = jnp.zeros((LANES - plan.heads, rows), jnp.float32)
            norm_out[j * rows : (j + 1) * rows, :] = jnp.concatenate([*lines, fill], axis=0).T

    outs = [
        shaped((2 * plan.cols, plan.block), jnp.bfloat16),
        shaped((plan.points, LANES), jnp.float32),
    ]
    return call(kernel, outs, slots)


def lane_tiles(plan):
    width = min(2 * plan.block, plan.latents)
    return [slice(at, at + width) for at in range(0, plan.latents, width)]


def store_blocks(plan, outs, rows, lanes, value):
    for at in range(lanes.start, lanes.stop, plan.block):
        outs[at // plan.block][rows, :] = value[:, at - lanes.start : at - lanes.start + plan.block]


def first_pass(plan, lats, pts, dec_norm, enc_norm):
    n_lat = len(lats)
    c, m = plan.cols, plan.latents

    def kernel(*refs):
        lat_refs, pts_refs, (dec_ref, enc_ref) = refs[:n_lat], refs[n_lat:-5 - n_lat], refs[-5 - n_lat : -3 - n_lat]
        outs = refs[-3 - n_lat : -3]
        query, sides, keys = refs[-3:]
        for k, ref in enumerate(lat_refs):
            query[:, k * plan.block : (k + 1) * plan.block] = ref[:c, :]
        for j, ref in enumerate(pts_refs):
            rows = slice(j * plan.rows, (j + 1) * plan.rows)
            keys[rows, :] = ref[: plan.rows, :c]
            sides[:c, rows] = turned(ref[: plan.rows, c:])
            for h in range(plan.heads):
                below = slice(c + h * HEAD_DIM, c + (h + 1) * HEAD_DIM)
                sides[below, rows] = ref[plan.rows :, h * plan.rows : (h + 1) * plan.rows]
        for h in range(plan.heads):
            mine = slice(h * HEAD_DIM, (h + 1) * HEAD_DIM)
            below = slice(c + h * HEAD_DIM, c + (h + 1) * HEAD_DIM)
            key = keys[:, mine]
            row_norm = dec_ref[:, h : h + 1] * LOG2E
            for lanes in lane_tiles(plan):
                scores = nn(key, query[mine, lanes]) * (HEAD_DIM**-0.5 * LOG2E)
                dec = jnp.exp2(scores - row_norm).astype(jnp.bfloat16)
                enc = jnp.exp2(scores - enc_ref[h : h + 1, lanes] * LOG2E).astype(jnp.bfloat16)
                store_blocks(plan, outs, mine, lanes, nn(sides[mine, :], dec))
                store_blocks(plan, outs, below, lanes, nn(sides[below, :], enc))

    outs = [shaped((2 * c, plan.block), jnp.float32)] * plan.plane
    scratch = [
        pltpu.VMEM((c, m), jnp.bfloat16),
        pltpu.VMEM((2 * c, plan.points), jnp.bfloat16),
        pltpu.VMEM((plan.points, c), jnp.bfloat16),
    ]
    flops = 6 * plan.points * m * c
    return call(kernel, outs, (*lats, *pts, dec_norm, enc_norm), scratch, flops)


def decoder_pass(plan, lats, pts, dec_norm, heads):
    n_lat = len(lats)
    c, m = plan.cols, plan.latents

    def kernel(*refs):
        lat_refs, pts_refs, dec_ref = refs[:n_lat], refs[n_lat:-6], refs[-6]
        key_ref, lat_ref = refs[-5:-3]
        both, keys_t, ds = refs[-3:]
        for k, ref in enumerate(lat_refs):
            both[:, k * plan.block : (k + 1) * plan.block] = ref[...]
        for j, ref in enumerate(pts_refs):
            keys_t[:, j * plan.rows : (j + 1) * plan.rows] = turned(ref[: plan.rows, :c])
        for at, h in enumerate(heads):
            mine = slice(h * HEAD_DIM, (h + 1) * HEAD_DIM)
            put = slice(at * HEAD_DIM, (at + 1) * HEAD_DIM)
            other = slice(c + h * HEAD_DIM, c + (h + 1) * HEAD_DIM)
            for j, ref in enumerate(pts_refs):
                rows = slice(j * plan.rows, (j + 1) * plan.rows)
                scores = nn(ref[: plan.rows, mine], both[mine, :]) * (HEAD_DIM**-0.5 * LOG2E)
                dec = jnp.exp2(scores - dec_ref[rows, h : h + 1] * LOG2E)
                grad = nn(ref[: plan.rows, other], both[other, :])
                total = jnp.sum(dec * grad, axis=1, keepdims=True)
                tile = (dec * (grad - total)).astype(jnp.bfloat16)
                ds[rows, :] = tile
            key_ref[put, :] = nt(both[mine, :], ds[...])
            lat_ref[put, :] = nn(keys_t[mine, :], ds[...])

    width = len(heads) * HEAD_DIM
    outs = [shaped((width, plan.points), jnp.float32), shaped((width, m), jnp.float32)]
    scratch = [
        pltpu.VMEM((2 * c, m), jnp.bfloat16),
        pltpu.VMEM((c, plan.points), jnp.bfloat16),
        pltpu.VMEM((plan.points, m), jnp.bfloat16),
    ]
    flops = 8 * plan.points * m * width
    return call(kernel, outs, (*lats, *pts, dec_norm), scratch, flops)


def reduce_mix(plan, parts):
    c, hs = plan.cols, plan.heads

    def kernel(*refs):
        *ins, out = refs
        total = ins[0][...]
        for ref in ins[1:]:
            total = total + ref[...]
        half = total[:c].astype(jnp.bfloat16)
        out[:c, :] = half
        product = half.astype(jnp.float32) * total[c:]
        sums = [
            jnp.sum(product[h * HEAD_DIM : (h + 1) * HEAD_DIM], axis=0, keepdims=True) for h in range(hs)
        ]
        fill = jnp.zeros((16 - 3 * hs, plan.block), jnp.float32)
        stack = jnp.concatenate([*split3(jnp.concatenate(sums, axis=0)), fill], axis=0)
        out[c:, :] = stack.astype(jnp.bfloat16)

    outs = [shaped((plan.ct_rows, plan.block), jnp.bfloat16)]
    return call(kernel, outs, parts)[0]


def encoder_pass(plan, lats, pts, norm, mixes, before):
    places = [(part, at) for part, (heads, _) in enumerate(before) for at in range(len(heads))]
    n_lat, n_pts, n_mix = len(lats), len(pts), len(mixes)
    c, m, hs = plan.cols, plan.latents, plan.heads

    def kernel(*refs):
        refs = list(refs)

        def take(n):
            got = refs[:n]
            del refs[:n]
            return got

        lat_refs, pts_refs = take(n_lat), take(n_pts)
        (norm_ref,) = take(1)
        mix_refs = take(n_mix)
        parts_in = [take(2) for _ in before]
        pts_outs, lat_outs = take(n_pts), take(n_lat)
        query, mix, keys, keys_t, values, ds, encs = refs
        for k, ref in enumerate(lat_refs):
            query[:, k * plan.block : (k + 1) * plan.block] = ref[:c, :]
        for k, ref in enumerate(mix_refs):
            mix[:, k * plan.block : (k + 1) * plan.block] = ref[...]
        for j, ref in enumerate(pts_refs):
            rows = slice(j * plan.rows, (j + 1) * plan.rows)
            keys[rows, :] = ref[: plan.rows, :c]
            keys_t[:, rows] = turned(ref[: plan.rows, :c])
            across = [ref[plan.rows :, h * plan.rows : (h + 1) * plan.rows] for h in range(hs)]
            values[rows, :] = turned(jnp.concatenate(across, axis=0))
        tail = mix[c:, :].astype(jnp.float32)
        columns = (tail[:hs] + tail[hs : 2 * hs]) + tail[2 * hs : 3 * hs]
        tiles = lane_tiles(plan)
        sums = {}

        def weigh(h, t, slot):
            mine, lanes = slice(h * HEAD_DIM, (h + 1) * HEAD_DIM), tiles[t]
            scores = nn(keys[:, mine], query[mine, lanes]) * (HEAD_DIM**-0.5 * LOG2E)
            enc = jnp.exp2(scores - norm_ref[h : h + 1, lanes] * LOG2E)
            grad = nn(values[:, mine], mix[mine, lanes])
            encs[slot] = enc.astype(jnp.bfloat16)
            ds[slot] = (enc * (grad - columns[h : h + 1, lanes])).astype(jnp.bfloat16)

        def gather(h, t, slot):
            mine, lanes = slice(h * HEAD_DIM, (h + 1) * HEAD_DIM), tiles[t]
            part, at = places[h]
            key_in, lat_in = parts_in[part]
            put = slice(at * HEAD_DIM, (at + 1) * HEAD_DIM)
            lat = (lat_in[put, lanes] + nn(keys_t[mine, :], ds[slot])) * HEAD_DIM**-0.5
            store_blocks(plan, lat_outs, mine, lanes, lat)
            key, value = nt(query[mine, lanes], ds[slot]), nt(mix[mine, lanes], encs[slot])
            key = key + (sums[h][0] if t else key_in[put, :])
            sums[h] = (key, value + sums[h][1] if t else value)
            if t < len(tiles) - 1:
                return
            key, value = sums.pop(h)
            key = (key * HEAD_DIM**-0.5).T.astype(jnp.bfloat16)
            value = value.T.astype(jnp.bfloat16)
            for j, out in enumerate(pts_outs):
                rows = slice(j * plan.rows, (j + 1) * plan.rows)
                out[:, mine] = key[rows]
                out[:, c + h * HEAD_DIM : c + (h + 1) * HEAD_DIM] = value[rows]

        work = [(h, t) for h in range(hs) for t in range(len(tiles))]
        for n, place in enumerate(work):
            weigh(*place, n % SLOTS)
            if n >= LAG:
                gather(*work[n - LAG], (n - LAG) % SLOTS)
        for n in range(len(work) - LAG, len(work)):
            gather(*work[n], n % SLOTS)

    outs = [shaped((plan.rows, 2 * c), jnp.bfloat16)] * n_pts
    outs += [shaped((c, plan.block), jnp.float32)] * n_lat
    scratch = [
        pltpu.VMEM((c, m), jnp.bfloat16),
        pltpu.VMEM((plan.ct_rows, m), jnp.bfloat16),
        pltpu.VMEM((plan.points, c), jnp.bfloat16),
        pltpu.VMEM((c, plan.points), jnp.bfloat16),
        pltpu.VMEM((plan.points, c), jnp.bfloat16),
        pltpu.VMEM((SLOTS, plan.points, 2 * plan.block), jnp.bfloat16),
        pltpu.VMEM((SLOTS, plan.points, 2 * plan.block), jnp.bfloat16),
    ]
    flops = 10 * plan.points * m * c
    args = (*lats, *pts, norm, *mixes, *(a for _, part in before for a in part))
    got = call(kernel, outs, args, scratch, flops)
    return got[:n_pts], got[n_pts:]


def add_pairs(mine, theirs):
    def kernel(*refs):
        n = len(mine)
        for a, b, out in zip(refs[:n], refs[n : 2 * n], refs[2 * n :], strict=True):
            out[...] = a[...] + b[...]

    outs = [shaped(a.shape, a.dtype) for a in mine]
    return call(kernel, outs, (*mine, *theirs))


def reduce_latents(plan, parts):
    def kernel(*refs):
        ins, outs = refs[: len(parts)], refs[len(parts) :]
        total = ins[0][...]
        for ref in ins[1:]:
            total = total + ref[...]
        total = total.T
        for j, out in enumerate(outs):
            rows = total[j * plan.lat_rows : (j + 1) * plan.lat_rows]
            n, half = plan.lat_rows, plan.lat_rows // 2
            out[:n, :] = rows[:, :LANES]
            out[n:, :] = jnp.concatenate([rows[:half, LANES:], rows[half:, LANES:]], axis=1)

    outs = [shaped((3 * plan.lat_rows // 2, LANES), jnp.float32)] * GROUPS
    return call(kernel, outs, parts)


def place_points(plan, slots):
    def kernel(*refs):
        ins, (key_out, value_out) = refs[:GROUPS], refs[GROUPS:]
        z = group_index(plan)
        c = plan.cols
        pieces = by_group([r[...].astype(jnp.float32) for r in ins], z)
        for g, piece in enumerate(pieces):
            key_out[:, g * c : (g + 1) * c] = piece[:, :c].astype(jnp.bfloat16)
            value_out[:, g * c : (g + 1) * c] = piece[:, c:].astype(jnp.bfloat16)

    outs = [shaped((plan.rows, plan.width), jnp.bfloat16)] * 2
    return call(kernel, outs, slots)


def place_latents(plan, slots):
    def kernel(*refs):
        *ins, out = refs
        n, at = plan.lat_rows, plan.cols - LANES
        for g, piece in enumerate(by_group([r[...] for r in ins], group_index(plan))):
            rest = jnp.concatenate([piece[n:, :at], piece[n:, at:]], axis=0)
            out[:, g * plan.cols : (g + 1) * plan.cols] = jnp.concatenate([piece[:n], rest], axis=1)

    outs = [shaped((plan.lat_rows, plan.width), jnp.float32)]
    return call(kernel, outs, slots)[0]


def grouped(
    plan, point_keys, point_values, out_grad, decoder_norm, latent_query, latent_out, encoder_norm
):
    def over_group(slots):
        got = [slots[0]]
        for j in range(1, GROUPS):
            got.append(plan.exchange(slots[j], True, j))
        return got

    def chip_steps():
        return [k for k in range(plan.plane) if not k & plan.fast]

    def from_chips(blocks):
        got = []
        for k, block in zip(chip_steps(), blocks, strict=True):
            got.append(plan.exchange(block, False, k) if k else block)
        return got

    def sum_cores(blocks):
        near = chip_steps()
        theirs = [plan.exchange(blocks[k | plan.fast], False, plan.fast) for k in near]
        return add_pairs([blocks[k] for k in near], theirs)

    def to_plane(block):
        got = dict(zip(chip_steps(), from_chips([block] * len(chip_steps())), strict=True))
        for k in chip_steps():
            got[k | plan.fast] = plan.exchange(got[k], False, plan.fast)
        return tuple(got[k] for k in range(plan.plane))

    lat_slots, pts = pack(
        plan, latent_query, latent_out, decoder_norm, point_keys, out_grad, point_values
    )
    lat_slots = over_group(lat_slots)
    pts = over_group(pts)
    norm = order_norm(plan, encoder_norm)
    block, dec_norm = turn_latents(plan, lat_slots)
    lats = to_plane(block)
    cores = sum_cores(first_pass(plan, lats, pts, dec_norm, norm))
    early, late = tuple(range(plan.heads))[:1], tuple(range(plan.heads))[1:]
    before = [(early, decoder_pass(plan, lats, pts, dec_norm, early))]
    sums = from_chips(cores)
    before.append((late, decoder_pass(plan, lats, pts, dec_norm, late)))
    mixes = to_plane(reduce_mix(plan, sums))
    pts_out, lat_out = encoder_pass(plan, lats, pts, norm, mixes, before)
    lat_out = from_chips(sum_cores(lat_out))
    pts_out = over_group(pts_out)
    lat_rows = over_group(reduce_latents(plan, lat_out))
    keys_grad, values_grad = place_points(plan, pts_out)
    return keys_grad, values_grad, place_latents(plan, lat_rows)


def column(block, current):
    return lax.dynamic_slice_in_dim(block, current * HEAD_DIM, HEAD_DIM, 1)


def put_head(total, piece, current):
    return lax.dynamic_update_slice_in_dim(total, piece, current * HEAD_DIM, 1)


def add_head(total, piece, current):
    return put_head(total, column(total, current) + piece, current)


def across(left, right):
    return lax.dot_general(
        left, right, (((1,), (1,)), ((), ())), preferred_element_type=jnp.float32
    )


def down_rows(left, right):
    return lax.dot_general(
        left, right, (((0,), (0,)), ((), ())), preferred_element_type=jnp.float32
    )


def gathered(
    point_keys, point_values, out_grad, decoder_norm, latent_query, latent_out, encoder_norm
):
    scale_factor = HEAD_DIM ** (-0.5)
    lat_all, out_all = (
        lax.all_gather(latent_query, ("pa", "pb"), axis=0, tiled=True),
        lax.all_gather(latent_out, ("pa", "pb"), axis=0, tiled=True),
    )
    point_rows = point_keys.shape[0]
    latent_rows = lat_all.shape[0]
    width = point_keys.shape[1]

    def encoder_row(current):
        return lax.dynamic_slice_in_dim(encoder_norm, current, 1, 0)

    def pass_one(current, state):
        mix_acc, query_acc, key_acc, weighted_acc = state
        key_head = column(point_keys, current)
        grad_head = column(out_grad, current)
        lat_head = column(lat_all, current)
        scores = across(key_head, lat_head) * scale_factor
        decoder_weights = jnp.exp(scores - lax.dynamic_slice_in_dim(decoder_norm, current, 1, 0).T)
        decoder_gradient = across(grad_head, column(out_all, current))
        row_total = jnp.sum(decoder_weights * decoder_gradient, axis=1, keepdims=True)
        decoder_scores_grad = (decoder_weights * (decoder_gradient - row_total)).astype(
            jnp.bfloat16
        )
        mix_acc = put_head(
            mix_acc, down_rows(decoder_weights.astype(jnp.bfloat16), grad_head), current
        )
        query_acc = put_head(
            query_acc, down_rows(decoder_scores_grad, key_head) * scale_factor, current
        )
        key_acc = put_head(
            key_acc,
            jnp.dot(decoder_scores_grad, lat_head, preferred_element_type=jnp.float32)
            * scale_factor,
            current,
        )
        return (mix_acc, query_acc, key_acc, weighted_acc)

    weighted_blank = jnp.zeros((1, 1), jnp.float32)
    latent_blank = jnp.zeros((latent_rows, width), jnp.float32)
    begin = (
        latent_blank,
        latent_blank,
        jnp.zeros((point_rows, width), jnp.float32),
        weighted_blank,
    )
    mix_acc, query_acc, key_acc, _ = lax.fori_loop(0, HEADS, pass_one, begin)
    mix_grad = lax.psum(mix_acc, ("pa", "pb"))
    mixing_portion = mix_grad.astype(jnp.bfloat16)

    def pass_two(current, state):
        partial_rows, value_acc = state
        scores = across(column(point_keys, current), column(lat_all, current)) * scale_factor
        encoder_portion = jnp.exp(scores - encoder_row(current)).astype(jnp.bfloat16)
        mix_head = column(mixing_portion, current)
        encoder_gradient = across(column(point_values, current), mix_head)
        sums = jnp.sum(encoder_portion.astype(jnp.float32) * encoder_gradient, axis=0)[None, :]
        partial_rows = lax.dynamic_update_slice_in_dim(partial_rows, sums, current, 0)
        value_acc = put_head(
            value_acc,
            jnp.dot(encoder_portion, mix_head, preferred_element_type=jnp.float32),
            current,
        )
        return (partial_rows, value_acc)

    partial_rows, value_acc = lax.fori_loop(
        0,
        HEADS,
        pass_two,
        (jnp.zeros((HEADS, latent_rows), jnp.float32), jnp.zeros((point_rows, width), jnp.float32)),
    )
    column_total = lax.psum(partial_rows, ("pa", "pb"))

    def pass_three(current, state):
        query_acc, key_acc, value_acc = state
        key_head = column(point_keys, current)
        lat_head = column(lat_all, current)
        mix_head = column(mixing_portion, current)
        scores = across(key_head, lat_head) * scale_factor
        encoder = jnp.exp(scores - encoder_row(current))
        encoder_gradient = across(column(point_values, current), mix_head)
        encoder_scores_grad = (
            encoder * (encoder_gradient - lax.dynamic_slice_in_dim(column_total, current, 1, 0))
        ).astype(jnp.bfloat16)
        query_acc = add_head(
            query_acc, down_rows(encoder_scores_grad, key_head) * scale_factor, current
        )
        key_acc = add_head(
            key_acc,
            jnp.dot(encoder_scores_grad, lat_head, preferred_element_type=jnp.float32)
            * scale_factor,
            current,
        )
        return (query_acc, key_acc, value_acc)

    query_acc, key_acc, value_acc = lax.fori_loop(
        0, HEADS, pass_three, (query_acc, key_acc, value_acc)
    )
    latent_grad = lax.psum_scatter(query_acc, ("pa", "pb"), scatter_dimension=0, tiled=True)
    return (key_acc.astype(jnp.bfloat16), value_acc.astype(jnp.bfloat16), latent_grad)


def solution(mesh):
    in_specs = (
        P(("pa", "pb"), None),
        P(("pa", "pb"), None),
        P(("pa", "pb"), None),
        P(None, ("pa", "pb")),
        P(("pa", "pb"), None),
        P(("pa", "pb"), None),
        P(),
    )
    out_specs = (P(("pa", "pb"), None), P(("pa", "pb"), None), P(("pa", "pb"), None))
    npa, npb = mesh.shape["pa"], mesh.shape["pb"]

    def shards(*args):
        plan_of = (npa, npb, args[0].shape[0], args[4].shape[0], args[0].shape[1])
        if Plan.fits(*plan_of):
            return grouped(Plan(*plan_of), *args)
        return gathered(*args)

    return jax.shard_map(shards, mesh=mesh, in_specs=in_specs, out_specs=out_specs, check_vma=False)
```

```python
import math

import jax
import jax.numpy as jnp
from jax import lax
from jax.experimental import pallas as pl
from jax.experimental.pallas import tpu as pltpu
from jax.sharding import PartitionSpec as P


HEADS = 12
HEAD_DIM = 64
LANES = 128
AXES = ("pa", "pb")
MOST_IN_PLANE = 16
HALF_SIZE, SMALLEST = 14.0, 2.0**-100
LAG, SLOTS = 1, 3
GROUPS = 4
VMEM_BYTES = 20 * 2**20
WHOLE_VMEM_BYTES = 60 * 2**20
LOG2E = math.log2(math.e)


class Plan:
    def __init__(self, npa, npb, rows, lat_rows, width):
        self.npa, self.npb = npa, npb
        self.fast = npb // GROUPS
        self.plane = npa * self.fast
        self.rows, self.lat_rows, self.width = rows, lat_rows, width
        self.heads = HEADS // GROUPS
        self.cols = self.heads * HEAD_DIM
        self.points = rows * GROUPS
        self.block = lat_rows * GROUPS
        self.latents = self.block * self.plane
        self.slot = lat_rows + 16
        self.ct_rows = self.cols + 16

    @staticmethod
    def fits(npa, npb, rows, lat_rows, width):
        def power(v):
            return v > 0 and v & (v - 1) == 0

        return (
            power(npa)
            and power(npb)
            and npb % GROUPS == 0
            and npa * npb // GROUPS <= MOST_IN_PLANE
            and lat_rows * GROUPS == LANES
            and rows == LANES
            and HEADS % GROUPS == 0
            and HEADS // GROUPS * rows == 2 * HEADS // GROUPS * HEAD_DIM
            and width == HEADS * HEAD_DIM
            and 2 * width // GROUPS == 3 * LANES
        )

    def exchange(self, value, over_group, step):
        pairs = []
        for a in range(self.npa):
            for b in range(self.npb):
                z, f = divmod(b, self.fast)
                if over_group:
                    a2, z2, f2 = a, z ^ step, f
                else:
                    a2, z2, f2 = a ^ (step // self.fast), z, f ^ (step % self.fast)
                pairs.append((a * self.npb + b, a2 * self.npb + z2 * self.fast + f2))
        return lax.ppermute(value, AXES, pairs)


def vmem():
    return pl.BlockSpec(memory_space=pltpu.VMEM)


def call(kernel, outs, args, scratch=(), flops=0, from_hbm=False):
    limit = WHOLE_VMEM_BYTES if from_hbm else VMEM_BYTES
    nbytes = sum(a.size * a.dtype.itemsize for a in args)
    nbytes += sum(math.prod(o.shape) * o.dtype.itemsize for o in outs)
    return pl.pallas_call(
        kernel,
        out_shape=tuple(outs),
        in_specs=[pl.BlockSpec(memory_space=pltpu.HBM) if from_hbm else vmem()] * len(args),
        out_specs=tuple(vmem() for _ in outs),
        scratch_shapes=list(scratch),
        cost_estimate=pl.CostEstimate(flops=flops, bytes_accessed=nbytes, transcendentals=flops // 256),
        compiler_params=pltpu.CompilerParams(vmem_limit_bytes=limit),
    )(*args)


def fetched(kernel, args):
    n = len(args)

    def body(*refs):
        held, sems = refs[-n - 1 : -1], refs[-1]
        copies = [
            pltpu.make_async_copy(src, dst, sems.at[i])
            for i, (src, dst) in enumerate(zip(refs[:n], held, strict=True))
        ]
        for copy in copies:
            copy.start()
        for copy in copies:
            copy.wait()
        kernel(*held, *refs[n : -n - 1])

    scratch = [pltpu.VMEM(a.shape, a.dtype) for a in args] + [pltpu.SemaphoreType.DMA((n,))]
    return body, scratch


def shaped(shape, dtype):
    return jax.ShapeDtypeStruct(shape, dtype)


def by_group(pieces, z):
    out = list(pieces)
    bit = 1
    while bit < len(out):
        on = (z & bit) != 0
        out = [jnp.where(on, out[g ^ bit], out[g]) for g in range(len(out))]
        bit *= 2
    return out


def group_index(plan):
    return lax.axis_index("pb") // plan.fast


def split3(value):
    hi = value.astype(jnp.bfloat16).astype(jnp.float32)
    rest = value - hi
    mid = rest.astype(jnp.bfloat16).astype(jnp.float32)
    return hi, mid, rest - mid


def nn(a, b):
    return lax.dot_general(a, b, (((1,), (0,)), ((), ())), preferred_element_type=jnp.float32)


def nt(a, b):
    return lax.dot_general(a, b, (((1,), (1,)), ((), ())), preferred_element_type=jnp.float32)


def turned(block):
    return block.astype(jnp.float32).T.astype(block.dtype)


def pack(plan, query, out, norm, keys, grads, values):
    def kernel(q_ref, o_ref, n_ref, k_ref, g_ref, v_ref, *outs):
        z = group_index(plan)
        c, hs = plan.cols, plan.heads
        q, o = q_ref[...].astype(jnp.float32), o_ref[...].astype(jnp.float32)
        parts = split3(n_ref[...])
        fill = jnp.zeros((plan.slot - plan.lat_rows - 3, hs * plan.rows), jnp.float32)
        pieces = []
        for g in range(GROUPS):
            top = jnp.concatenate([q[:, g * c : (g + 1) * c], o[:, g * c : (g + 1) * c]], axis=1)
            lines = [
                jnp.concatenate([p[h : h + 1, :] for h in range(g * hs, (g + 1) * hs)], axis=1) for p in parts
            ]
            pieces.append(jnp.concatenate([top, *lines, fill], axis=0).astype(jnp.bfloat16))
        for ref, piece in zip(outs[:GROUPS], by_group(pieces, z), strict=True):
            ref[...] = piece
        outs = outs[GROUPS:]
        for first, ref in ((0, k_ref), (1, g_ref)):
            pieces = by_group([ref[:, g * c : (g + 1) * c] for g in range(GROUPS)], z)
            for out, piece in zip(outs, pieces, strict=True):
                out[: plan.rows, first * c : (first + 1) * c] = piece
        across = v_ref[...].T
        pieces = by_group([across[g * c : (g + 1) * c] for g in range(GROUPS)], z)
        for out, piece in zip(outs, pieces, strict=True):
            for h in range(hs):
                lanes = slice(h * plan.rows, (h + 1) * plan.rows)
                out[plan.rows :, lanes] = piece[h * HEAD_DIM : (h + 1) * HEAD_DIM]

    outs = [shaped((plan.slot, 2 * plan.cols), jnp.bfloat16)] * GROUPS
    outs += [shaped((plan.rows + HEAD_DIM, 2 * plan.cols), jnp.bfloat16)] * GROUPS
    args = (query, out, norm, keys, grads, values)
    body, scratch = fetched(kernel, args)
    got = call(body, outs, args, scratch, from_hbm=True)
    return got[:GROUPS], got[GROUPS:]


def order_norm(plan, norm):
    def kernel(n_ref, out_ref):
        z = group_index(plan)
        member = lax.axis_index("pa") * plan.npb + lax.axis_index("pb")
        hs, m = plan.heads, plan.latents
        rows = by_group([n_ref[g * hs : (g + 1) * hs, :] for g in range(GROUPS)], z)[0]
        fill = jnp.zeros((16 - 3 * hs, m), jnp.float32)
        stack = jnp.concatenate([*split3(rows), fill], axis=0).astype(jnp.bfloat16)
        lane = lax.broadcasted_iota(jnp.int32, (1, m), 1)
        inner, j, k = lane % plan.lat_rows, (lane // plan.lat_rows) % GROUPS, lane // plan.block
        owner = (k // plan.fast) * plan.npb + j * plan.fast + k % plan.fast
        source = (owner ^ member) * plan.lat_rows + inner
        total = jnp.zeros((16, m), jnp.float32)
        step = 256
        for start in range(0, m, step):
            row = lax.broadcasted_iota(jnp.int32, (step, m), 0) + start
            chosen = jnp.where(row == source, 1.0, 0.0).astype(jnp.bfloat16)
            total = total + nn(stack[:, start : start + step], chosen)
        out_ref[0:hs, :] = (total[:hs] + total[hs : 2 * hs]) + total[2 * hs : 3 * hs]

    return call(kernel, [shaped((plan.heads, plan.latents), jnp.float32)], (norm,))[0]


def turn_latents(plan, slots):
    def kernel(*refs):
        *slots, out, norm_out = refs
        n, rows = plan.lat_rows, plan.rows
        slots = [s[...] for s in slots]
        out[...] = turned(jnp.concatenate([s[:n] for s in slots], axis=0))
        for j, slot in enumerate(slots):
            parts = slot[n : n + 3].astype(jnp.float32)
            line = (parts[0:1] + parts[1:2]) + parts[2:3]
            lines = [line[:, h * rows : (h + 1) * rows] for h in range(plan.heads)]
            fill = jnp.zeros((LANES - plan.heads, rows), jnp.float32)
            norm_out[j * rows : (j + 1) * rows, :] = jnp.concatenate([*lines, fill], axis=0).T

    outs = [
        shaped((2 * plan.cols, plan.block), jnp.bfloat16),
        shaped((plan.points, LANES), jnp.float32),
    ]
    return call(kernel, outs, slots)


def lane_tiles(plan):
    width = min(2 * plan.block, plan.latents)
    return [slice(at, at + width) for at in range(0, plan.latents, width)]


def store_blocks(plan, outs, rows, lanes, value):
    for at in range(lanes.start, lanes.stop, plan.block):
        outs[at // plan.block][rows, :] = value[:, at - lanes.start : at - lanes.start + plan.block]


def first_pass(plan, lats, pts, dec_norm, enc_norm):
    n_lat = len(lats)
    c, m = plan.cols, plan.latents

    def kernel(*refs):
        lat_refs, pts_refs, (dec_ref, enc_ref) = refs[:n_lat], refs[n_lat:-5 - n_lat], refs[-5 - n_lat : -3 - n_lat]
        outs = refs[-3 - n_lat : -3]
        query, sides, keys = refs[-3:]
        for k, ref in enumerate(lat_refs):
            query[:, k * plan.block : (k + 1) * plan.block] = ref[:c, :]
        for j, ref in enumerate(pts_refs):
            rows = slice(j * plan.rows, (j + 1) * plan.rows)
            keys[rows, :] = ref[: plan.rows, :c]
            sides[:c, rows] = turned(ref[: plan.rows, c:])
            for h in range(plan.heads):
                below = slice(c + h * HEAD_DIM, c + (h + 1) * HEAD_DIM)
                sides[below, rows] = ref[plan.rows :, h * plan.rows : (h + 1) * plan.rows]
        for h in range(plan.heads):
            mine = slice(h * HEAD_DIM, (h + 1) * HEAD_DIM)
            below = slice(c + h * HEAD_DIM, c + (h + 1) * HEAD_DIM)
            key = keys[:, mine]
            row_norm = dec_ref[:, h : h + 1] * LOG2E
            for lanes in lane_tiles(plan):
                scores = nn(key, query[mine, lanes]) * (HEAD_DIM**-0.5 * LOG2E)
                dec = jnp.exp2(scores - row_norm).astype(jnp.bfloat16)
                enc = jnp.exp2(scores - enc_ref[h : h + 1, lanes] * LOG2E).astype(jnp.bfloat16)
                store_blocks(plan, outs, mine, lanes, nn(sides[mine, :], dec))
                store_blocks(plan, outs, below, lanes, nn(sides[below, :], enc))

    outs = [shaped((2 * c, plan.block), jnp.float32)] * plan.plane
    scratch = [
        pltpu.VMEM((c, m), jnp.bfloat16),
        pltpu.VMEM((2 * c, plan.points), jnp.bfloat16),
        pltpu.VMEM((plan.points, c), jnp.bfloat16),
    ]
    flops = 6 * plan.points * m * c
    return call(kernel, outs, (*lats, *pts, dec_norm, enc_norm), scratch, flops)


def decoder_pass(plan, lats, pts, dec_norm, heads):
    n_lat = len(lats)
    c, m = plan.cols, plan.latents

    def kernel(*refs):
        lat_refs, pts_refs, dec_ref = refs[:n_lat], refs[n_lat:-6], refs[-6]
        key_ref, lat_ref = refs[-5:-3]
        both, keys_t, ds = refs[-3:]
        for k, ref in enumerate(lat_refs):
            both[:, k * plan.block : (k + 1) * plan.block] = ref[...]
        for j, ref in enumerate(pts_refs):
            keys_t[:, j * plan.rows : (j + 1) * plan.rows] = turned(ref[: plan.rows, :c])
        for at, h in enumerate(heads):
            mine = slice(h * HEAD_DIM, (h + 1) * HEAD_DIM)
            put = slice(at * HEAD_DIM, (at + 1) * HEAD_DIM)
            other = slice(c + h * HEAD_DIM, c + (h + 1) * HEAD_DIM)
            for j, ref in enumerate(pts_refs):
                rows = slice(j * plan.rows, (j + 1) * plan.rows)
                scores = nn(ref[: plan.rows, mine], both[mine, :]) * (HEAD_DIM**-0.5 * LOG2E)
                dec = jnp.exp2(scores - dec_ref[rows, h : h + 1] * LOG2E)
                grad = nn(ref[: plan.rows, other], both[other, :])
                total = jnp.sum(dec * grad, axis=1, keepdims=True)
                tile = (dec * (grad - total)).astype(jnp.bfloat16)
                ds[rows, :] = tile
            key_ref[put, :] = nt(both[mine, :], ds[...])
            lat_ref[put, :] = nn(keys_t[mine, :], ds[...])

    width = len(heads) * HEAD_DIM
    outs = [shaped((width, plan.points), jnp.float32), shaped((width, m), jnp.float32)]
    scratch = [
        pltpu.VMEM((2 * c, m), jnp.bfloat16),
        pltpu.VMEM((c, plan.points), jnp.bfloat16),
        pltpu.VMEM((plan.points, m), jnp.bfloat16),
    ]
    flops = 8 * plan.points * m * width
    return call(kernel, outs, (*lats, *pts, dec_norm), scratch, flops)


def add_and_scale(plan, mine, theirs):
    tall = mine[0].shape[0]

    def kernel(*refs):
        n = len(mine)
        for k, (a, b, out) in enumerate(zip(refs[:n], refs[n : 2 * n], refs[2 * n :], strict=True)):
            total = a[...] + b[...]
            if k == 0:
                out[...] = total
                continue
            sizes = []
            for at in range(0, tall, HEAD_DIM):
                part = total[at : at + HEAD_DIM]
                most = jnp.max(jnp.abs(part), axis=0, keepdims=True)
                size = jnp.ceil(jnp.log2(jnp.maximum(most, SMALLEST)))
                out[at : at + HEAD_DIM, :] = part * jnp.exp2(HALF_SIZE - size)
                sizes.append(size)
            fill = jnp.zeros((16 - len(sizes), plan.block), jnp.float32)
            out[tall:, :] = jnp.concatenate([*sizes, fill], axis=0)

    outs = [shaped((tall + 16 * (k > 0), plan.block), jnp.float32) for k in range(len(mine))]
    return call(kernel, outs, (*mine, *theirs))


def scaled_sum(own, *scaled):
    tall = own.shape[0]
    pieces = []
    for n, at in enumerate(range(0, tall, HEAD_DIM)):
        piece = own[at : at + HEAD_DIM, :]
        for ref in scaled:
            size = ref[tall + n : tall + n + 1, :]
            piece = piece + ref[at : at + HEAD_DIM, :] * jnp.exp2(size - HALF_SIZE)
        pieces.append(piece)
    return jnp.concatenate(pieces, axis=0)


def reduce_mix(plan, parts):
    c, hs = plan.cols, plan.heads

    def kernel(*refs):
        *ins, out = refs
        total = scaled_sum(*ins)
        half = total[:c].astype(jnp.bfloat16)
        out[:c, :] = half
        product = half.astype(jnp.float32) * total[c:]
        sums = [
            jnp.sum(product[h * HEAD_DIM : (h + 1) * HEAD_DIM], axis=0, keepdims=True) for h in range(hs)
        ]
        fill = jnp.zeros((16 - 3 * hs, plan.block), jnp.float32)
        stack = jnp.concatenate([*split3(jnp.concatenate(sums, axis=0)), fill], axis=0)
        out[c:, :] = stack.astype(jnp.bfloat16)

    outs = [shaped((plan.ct_rows, plan.block), jnp.bfloat16)]
    return call(kernel, outs, parts)[0]


def encoder_pass(plan, lats, pts, norm, mixes, before):
    places = [(part, at) for part, (heads, _) in enumerate(before) for at in range(len(heads))]
    n_lat, n_pts, n_mix = len(lats), len(pts), len(mixes)
    c, m, hs = plan.cols, plan.latents, plan.heads

    def kernel(*refs):
        refs = list(refs)

        def take(n):
            got = refs[:n]
            del refs[:n]
            return got

        lat_refs, pts_refs = take(n_lat), take(n_pts)
        (norm_ref,) = take(1)
        mix_refs = take(n_mix)
        parts_in = [take(2) for _ in before]
        pts_outs, lat_outs = take(n_pts), take(n_lat)
        query, mix, keys, keys_t, values, ds, encs = refs
        for k, ref in enumerate(lat_refs):
            query[:, k * plan.block : (k + 1) * plan.block] = ref[:c, :]
        for k, ref in enumerate(mix_refs):
            mix[:, k * plan.block : (k + 1) * plan.block] = ref[...]
        for j, ref in enumerate(pts_refs):
            rows = slice(j * plan.rows, (j + 1) * plan.rows)
            keys[rows, :] = ref[: plan.rows, :c]
            keys_t[:, rows] = turned(ref[: plan.rows, :c])
            across = [ref[plan.rows :, h * plan.rows : (h + 1) * plan.rows] for h in range(hs)]
            values[rows, :] = turned(jnp.concatenate(across, axis=0))
        tail = mix[c:, :].astype(jnp.float32)
        columns = (tail[:hs] + tail[hs : 2 * hs]) + tail[2 * hs : 3 * hs]
        tiles = lane_tiles(plan)
        sums = {}

        def weigh(h, t, slot):
            mine, lanes = slice(h * HEAD_DIM, (h + 1) * HEAD_DIM), tiles[t]
            scores = nn(keys[:, mine], query[mine, lanes]) * (HEAD_DIM**-0.5 * LOG2E)
            enc = jnp.exp2(scores - norm_ref[h : h + 1, lanes] * LOG2E)
            grad = nn(values[:, mine], mix[mine, lanes])
            encs[slot] = enc.astype(jnp.bfloat16)
            ds[slot] = (enc * (grad - columns[h : h + 1, lanes])).astype(jnp.bfloat16)

        def gather(h, t, slot):
            mine, lanes = slice(h * HEAD_DIM, (h + 1) * HEAD_DIM), tiles[t]
            part, at = places[h]
            key_in, lat_in = parts_in[part]
            put = slice(at * HEAD_DIM, (at + 1) * HEAD_DIM)
            lat = (lat_in[put, lanes] + nn(keys_t[mine, :], ds[slot])) * HEAD_DIM**-0.5
            store_blocks(plan, lat_outs, mine, lanes, lat)
            key, value = nt(query[mine, lanes], ds[slot]), nt(mix[mine, lanes], encs[slot])
            key = key + (sums[h][0] if t else key_in[put, :])
            sums[h] = (key, value + sums[h][1] if t else value)
            if t < len(tiles) - 1:
                return
            key, value = sums.pop(h)
            key = (key * HEAD_DIM**-0.5).T.astype(jnp.bfloat16)
            value = value.T.astype(jnp.bfloat16)
            for j, out in enumerate(pts_outs):
                rows = slice(j * plan.rows, (j + 1) * plan.rows)
                out[:, mine] = key[rows]
                out[:, c + h * HEAD_DIM : c + (h + 1) * HEAD_DIM] = value[rows]

        work = [(h, t) for h in range(hs) for t in range(len(tiles))]
        for n, place in enumerate(work):
            weigh(*place, n % SLOTS)
            if n >= LAG:
                gather(*work[n - LAG], (n - LAG) % SLOTS)
        for n in range(len(work) - LAG, len(work)):
            gather(*work[n], n % SLOTS)

    outs = [shaped((plan.rows, 2 * c), jnp.bfloat16)] * n_pts
    outs += [shaped((c, plan.block), jnp.float32)] * n_lat
    scratch = [
        pltpu.VMEM((c, m), jnp.bfloat16),
        pltpu.VMEM((plan.ct_rows, m), jnp.bfloat16),
        pltpu.VMEM((plan.points, c), jnp.bfloat16),
        pltpu.VMEM((c, plan.points), jnp.bfloat16),
        pltpu.VMEM((plan.points, c), jnp.bfloat16),
        pltpu.VMEM((SLOTS, plan.points, 2 * plan.block), jnp.bfloat16),
        pltpu.VMEM((SLOTS, plan.points, 2 * plan.block), jnp.bfloat16),
    ]
    flops = 10 * plan.points * m * c
    args = (*lats, *pts, norm, *mixes, *(a for _, part in before for a in part))
    got = call(kernel, outs, args, scratch, flops)
    return got[:n_pts], got[n_pts:]


def reduce_latents(plan, parts):
    def kernel(*refs):
        ins, outs = refs[: len(parts)], refs[len(parts) :]
        total = scaled_sum(*ins).T
        for j, out in enumerate(outs):
            rows = total[j * plan.lat_rows : (j + 1) * plan.lat_rows]
            n, half = plan.lat_rows, plan.lat_rows // 2
            out[:n, :] = rows[:, :LANES]
            out[n:, :] = jnp.concatenate([rows[:half, LANES:], rows[half:, LANES:]], axis=1)

    outs = [shaped((3 * plan.lat_rows // 2, LANES), jnp.float32)] * GROUPS
    return call(kernel, outs, parts)


def place_points(plan, slots):
    def kernel(*refs):
        ins, (key_out, value_out) = refs[:GROUPS], refs[GROUPS:]
        z = group_index(plan)
        c = plan.cols
        pieces = by_group([r[...].astype(jnp.float32) for r in ins], z)
        for g, piece in enumerate(pieces):
            key_out[:, g * c : (g + 1) * c] = piece[:, :c].astype(jnp.bfloat16)
            value_out[:, g * c : (g + 1) * c] = piece[:, c:].astype(jnp.bfloat16)

    outs = [shaped((plan.rows, plan.width), jnp.bfloat16)] * 2
    return call(kernel, outs, slots)


def place_latents(plan, slots):
    def kernel(*refs):
        *ins, out = refs
        n, at = plan.lat_rows, plan.cols - LANES
        for g, piece in enumerate(by_group([r[...] for r in ins], group_index(plan))):
            rest = jnp.concatenate([piece[n:, :at], piece[n:, at:]], axis=0)
            out[:, g * plan.cols : (g + 1) * plan.cols] = jnp.concatenate([piece[:n], rest], axis=1)

    outs = [shaped((plan.lat_rows, plan.width), jnp.float32)]
    return call(kernel, outs, slots)[0]


def grouped(
    plan, point_keys, point_values, out_grad, decoder_norm, latent_query, latent_out, encoder_norm
):
    def over_group(slots):
        got = [slots[0]]
        for j in range(1, GROUPS):
            got.append(plan.exchange(slots[j], True, j))
        return got

    def chip_steps():
        return [k for k in range(plan.plane) if not k & plan.fast]

    def from_chips(blocks):
        got = []
        for k, block in zip(chip_steps(), blocks, strict=True):
            got.append(plan.exchange(block, False, k) if k else block)
        return got

    def sum_cores(blocks):
        near = chip_steps()
        theirs = [plan.exchange(blocks[k | plan.fast], False, plan.fast) for k in near]
        return add_and_scale(plan, [blocks[k] for k in near], theirs)

    def sum_chips(blocks):
        halves = [blocks[0], *(block.astype(jnp.float16) for block in blocks[1:])]
        return [block.astype(jnp.float32) for block in from_chips(halves)]

    def to_plane(block):
        got = dict(zip(chip_steps(), from_chips([block] * len(chip_steps())), strict=True))
        for k in chip_steps():
            got[k | plan.fast] = plan.exchange(got[k], False, plan.fast)
        return tuple(got[k] for k in range(plan.plane))

    lat_slots, pts = pack(
        plan, latent_query, latent_out, decoder_norm, point_keys, out_grad, point_values
    )
    lat_slots = over_group(lat_slots)
    pts = over_group(pts)
    norm = order_norm(plan, encoder_norm)
    block, dec_norm = turn_latents(plan, lat_slots)
    lats = to_plane(block)
    cores = sum_cores(first_pass(plan, lats, pts, dec_norm, norm))
    early, late = tuple(range(plan.heads))[:1], tuple(range(plan.heads))[1:]
    before = [(early, decoder_pass(plan, lats, pts, dec_norm, early))]
    sums = sum_chips(cores)
    before.append((late, decoder_pass(plan, lats, pts, dec_norm, late)))
    mixes = to_plane(reduce_mix(plan, sums))
    pts_out, lat_out = encoder_pass(plan, lats, pts, norm, mixes, before)
    lat_out = sum_chips(sum_cores(lat_out))
    pts_out = over_group(pts_out)
    lat_rows = over_group(reduce_latents(plan, lat_out))
    keys_grad, values_grad = place_points(plan, pts_out)
    return keys_grad, values_grad, place_latents(plan, lat_rows)


def column(block, current):
    return lax.dynamic_slice_in_dim(block, current * HEAD_DIM, HEAD_DIM, 1)


def put_head(total, piece, current):
    return lax.dynamic_update_slice_in_dim(total, piece, current * HEAD_DIM, 1)


def add_head(total, piece, current):
    return put_head(total, column(total, current) + piece, current)


def across(left, right):
    return lax.dot_general(
        left, right, (((1,), (1,)), ((), ())), preferred_element_type=jnp.float32
    )


def down_rows(left, right):
    return lax.dot_general(
        left, right, (((0,), (0,)), ((), ())), preferred_element_type=jnp.float32
    )


def gathered(
    point_keys, point_values, out_grad, decoder_norm, latent_query, latent_out, encoder_norm
):
    scale_factor = HEAD_DIM ** (-0.5)
    lat_all, out_all = (
        lax.all_gather(latent_query, ("pa", "pb"), axis=0, tiled=True),
        lax.all_gather(latent_out, ("pa", "pb"), axis=0, tiled=True),
    )
    point_rows = point_keys.shape[0]
    latent_rows = lat_all.shape[0]
    width = point_keys.shape[1]

    def encoder_row(current):
        return lax.dynamic_slice_in_dim(encoder_norm, current, 1, 0)

    def pass_one(current, state):
        mix_acc, query_acc, key_acc, weighted_acc = state
        key_head = column(point_keys, current)
        grad_head = column(out_grad, current)
        lat_head = column(lat_all, current)
        scores = across(key_head, lat_head) * scale_factor
        decoder_weights = jnp.exp(scores - lax.dynamic_slice_in_dim(decoder_norm, current, 1, 0).T)
        decoder_gradient = across(grad_head, column(out_all, current))
        row_total = jnp.sum(decoder_weights * decoder_gradient, axis=1, keepdims=True)
        decoder_scores_grad = (decoder_weights * (decoder_gradient - row_total)).astype(
            jnp.bfloat16
        )
        mix_acc = put_head(
            mix_acc, down_rows(decoder_weights.astype(jnp.bfloat16), grad_head), current
        )
        query_acc = put_head(
            query_acc, down_rows(decoder_scores_grad, key_head) * scale_factor, current
        )
        key_acc = put_head(
            key_acc,
            jnp.dot(decoder_scores_grad, lat_head, preferred_element_type=jnp.float32)
            * scale_factor,
            current,
        )
        return (mix_acc, query_acc, key_acc, weighted_acc)

    weighted_blank = jnp.zeros((1, 1), jnp.float32)
    latent_blank = jnp.zeros((latent_rows, width), jnp.float32)
    begin = (
        latent_blank,
        latent_blank,
        jnp.zeros((point_rows, width), jnp.float32),
        weighted_blank,
    )
    mix_acc, query_acc, key_acc, _ = lax.fori_loop(0, HEADS, pass_one, begin)
    mix_grad = lax.psum(mix_acc, ("pa", "pb"))
    mixing_portion = mix_grad.astype(jnp.bfloat16)

    def pass_two(current, state):
        partial_rows, value_acc = state
        scores = across(column(point_keys, current), column(lat_all, current)) * scale_factor
        encoder_portion = jnp.exp(scores - encoder_row(current)).astype(jnp.bfloat16)
        mix_head = column(mixing_portion, current)
        encoder_gradient = across(column(point_values, current), mix_head)
        sums = jnp.sum(encoder_portion.astype(jnp.float32) * encoder_gradient, axis=0)[None, :]
        partial_rows = lax.dynamic_update_slice_in_dim(partial_rows, sums, current, 0)
        value_acc = put_head(
            value_acc,
            jnp.dot(encoder_portion, mix_head, preferred_element_type=jnp.float32),
            current,
        )
        return (partial_rows, value_acc)

    partial_rows, value_acc = lax.fori_loop(
        0,
        HEADS,
        pass_two,
        (jnp.zeros((HEADS, latent_rows), jnp.float32), jnp.zeros((point_rows, width), jnp.float32)),
    )
    column_total = lax.psum(partial_rows, ("pa", "pb"))

    def pass_three(current, state):
        query_acc, key_acc, value_acc = state
        key_head = column(point_keys, current)
        lat_head = column(lat_all, current)
        mix_head = column(mixing_portion, current)
        scores = across(key_head, lat_head) * scale_factor
        encoder = jnp.exp(scores - encoder_row(current))
        encoder_gradient = across(column(point_values, current), mix_head)
        encoder_scores_grad = (
            encoder * (encoder_gradient - lax.dynamic_slice_in_dim(column_total, current, 1, 0))
        ).astype(jnp.bfloat16)
        query_acc = add_head(
            query_acc, down_rows(encoder_scores_grad, key_head) * scale_factor, current
        )
        key_acc = add_head(
            key_acc,
            jnp.dot(encoder_scores_grad, lat_head, preferred_element_type=jnp.float32)
            * scale_factor,
            current,
        )
        return (query_acc, key_acc, value_acc)

    query_acc, key_acc, value_acc = lax.fori_loop(
        0, HEADS, pass_three, (query_acc, key_acc, value_acc)
    )
    latent_grad = lax.psum_scatter(query_acc, ("pa", "pb"), scatter_dimension=0, tiled=True)
    return (key_acc.astype(jnp.bfloat16), value_acc.astype(jnp.bfloat16), latent_grad)


def solution(mesh):
    in_specs = (
        P(("pa", "pb"), None),
        P(("pa", "pb"), None),
        P(("pa", "pb"), None),
        P(None, ("pa", "pb")),
        P(("pa", "pb"), None),
        P(("pa", "pb"), None),
        P(),
    )
    out_specs = (P(("pa", "pb"), None), P(("pa", "pb"), None), P(("pa", "pb"), None))
    npa, npb = mesh.shape["pa"], mesh.shape["pb"]

    def shards(*args):
        plan_of = (npa, npb, args[0].shape[0], args[4].shape[0], args[0].shape[1])
        if Plan.fits(*plan_of):
            return grouped(Plan(*plan_of), *args)
        return gathered(*args)

    return jax.shard_map(shards, mesh=mesh, in_specs=in_specs, out_specs=out_specs, check_vma=False)
```

```python
import math

import jax
import jax.numpy as jnp
from jax import lax
from jax.experimental import pallas as pl
from jax.experimental.pallas import tpu as pltpu
from jax.sharding import PartitionSpec as P


HEADS = 12
HEAD_DIM = 64
LANES = 128
AXES = ("pa", "pb")
MOST_IN_PLANE = 16
HALF_SIZE, SMALLEST = 14.0, 2.0**-100
LAG, SLOTS = 1, 3
GROUPS = 4
VMEM_BYTES = 20 * 2**20
LOG2E = math.log2(math.e)


class Plan:
    def __init__(self, npa, npb, rows, lat_rows, width):
        self.npa, self.npb = npa, npb
        self.fast = npb // GROUPS
        self.plane = npa * self.fast
        self.rows, self.lat_rows, self.width = rows, lat_rows, width
        self.heads = HEADS // GROUPS
        self.cols = self.heads * HEAD_DIM
        self.points = rows * GROUPS
        self.block = lat_rows * GROUPS
        self.latents = self.block * self.plane
        self.slot = lat_rows + 16
        self.ct_rows = self.cols + 16

    @staticmethod
    def fits(npa, npb, rows, lat_rows, width):
        def power(v):
            return v > 0 and v & (v - 1) == 0

        return (
            power(npa)
            and power(npb)
            and npb % GROUPS == 0
            and npa * npb // GROUPS <= MOST_IN_PLANE
            and lat_rows * GROUPS == LANES
            and rows == LANES
            and HEADS % GROUPS == 0
            and HEADS // GROUPS * rows == 2 * HEADS // GROUPS * HEAD_DIM
            and width == HEADS * HEAD_DIM
            and 2 * width // GROUPS == 3 * LANES
        )

    def exchange(self, value, over_group, step):
        pairs = []
        for a in range(self.npa):
            for b in range(self.npb):
                z, f = divmod(b, self.fast)
                if over_group:
                    a2, z2, f2 = a, z ^ step, f
                else:
                    a2, z2, f2 = a ^ (step // self.fast), z, f ^ (step % self.fast)
                pairs.append((a * self.npb + b, a2 * self.npb + z2 * self.fast + f2))
        return lax.ppermute(value, AXES, pairs)


def call(kernel, outs, args, scratch=(), flops=0, space=pltpu.VMEM):
    nbytes = sum(a.size * a.dtype.itemsize for a in args)
    nbytes += sum(math.prod(o.shape) * o.dtype.itemsize for o in outs)
    return pl.pallas_call(
        kernel,
        out_shape=tuple(outs),
        in_specs=[pl.BlockSpec(memory_space=space)] * len(args),
        out_specs=tuple(pl.BlockSpec(memory_space=pltpu.VMEM) for _ in outs),
        scratch_shapes=list(scratch),
        cost_estimate=pl.CostEstimate(flops=flops, bytes_accessed=nbytes, transcendentals=flops // 256),
        compiler_params=pltpu.CompilerParams(vmem_limit_bytes=VMEM_BYTES),
    )(*args)


def call_from_hbm(kernel, outs, args):
    n = len(args)

    def body(*refs):
        held, sems = refs[-n - 1 : -1], refs[-1]
        copies = [
            pltpu.make_async_copy(src, dst, sems.at[i])
            for i, (src, dst) in enumerate(zip(refs[:n], held, strict=True))
        ]
        for copy in copies:
            copy.start()
        for copy in copies:
            copy.wait()
        kernel(*held, *refs[n : -n - 1])

    scratch = [pltpu.VMEM(a.shape, a.dtype) for a in args] + [pltpu.SemaphoreType.DMA((n,))]
    args = [pltpu.with_memory_space_constraint(a, pltpu.HBM) for a in args]
    return call(body, outs, args, scratch, space=pltpu.HBM)


def shaped(shape, dtype):
    return jax.ShapeDtypeStruct(shape, dtype)


def by_group(pieces, z):
    out = list(pieces)
    bit = 1
    while bit < len(out):
        on = (z & bit) != 0
        out = [jnp.where(on, out[g ^ bit], out[g]) for g in range(len(out))]
        bit *= 2
    return out


def group_index(plan):
    return lax.axis_index("pb") // plan.fast


def split3(value):
    hi = value.astype(jnp.bfloat16).astype(jnp.float32)
    rest = value - hi
    mid = rest.astype(jnp.bfloat16).astype(jnp.float32)
    return hi, mid, rest - mid


def nn(a, b):
    return lax.dot_general(a, b, (((1,), (0,)), ((), ())), preferred_element_type=jnp.float32)


def nt(a, b):
    return lax.dot_general(a, b, (((1,), (1,)), ((), ())), preferred_element_type=jnp.float32)


def turned(block):
    return block.astype(jnp.float32).T.astype(block.dtype)


def pack(plan, query, out, norm, keys, grads, values):
    def kernel(q_ref, o_ref, n_ref, k_ref, g_ref, v_ref, *outs):
        z = group_index(plan)
        c, hs = plan.cols, plan.heads
        q, o = q_ref[...].astype(jnp.float32), o_ref[...].astype(jnp.float32)
        parts = split3(n_ref[...])
        fill = jnp.zeros((plan.slot - plan.lat_rows - 3, hs * plan.rows), jnp.float32)
        pieces = []
        for g in range(GROUPS):
            top = jnp.concatenate([q[:, g * c : (g + 1) * c], o[:, g * c : (g + 1) * c]], axis=1)
            lines = [
                jnp.concatenate([p[h : h + 1, :] for h in range(g * hs, (g + 1) * hs)], axis=1) for p in parts
            ]
            pieces.append(jnp.concatenate([top, *lines, fill], axis=0).astype(jnp.bfloat16))
        for ref, piece in zip(outs[:GROUPS], by_group(pieces, z), strict=True):
            ref[...] = piece
        outs = outs[GROUPS:]
        for first, ref in ((0, k_ref), (1, g_ref)):
            pieces = by_group([ref[:, g * c : (g + 1) * c] for g in range(GROUPS)], z)
            for out, piece in zip(outs, pieces, strict=True):
                out[: plan.rows, first * c : (first + 1) * c] = piece
        across = v_ref[...].T
        pieces = by_group([across[g * c : (g + 1) * c] for g in range(GROUPS)], z)
        for out, piece in zip(outs, pieces, strict=True):
            for h in range(hs):
                lanes = slice(h * plan.rows, (h + 1) * plan.rows)
                out[plan.rows :, lanes] = piece[h * HEAD_DIM : (h + 1) * HEAD_DIM]

    outs = [shaped((plan.slot, 2 * plan.cols), jnp.bfloat16)] * GROUPS
    outs += [shaped((plan.rows + HEAD_DIM, 2 * plan.cols), jnp.bfloat16)] * GROUPS
    got = call_from_hbm(kernel, outs, (query, out, norm, keys, grads, values))
    return got[:GROUPS], got[GROUPS:]


def order_norm(plan, norm):
    def kernel(n_ref, out_ref):
        z = group_index(plan)
        member = lax.axis_index("pa") * plan.npb + lax.axis_index("pb")
        hs, m = plan.heads, plan.latents
        rows = by_group([n_ref[g * hs : (g + 1) * hs, :] for g in range(GROUPS)], z)[0]
        fill = jnp.zeros((16 - 3 * hs, m), jnp.float32)
        stack = jnp.concatenate([*split3(rows), fill], axis=0).astype(jnp.bfloat16)
        lane = lax.broadcasted_iota(jnp.int32, (1, m), 1)
        inner, j, k = lane % plan.lat_rows, (lane // plan.lat_rows) % GROUPS, lane // plan.block
        owner = (k // plan.fast) * plan.npb + j * plan.fast + k % plan.fast
        source = (owner ^ member) * plan.lat_rows + inner
        total = jnp.zeros((16, m), jnp.float32)
        step = 256
        for start in range(0, m, step):
            row = lax.broadcasted_iota(jnp.int32, (step, m), 0) + start
            chosen = jnp.where(row == source, 1.0, 0.0).astype(jnp.bfloat16)
            total = total + nn(stack[:, start : start + step], chosen)
        out_ref[0:hs, :] = (total[:hs] + total[hs : 2 * hs]) + total[2 * hs : 3 * hs]

    outs = [shaped((plan.heads, plan.latents), jnp.float32)]
    return call_from_hbm(kernel, outs, (norm,))[0]


def turn_latents(plan, slots):
    def kernel(*refs):
        *slots, out, norm_out = refs
        n, rows = plan.lat_rows, plan.rows
        slots = [s[...] for s in slots]
        out[...] = turned(jnp.concatenate([s[:n] for s in slots], axis=0))
        for j, slot in enumerate(slots):
            parts = slot[n : n + 3].astype(jnp.float32)
            line = (parts[0:1] + parts[1:2]) + parts[2:3]
            lines = [line[:, h * rows : (h + 1) * rows] for h in range(plan.heads)]
            fill = jnp.zeros((LANES - plan.heads, rows), jnp.float32)
            norm_out[j * rows : (j + 1) * rows, :] = jnp.concatenate([*lines, fill], axis=0).T

    outs = [
        shaped((2 * plan.cols, plan.block), jnp.bfloat16),
        shaped((plan.points, LANES), jnp.float32),
    ]
    return call(kernel, outs, slots)


def lane_tiles(plan):
    width = min(2 * plan.block, plan.latents)
    return [slice(at, at + width) for at in range(0, plan.latents, width)]


def store_blocks(plan, outs, rows, lanes, value):
    for at in range(lanes.start, lanes.stop, plan.block):
        outs[at // plan.block][rows, :] = value[:, at - lanes.start : at - lanes.start + plan.block]


def first_pass(plan, lats, pts, dec_norm, enc_norm):
    n_lat = len(lats)
    c, m = plan.cols, plan.latents

    def kernel(*refs):
        lat_refs, pts_refs, (dec_ref, enc_ref) = refs[:n_lat], refs[n_lat:-6 - n_lat], refs[-6 - n_lat : -4 - n_lat]
        outs, kept = refs[-4 - n_lat : -4], refs[-4]
        query, sides, keys = refs[-3:]
        for k, ref in enumerate(lat_refs):
            query[:, k * plan.block : (k + 1) * plan.block] = ref[:c, :]
        for j, ref in enumerate(pts_refs):
            rows = slice(j * plan.rows, (j + 1) * plan.rows)
            keys[rows, :] = ref[: plan.rows, :c]
            sides[:c, rows] = turned(ref[: plan.rows, c:])
            for h in range(plan.heads):
                below = slice(c + h * HEAD_DIM, c + (h + 1) * HEAD_DIM)
                sides[below, rows] = ref[plan.rows :, h * plan.rows : (h + 1) * plan.rows]
        for h in range(plan.heads):
            mine = slice(h * HEAD_DIM, (h + 1) * HEAD_DIM)
            below = slice(c + h * HEAD_DIM, c + (h + 1) * HEAD_DIM)
            key = keys[:, mine]
            row_norm = dec_ref[:, h : h + 1] * LOG2E
            for lanes in lane_tiles(plan):
                scores = nn(key, query[mine, lanes]) * (HEAD_DIM**-0.5 * LOG2E)
                dec = jnp.exp2(scores - row_norm).astype(jnp.bfloat16)
                enc = jnp.exp2(scores - enc_ref[h : h + 1, lanes] * LOG2E)
                kept[h, :, lanes] = enc
                store_blocks(plan, outs, mine, lanes, nn(sides[mine, :], dec))
                store_blocks(plan, outs, below, lanes, nn(sides[below, :], enc.astype(jnp.bfloat16)))

    outs = [shaped((2 * c, plan.block), jnp.float32)] * plan.plane
    outs += [shaped((plan.heads, plan.points, m), jnp.float32)]
    scratch = [
        pltpu.VMEM((c, m), jnp.bfloat16),
        pltpu.VMEM((2 * c, plan.points), jnp.bfloat16),
        pltpu.VMEM((plan.points, c), jnp.bfloat16),
    ]
    flops = 6 * plan.points * m * c
    *sums, kept = call(kernel, outs, (*lats, *pts, dec_norm, enc_norm), scratch, flops)
    return sums, kept


def decoder_pass(plan, lats, pts, dec_norm, heads):
    n_lat = len(lats)
    c, m = plan.cols, plan.latents

    def kernel(*refs):
        lat_refs, pts_refs, dec_ref = refs[:n_lat], refs[n_lat:-6], refs[-6]
        key_ref, lat_ref = refs[-5:-3]
        both, keys_t, ds = refs[-3:]
        for k, ref in enumerate(lat_refs):
            both[:, k * plan.block : (k + 1) * plan.block] = ref[...]
        for j, ref in enumerate(pts_refs):
            keys_t[:, j * plan.rows : (j + 1) * plan.rows] = turned(ref[: plan.rows, :c])
        for at, h in enumerate(heads):
            mine = slice(h * HEAD_DIM, (h + 1) * HEAD_DIM)
            put = slice(at * HEAD_DIM, (at + 1) * HEAD_DIM)
            other = slice(c + h * HEAD_DIM, c + (h + 1) * HEAD_DIM)
            for j, ref in enumerate(pts_refs):
                rows = slice(j * plan.rows, (j + 1) * plan.rows)
                scores = nn(ref[: plan.rows, mine], both[mine, :]) * (HEAD_DIM**-0.5 * LOG2E)
                dec = jnp.exp2(scores - dec_ref[rows, h : h + 1] * LOG2E)
                grad = nn(ref[: plan.rows, other], both[other, :])
                total = jnp.sum(dec * grad, axis=1, keepdims=True)
                tile = (dec * (grad - total)).astype(jnp.bfloat16)
                ds[rows, :] = tile
            key_ref[put, :] = nt(both[mine, :], ds[...])
            lat_ref[put, :] = nn(keys_t[mine, :], ds[...])

    width = len(heads) * HEAD_DIM
    outs = [shaped((width, plan.points), jnp.float32), shaped((width, m), jnp.float32)]
    scratch = [
        pltpu.VMEM((2 * c, m), jnp.bfloat16),
        pltpu.VMEM((c, plan.points), jnp.bfloat16),
        pltpu.VMEM((plan.points, m), jnp.bfloat16),
    ]
    flops = 8 * plan.points * m * width
    return call(kernel, outs, (*lats, *pts, dec_norm), scratch, flops)


def add_and_scale(plan, mine, theirs):
    tall = mine[0].shape[0]

    def kernel(*refs):
        n = len(mine)
        for k, (a, b, out) in enumerate(zip(refs[:n], refs[n : 2 * n], refs[2 * n :], strict=True)):
            total = a[...] + b[...]
            if k == 0:
                out[...] = total
                continue
            sizes = []
            for at in range(0, tall, HEAD_DIM):
                part = total[at : at + HEAD_DIM]
                most = jnp.max(jnp.abs(part), axis=0, keepdims=True)
                size = jnp.ceil(jnp.log2(jnp.maximum(most, SMALLEST)))
                out[at : at + HEAD_DIM, :] = part * jnp.exp2(HALF_SIZE - size)
                sizes.append(size)
            fill = jnp.zeros((16 - len(sizes), plan.block), jnp.float32)
            out[tall:, :] = jnp.concatenate([*sizes, fill], axis=0)

    outs = [shaped((tall + 16 * (k > 0), plan.block), jnp.float32) for k in range(len(mine))]
    return call(kernel, outs, (*mine, *theirs))


def scaled_sum(own, *scaled):
    tall = own.shape[0]
    pieces = []
    for n, at in enumerate(range(0, tall, HEAD_DIM)):
        piece = own[at : at + HEAD_DIM, :]
        for ref in scaled:
            size = ref[tall + n : tall + n + 1, :]
            piece = piece + ref[at : at + HEAD_DIM, :] * jnp.exp2(size - HALF_SIZE)
        pieces.append(piece)
    return jnp.concatenate(pieces, axis=0)


def reduce_mix(plan, parts):
    c, hs = plan.cols, plan.heads

    def kernel(*refs):
        *ins, out = refs
        total = scaled_sum(*ins)
        half = total[:c].astype(jnp.bfloat16)
        out[:c, :] = half
        product = half.astype(jnp.float32) * total[c:]
        sums = [
            jnp.sum(product[h * HEAD_DIM : (h + 1) * HEAD_DIM], axis=0, keepdims=True) for h in range(hs)
        ]
        fill = jnp.zeros((16 - 3 * hs, plan.block), jnp.float32)
        stack = jnp.concatenate([*split3(jnp.concatenate(sums, axis=0)), fill], axis=0)
        out[c:, :] = stack.astype(jnp.bfloat16)

    outs = [shaped((plan.ct_rows, plan.block), jnp.bfloat16)]
    return call(kernel, outs, parts)[0]


def encoder_pass(plan, lats, pts, kept, mixes, before):
    places = [(part, at) for part, (heads, _) in enumerate(before) for at in range(len(heads))]
    n_lat, n_pts, n_mix = len(lats), len(pts), len(mixes)
    c, m, hs = plan.cols, plan.latents, plan.heads

    def kernel(*refs):
        refs = list(refs)

        def take(n):
            got = refs[:n]
            del refs[:n]
            return got

        lat_refs, pts_refs = take(n_lat), take(n_pts)
        (kept_ref,) = take(1)
        mix_refs = take(n_mix)
        parts_in = [take(2) for _ in before]
        pts_outs, lat_outs = take(n_pts), take(n_lat)
        query, mix, keys_t, values, ds, encs = refs
        for k, ref in enumerate(lat_refs):
            query[:, k * plan.block : (k + 1) * plan.block] = ref[:c, :]
        for k, ref in enumerate(mix_refs):
            mix[:, k * plan.block : (k + 1) * plan.block] = ref[...]
        for j, ref in enumerate(pts_refs):
            rows = slice(j * plan.rows, (j + 1) * plan.rows)
            keys_t[:, rows] = turned(ref[: plan.rows, :c])
            across = [ref[plan.rows :, h * plan.rows : (h + 1) * plan.rows] for h in range(hs)]
            values[rows, :] = turned(jnp.concatenate(across, axis=0))
        tail = mix[c:, :].astype(jnp.float32)
        columns = (tail[:hs] + tail[hs : 2 * hs]) + tail[2 * hs : 3 * hs]
        tiles = lane_tiles(plan)
        sums = {}

        def weigh(h, t, slot):
            mine, lanes = slice(h * HEAD_DIM, (h + 1) * HEAD_DIM), tiles[t]
            enc = kept_ref[h, :, lanes]
            grad = nn(values[:, mine], mix[mine, lanes])
            encs[slot] = enc.astype(jnp.bfloat16)
            ds[slot] = (enc * (grad - columns[h : h + 1, lanes])).astype(jnp.bfloat16)

        def gather(h, t, slot):
            mine, lanes = slice(h * HEAD_DIM, (h + 1) * HEAD_DIM), tiles[t]
            part, at = places[h]
            key_in, lat_in = parts_in[part]
            put = slice(at * HEAD_DIM, (at + 1) * HEAD_DIM)
            lat = (lat_in[put, lanes] + nn(keys_t[mine, :], ds[slot])) * HEAD_DIM**-0.5
            store_blocks(plan, lat_outs, mine, lanes, lat)
            key, value = nt(query[mine, lanes], ds[slot]), nt(mix[mine, lanes], encs[slot])
            key = key + (sums[h][0] if t else key_in[put, :])
            sums[h] = (key, value + sums[h][1] if t else value)
            if t < len(tiles) - 1:
                return
            key, value = sums.pop(h)
            key = (key * HEAD_DIM**-0.5).T.astype(jnp.bfloat16)
            value = value.T.astype(jnp.bfloat16)
            for j, out in enumerate(pts_outs):
                rows = slice(j * plan.rows, (j + 1) * plan.rows)
                out[:, mine] = key[rows]
                out[:, c + h * HEAD_DIM : c + (h + 1) * HEAD_DIM] = value[rows]

        work = [(h, t) for h in range(hs) for t in range(len(tiles))]
        for n, place in enumerate(work):
            weigh(*place, n % SLOTS)
            if n >= LAG:
                gather(*work[n - LAG], (n - LAG) % SLOTS)
        for n in range(len(work) - LAG, len(work)):
            gather(*work[n], n % SLOTS)

    outs = [shaped((plan.rows, 2 * c), jnp.bfloat16)] * n_pts
    outs += [shaped((c, plan.block), jnp.float32)] * n_lat
    scratch = [
        pltpu.VMEM((c, m), jnp.bfloat16),
        pltpu.VMEM((plan.ct_rows, m), jnp.bfloat16),
        pltpu.VMEM((c, plan.points), jnp.bfloat16),
        pltpu.VMEM((plan.points, c), jnp.bfloat16),
        pltpu.VMEM((SLOTS, plan.points, 2 * plan.block), jnp.bfloat16),
        pltpu.VMEM((SLOTS, plan.points, 2 * plan.block), jnp.bfloat16),
    ]
    flops = 10 * plan.points * m * c
    args = (*lats, *pts, kept, *mixes, *(a for _, part in before for a in part))
    got = call(kernel, outs, args, scratch, flops)
    return got[:n_pts], got[n_pts:]


def reduce_latents(plan, parts):
    def kernel(*refs):
        ins, outs = refs[: len(parts)], refs[len(parts) :]
        total = scaled_sum(*ins).T
        for j, out in enumerate(outs):
            rows = total[j * plan.lat_rows : (j + 1) * plan.lat_rows]
            n, half = plan.lat_rows, plan.lat_rows // 2
            out[:n, :] = rows[:, :LANES]
            out[n:, :] = jnp.concatenate([rows[:half, LANES:], rows[half:, LANES:]], axis=1)

    outs = [shaped((3 * plan.lat_rows // 2, LANES), jnp.float32)] * GROUPS
    return call(kernel, outs, parts)


def place_points(plan, slots):
    def kernel(*refs):
        ins, (key_out, value_out) = refs[:GROUPS], refs[GROUPS:]
        z = group_index(plan)
        c = plan.cols
        pieces = by_group([r[...].astype(jnp.float32) for r in ins], z)
        for g, piece in enumerate(pieces):
            key_out[:, g * c : (g + 1) * c] = piece[:, :c].astype(jnp.bfloat16)
            value_out[:, g * c : (g + 1) * c] = piece[:, c:].astype(jnp.bfloat16)

    outs = [shaped((plan.rows, plan.width), jnp.bfloat16)] * 2
    return call(kernel, outs, slots)


def place_latents(plan, slots):
    def kernel(*refs):
        *ins, out = refs
        n, at = plan.lat_rows, plan.cols - LANES
        for g, piece in enumerate(by_group([r[...] for r in ins], group_index(plan))):
            rest = jnp.concatenate([piece[n:, :at], piece[n:, at:]], axis=0)
            out[:, g * plan.cols : (g + 1) * plan.cols] = jnp.concatenate([piece[:n], rest], axis=1)

    outs = [shaped((plan.lat_rows, plan.width), jnp.float32)]
    return call(kernel, outs, slots)[0]


def grouped(
    plan, point_keys, point_values, out_grad, decoder_norm, latent_query, latent_out, encoder_norm
):
    def over_group(slots):
        got = [slots[0]]
        for j in range(1, GROUPS):
            got.append(plan.exchange(slots[j], True, j))
        return got

    def chip_steps():
        return [k for k in range(plan.plane) if not k & plan.fast]

    def from_chips(blocks):
        got = []
        for k, block in zip(chip_steps(), blocks, strict=True):
            got.append(plan.exchange(block, False, k) if k else block)
        return got

    def sum_cores(blocks):
        near = chip_steps()
        theirs = [plan.exchange(blocks[k | plan.fast], False, plan.fast) for k in near]
        return add_and_scale(plan, [blocks[k] for k in near], theirs)

    def sum_chips(blocks):
        halves = [blocks[0], *(block.astype(jnp.float16) for block in blocks[1:])]
        return [block.astype(jnp.float32) for block in from_chips(halves)]

    def to_plane(block):
        got = dict(zip(chip_steps(), from_chips([block] * len(chip_steps())), strict=True))
        for k in chip_steps():
            got[k | plan.fast] = plan.exchange(got[k], False, plan.fast)
        return tuple(got[k] for k in range(plan.plane))

    lat_slots, pts = pack(
        plan, latent_query, latent_out, decoder_norm, point_keys, out_grad, point_values
    )
    lat_slots = over_group(lat_slots)
    pts = over_group(pts)
    norm = order_norm(plan, encoder_norm)
    block, dec_norm = turn_latents(plan, lat_slots)
    lats = to_plane(block)
    sums, kept = first_pass(plan, lats, pts, dec_norm, norm)
    cores = sum_cores(sums)
    early, late = tuple(range(plan.heads))[:1], tuple(range(plan.heads))[1:]
    before = [(early, decoder_pass(plan, lats, pts, dec_norm, early))]
    sums = sum_chips(cores)
    before.append((late, decoder_pass(plan, lats, pts, dec_norm, late)))
    mixes = to_plane(reduce_mix(plan, sums))
    pts_out, lat_out = encoder_pass(plan, lats, pts, kept, mixes, before)
    lat_out = sum_chips(sum_cores(lat_out))
    pts_out = over_group(pts_out)
    lat_rows = over_group(reduce_latents(plan, lat_out))
    keys_grad, values_grad = place_points(plan, pts_out)
    return keys_grad, values_grad, place_latents(plan, lat_rows)


def column(block, current):
    return lax.dynamic_slice_in_dim(block, current * HEAD_DIM, HEAD_DIM, 1)


def put_head(total, piece, current):
    return lax.dynamic_update_slice_in_dim(total, piece, current * HEAD_DIM, 1)


def add_head(total, piece, current):
    return put_head(total, column(total, current) + piece, current)


def across(left, right):
    return lax.dot_general(
        left, right, (((1,), (1,)), ((), ())), preferred_element_type=jnp.float32
    )


def down_rows(left, right):
    return lax.dot_general(
        left, right, (((0,), (0,)), ((), ())), preferred_element_type=jnp.float32
    )


def gathered(
    point_keys, point_values, out_grad, decoder_norm, latent_query, latent_out, encoder_norm
):
    scale_factor = HEAD_DIM ** (-0.5)
    lat_all, out_all = (
        lax.all_gather(latent_query, ("pa", "pb"), axis=0, tiled=True),
        lax.all_gather(latent_out, ("pa", "pb"), axis=0, tiled=True),
    )
    point_rows = point_keys.shape[0]
    latent_rows = lat_all.shape[0]
    width = point_keys.shape[1]

    def encoder_row(current):
        return lax.dynamic_slice_in_dim(encoder_norm, current, 1, 0)

    def pass_one(current, state):
        mix_acc, query_acc, key_acc, weighted_acc = state
        key_head = column(point_keys, current)
        grad_head = column(out_grad, current)
        lat_head = column(lat_all, current)
        scores = across(key_head, lat_head) * scale_factor
        decoder_weights = jnp.exp(scores - lax.dynamic_slice_in_dim(decoder_norm, current, 1, 0).T)
        decoder_gradient = across(grad_head, column(out_all, current))
        row_total = jnp.sum(decoder_weights * decoder_gradient, axis=1, keepdims=True)
        decoder_scores_grad = (decoder_weights * (decoder_gradient - row_total)).astype(
            jnp.bfloat16
        )
        mix_acc = put_head(
            mix_acc, down_rows(decoder_weights.astype(jnp.bfloat16), grad_head), current
        )
        query_acc = put_head(
            query_acc, down_rows(decoder_scores_grad, key_head) * scale_factor, current
        )
        key_acc = put_head(
            key_acc,
            jnp.dot(decoder_scores_grad, lat_head, preferred_element_type=jnp.float32)
            * scale_factor,
            current,
        )
        return (mix_acc, query_acc, key_acc, weighted_acc)

    weighted_blank = jnp.zeros((1, 1), jnp.float32)
    latent_blank = jnp.zeros((latent_rows, width), jnp.float32)
    begin = (
        latent_blank,
        latent_blank,
        jnp.zeros((point_rows, width), jnp.float32),
        weighted_blank,
    )
    mix_acc, query_acc, key_acc, _ = lax.fori_loop(0, HEADS, pass_one, begin)
    mix_grad = lax.psum(mix_acc, ("pa", "pb"))
    mixing_portion = mix_grad.astype(jnp.bfloat16)

    def pass_two(current, state):
        partial_rows, value_acc = state
        scores = across(column(point_keys, current), column(lat_all, current)) * scale_factor
        encoder_portion = jnp.exp(scores - encoder_row(current)).astype(jnp.bfloat16)
        mix_head = column(mixing_portion, current)
        encoder_gradient = across(column(point_values, current), mix_head)
        sums = jnp.sum(encoder_portion.astype(jnp.float32) * encoder_gradient, axis=0)[None, :]
        partial_rows = lax.dynamic_update_slice_in_dim(partial_rows, sums, current, 0)
        value_acc = put_head(
            value_acc,
            jnp.dot(encoder_portion, mix_head, preferred_element_type=jnp.float32),
            current,
        )
        return (partial_rows, value_acc)

    partial_rows, value_acc = lax.fori_loop(
        0,
        HEADS,
        pass_two,
        (jnp.zeros((HEADS, latent_rows), jnp.float32), jnp.zeros((point_rows, width), jnp.float32)),
    )
    column_total = lax.psum(partial_rows, ("pa", "pb"))

    def pass_three(current, state):
        query_acc, key_acc, value_acc = state
        key_head = column(point_keys, current)
        lat_head = column(lat_all, current)
        mix_head = column(mixing_portion, current)
        scores = across(key_head, lat_head) * scale_factor
        encoder = jnp.exp(scores - encoder_row(current))
        encoder_gradient = across(column(point_values, current), mix_head)
        encoder_scores_grad = (
            encoder * (encoder_gradient - lax.dynamic_slice_in_dim(column_total, current, 1, 0))
        ).astype(jnp.bfloat16)
        query_acc = add_head(
            query_acc, down_rows(encoder_scores_grad, key_head) * scale_factor, current
        )
        key_acc = add_head(
            key_acc,
            jnp.dot(encoder_scores_grad, lat_head, preferred_element_type=jnp.float32)
            * scale_factor,
            current,
        )
        return (query_acc, key_acc, value_acc)

    query_acc, key_acc, value_acc = lax.fori_loop(
        0, HEADS, pass_three, (query_acc, key_acc, value_acc)
    )
    latent_grad = lax.psum_scatter(query_acc, ("pa", "pb"), scatter_dimension=0, tiled=True)
    return (key_acc.astype(jnp.bfloat16), value_acc.astype(jnp.bfloat16), latent_grad)


def solution(mesh):
    in_specs = (
        P(("pa", "pb"), None),
        P(("pa", "pb"), None),
        P(("pa", "pb"), None),
        P(None, ("pa", "pb")),
        P(("pa", "pb"), None),
        P(("pa", "pb"), None),
        P(),
    )
    out_specs = (P(("pa", "pb"), None), P(("pa", "pb"), None), P(("pa", "pb"), None))
    npa, npb = mesh.shape["pa"], mesh.shape["pb"]

    def shards(*args):
        plan_of = (npa, npb, args[0].shape[0], args[4].shape[0], args[0].shape[1])
        if Plan.fits(*plan_of):
            return grouped(Plan(*plan_of), *args)
        return gathered(*args)

    return jax.shard_map(shards, mesh=mesh, in_specs=in_specs, out_specs=out_specs, check_vma=False)
```

```python
import math

import jax
import jax.numpy as jnp
from jax import lax
from jax.experimental import pallas as pl
from jax.experimental.pallas import tpu as pltpu
from jax.sharding import PartitionSpec as P


HEADS = 12
HEAD_DIM = 64
LANES = 128
AXES = ("pa", "pb")
MOST_IN_PLANE = 16
HALF_SIZE, SMALLEST = 14.0, 2.0**-100
LAG, SLOTS = 1, 3
GROUPS = 4
VMEM_BYTES = 20 * 2**20
LOG2E = math.log2(math.e)


class Plan:
    def __init__(self, npa, npb, rows, lat_rows, width):
        self.npa, self.npb = npa, npb
        self.fast = npb // GROUPS
        self.plane = npa * self.fast
        self.rows, self.lat_rows, self.width = rows, lat_rows, width
        self.heads = HEADS // GROUPS
        self.cols = self.heads * HEAD_DIM
        self.points = rows * GROUPS
        self.block = lat_rows * GROUPS
        self.latents = self.block * self.plane
        self.slot = lat_rows + 16
        self.ct_rows = self.cols + 16

    @staticmethod
    def fits(npa, npb, rows, lat_rows, width):
        def power(v):
            return v > 0 and v & (v - 1) == 0

        return (
            power(npa)
            and power(npb)
            and npb % GROUPS == 0
            and npa * npb // GROUPS <= MOST_IN_PLANE
            and lat_rows * GROUPS == LANES
            and rows == LANES
            and HEADS % GROUPS == 0
            and HEADS // GROUPS * rows == 2 * HEADS // GROUPS * HEAD_DIM
            and width == HEADS * HEAD_DIM
            and 2 * width // GROUPS == 3 * LANES
        )

    def exchange(self, value, over_group, step):
        pairs = []
        for a in range(self.npa):
            for b in range(self.npb):
                z, f = divmod(b, self.fast)
                if over_group:
                    a2, z2, f2 = a, z ^ step, f
                else:
                    a2, z2, f2 = a ^ (step // self.fast), z, f ^ (step % self.fast)
                pairs.append((a * self.npb + b, a2 * self.npb + z2 * self.fast + f2))
        return lax.ppermute(value, AXES, pairs)


def call(kernel, outs, args, scratch=(), flops=0, space=pltpu.VMEM):
    nbytes = sum(a.size * a.dtype.itemsize for a in args)
    nbytes += sum(math.prod(o.shape) * o.dtype.itemsize for o in outs)
    return pl.pallas_call(
        kernel,
        out_shape=tuple(outs),
        in_specs=[pl.BlockSpec(memory_space=space)] * len(args),
        out_specs=tuple(pl.BlockSpec(memory_space=pltpu.VMEM) for _ in outs),
        scratch_shapes=list(scratch),
        cost_estimate=pl.CostEstimate(flops=flops, bytes_accessed=nbytes, transcendentals=flops // 256),
        compiler_params=pltpu.CompilerParams(vmem_limit_bytes=VMEM_BYTES),
    )(*args)


def call_from_hbm(kernel, outs, args):
    n = len(args)

    def body(*refs):
        held, sems = refs[-n - 1 : -1], refs[-1]
        copies = [
            pltpu.make_async_copy(src, dst, sems.at[i])
            for i, (src, dst) in enumerate(zip(refs[:n], held, strict=True))
        ]
        for copy in copies:
            copy.start()
        for copy in copies:
            copy.wait()
        kernel(*held, *refs[n : -n - 1])

    scratch = [pltpu.VMEM(a.shape, a.dtype) for a in args] + [pltpu.SemaphoreType.DMA((n,))]
    args = [pltpu.with_memory_space_constraint(a, pltpu.HBM) for a in args]
    return call(body, outs, args, scratch, space=pltpu.HBM)


def shaped(shape, dtype):
    return jax.ShapeDtypeStruct(shape, dtype)


def by_group(pieces, z):
    out = list(pieces)
    bit = 1
    while bit < len(out):
        on = (z & bit) != 0
        out = [jnp.where(on, out[g ^ bit], out[g]) for g in range(len(out))]
        bit *= 2
    return out


def group_index(plan):
    return lax.axis_index("pb") // plan.fast


def split3(value):
    hi = value.astype(jnp.bfloat16).astype(jnp.float32)
    rest = value - hi
    mid = rest.astype(jnp.bfloat16).astype(jnp.float32)
    return hi, mid, rest - mid


def nn(a, b):
    return lax.dot_general(a, b, (((1,), (0,)), ((), ())), preferred_element_type=jnp.float32)


def nt(a, b):
    return lax.dot_general(a, b, (((1,), (1,)), ((), ())), preferred_element_type=jnp.float32)


def turned(block):
    return block.astype(jnp.float32).T.astype(block.dtype)


def pack(plan, query, out, norm, keys, grads, values):
    def kernel(q_ref, o_ref, n_ref, k_ref, g_ref, v_ref, *outs):
        z = group_index(plan)
        c, hs = plan.cols, plan.heads
        q, o = q_ref[...].astype(jnp.float32), o_ref[...].astype(jnp.float32)
        parts = split3(n_ref[...])
        fill = jnp.zeros((plan.slot - plan.lat_rows - 3, hs * plan.rows), jnp.float32)
        pieces = []
        for g in range(GROUPS):
            top = jnp.concatenate([q[:, g * c : (g + 1) * c], o[:, g * c : (g + 1) * c]], axis=1)
            lines = [
                jnp.concatenate([p[h : h + 1, :] for h in range(g * hs, (g + 1) * hs)], axis=1) for p in parts
            ]
            pieces.append(jnp.concatenate([top, *lines, fill], axis=0).astype(jnp.bfloat16))
        for ref, piece in zip(outs[:GROUPS], by_group(pieces, z), strict=True):
            ref[...] = piece
        outs = outs[GROUPS:]
        for first, ref in ((0, k_ref), (1, g_ref)):
            pieces = by_group([ref[:, g * c : (g + 1) * c] for g in range(GROUPS)], z)
            for out, piece in zip(outs, pieces, strict=True):
                out[: plan.rows, first * c : (first + 1) * c] = piece
        across = v_ref[...].T
        pieces = by_group([across[g * c : (g + 1) * c] for g in range(GROUPS)], z)
        for out, piece in zip(outs, pieces, strict=True):
            for h in range(hs):
                lanes = slice(h * plan.rows, (h + 1) * plan.rows)
                out[plan.rows :, lanes] = piece[h * HEAD_DIM : (h + 1) * HEAD_DIM]

    outs = [shaped((plan.slot, 2 * plan.cols), jnp.bfloat16)] * GROUPS
    outs += [shaped((plan.rows + HEAD_DIM, 2 * plan.cols), jnp.bfloat16)] * GROUPS
    got = call_from_hbm(kernel, outs, (query, out, norm, keys, grads, values))
    return got[:GROUPS], got[GROUPS:]


def order_norm(plan, norm):
    def kernel(n_ref, out_ref):
        z = group_index(plan)
        member = lax.axis_index("pa") * plan.npb + lax.axis_index("pb")
        hs, m = plan.heads, plan.latents
        rows = by_group([n_ref[g * hs : (g + 1) * hs, :] for g in range(GROUPS)], z)[0]
        fill = jnp.zeros((16 - 3 * hs, m), jnp.float32)
        stack = jnp.concatenate([*split3(rows), fill], axis=0).astype(jnp.bfloat16)
        lane = lax.broadcasted_iota(jnp.int32, (1, m), 1)
        inner, j, k = lane % plan.lat_rows, (lane // plan.lat_rows) % GROUPS, lane // plan.block
        owner = (k // plan.fast) * plan.npb + j * plan.fast + k % plan.fast
        source = (owner ^ member) * plan.lat_rows + inner
        total = jnp.zeros((16, m), jnp.float32)
        step = 256
        for start in range(0, m, step):
            row = lax.broadcasted_iota(jnp.int32, (step, m), 0) + start
            chosen = jnp.where(row == source, 1.0, 0.0).astype(jnp.bfloat16)
            total = total + nn(stack[:, start : start + step], chosen)
        out_ref[0:hs, :] = (total[:hs] + total[hs : 2 * hs]) + total[2 * hs : 3 * hs]

    outs = [shaped((plan.heads, plan.latents), jnp.float32)]
    return call_from_hbm(kernel, outs, (norm,))[0]


def turn_latents(plan, slots):
    def kernel(*refs):
        *slots, out, norm_out = refs
        n, rows = plan.lat_rows, plan.rows
        slots = [s[...] for s in slots]
        out[...] = turned(jnp.concatenate([s[:n] for s in slots], axis=0))
        for j, slot in enumerate(slots):
            parts = slot[n : n + 3].astype(jnp.float32)
            line = (parts[0:1] + parts[1:2]) + parts[2:3]
            lines = [line[:, h * rows : (h + 1) * rows] for h in range(plan.heads)]
            fill = jnp.zeros((LANES - plan.heads, rows), jnp.float32)
            norm_out[j * rows : (j + 1) * rows, :] = jnp.concatenate([*lines, fill], axis=0).T

    outs = [
        shaped((2 * plan.cols, plan.block), jnp.bfloat16),
        shaped((plan.points, LANES), jnp.float32),
    ]
    return call(kernel, outs, slots)


def lane_tiles(plan):
    width = min(2 * plan.block, plan.latents)
    return [slice(at, at + width) for at in range(0, plan.latents, width)]


def store_blocks(plan, outs, rows, lanes, value):
    for at in range(lanes.start, lanes.stop, plan.block):
        outs[at // plan.block][rows, :] = value[:, at - lanes.start : at - lanes.start + plan.block]


def load_blocks(plan, refs, rows, lanes):
    blocks = range(lanes.start // plan.block, lanes.stop // plan.block)
    return jnp.concatenate([refs[k][rows, :] for k in blocks], axis=1)


def first_pass(plan, lats, pts, at, dec_norm, enc_norm, before=()):
    n_lat, n_pts = len(lats), len(pts)
    c, m = plan.cols, plan.latents
    points = n_pts * plan.rows

    def kernel(*refs):
        lat_refs, pts_refs, rest = refs[:n_lat], refs[n_lat : n_lat + n_pts], refs[n_lat + n_pts :]
        (dec_ref, enc_ref), earlier = rest[:2], rest[2 : 2 + len(before)]
        outs, kept = refs[-4 - n_lat : -4], refs[-4]
        query, sides, keys = refs[-3:]
        for k, ref in enumerate(lat_refs):
            query[:, k * plan.block : (k + 1) * plan.block] = ref[:c, :]
        for j, ref in enumerate(pts_refs):
            rows = slice(j * plan.rows, (j + 1) * plan.rows)
            keys[rows, :] = ref[: plan.rows, :c]
            sides[:c, rows] = turned(ref[: plan.rows, c:])
            for h in range(plan.heads):
                below = slice(c + h * HEAD_DIM, c + (h + 1) * HEAD_DIM)
                sides[below, rows] = ref[plan.rows :, h * plan.rows : (h + 1) * plan.rows]
        for h in range(plan.heads):
            mine = slice(h * HEAD_DIM, (h + 1) * HEAD_DIM)
            below = slice(c + h * HEAD_DIM, c + (h + 1) * HEAD_DIM)
            key = keys[:, mine]
            row_norm = dec_ref[at * plan.rows : at * plan.rows + points, h : h + 1] * LOG2E
            for lanes in lane_tiles(plan):
                scores = nn(key, query[mine, lanes]) * (HEAD_DIM**-0.5 * LOG2E)
                dec = jnp.exp2(scores - row_norm).astype(jnp.bfloat16)
                enc = jnp.exp2(scores - enc_ref[h : h + 1, lanes] * LOG2E)
                kept[h, :, lanes] = enc
                for rows, half in ((mine, dec), (below, enc.astype(jnp.bfloat16))):
                    total = nn(sides[rows, :], half)
                    if earlier:
                        total = total + load_blocks(plan, earlier, rows, lanes)
                    store_blocks(plan, outs, rows, lanes, total)

    outs = [shaped((2 * c, plan.block), jnp.float32)] * plan.plane
    outs += [shaped((plan.heads, points, m), jnp.float32)]
    scratch = [
        pltpu.VMEM((c, m), jnp.bfloat16),
        pltpu.VMEM((2 * c, points), jnp.bfloat16),
        pltpu.VMEM((points, c), jnp.bfloat16),
    ]
    flops = 6 * points * m * c
    args = (*lats, *pts, dec_norm, enc_norm, *before)
    *sums, kept = call(kernel, outs, args, scratch, flops)
    return sums, kept


def decoder_pass(plan, lats, pts, dec_norm, heads):
    n_lat = len(lats)
    c, m = plan.cols, plan.latents

    def kernel(*refs):
        lat_refs, pts_refs, dec_ref = refs[:n_lat], refs[n_lat:-6], refs[-6]
        key_ref, lat_ref = refs[-5:-3]
        both, keys_t, ds = refs[-3:]
        for k, ref in enumerate(lat_refs):
            both[:, k * plan.block : (k + 1) * plan.block] = ref[...]
        for j, ref in enumerate(pts_refs):
            keys_t[:, j * plan.rows : (j + 1) * plan.rows] = turned(ref[: plan.rows, :c])
        for at, h in enumerate(heads):
            mine = slice(h * HEAD_DIM, (h + 1) * HEAD_DIM)
            put = slice(at * HEAD_DIM, (at + 1) * HEAD_DIM)
            other = slice(c + h * HEAD_DIM, c + (h + 1) * HEAD_DIM)
            for j, ref in enumerate(pts_refs):
                rows = slice(j * plan.rows, (j + 1) * plan.rows)
                scores = nn(ref[: plan.rows, mine], both[mine, :]) * (HEAD_DIM**-0.5 * LOG2E)
                dec = jnp.exp2(scores - dec_ref[rows, h : h + 1] * LOG2E)
                grad = nn(ref[: plan.rows, other], both[other, :])
                total = jnp.sum(dec * grad, axis=1, keepdims=True)
                tile = (dec * (grad - total)).astype(jnp.bfloat16)
                ds[rows, :] = tile
            key_ref[put, :] = nt(both[mine, :], ds[...])
            lat_ref[put, :] = nn(keys_t[mine, :], ds[...])

    width = len(heads) * HEAD_DIM
    outs = [shaped((width, plan.points), jnp.float32), shaped((width, m), jnp.float32)]
    scratch = [
        pltpu.VMEM((2 * c, m), jnp.bfloat16),
        pltpu.VMEM((c, plan.points), jnp.bfloat16),
        pltpu.VMEM((plan.points, m), jnp.bfloat16),
    ]
    flops = 8 * plan.points * m * width
    return call(kernel, outs, (*lats, *pts, dec_norm), scratch, flops)


def add_and_scale(plan, mine, theirs):
    tall = mine[0].shape[0]

    def kernel(*refs):
        n = len(mine)
        for k, (a, b, out) in enumerate(zip(refs[:n], refs[n : 2 * n], refs[2 * n :], strict=True)):
            total = a[...] + b[...]
            if k == 0:
                out[...] = total
                continue
            sizes = []
            for at in range(0, tall, HEAD_DIM):
                part = total[at : at + HEAD_DIM]
                most = jnp.max(jnp.abs(part), axis=0, keepdims=True)
                size = jnp.ceil(jnp.log2(jnp.maximum(most, SMALLEST)))
                out[at : at + HEAD_DIM, :] = part * jnp.exp2(HALF_SIZE - size)
                sizes.append(size)
            fill = jnp.zeros((16 - len(sizes), plan.block), jnp.float32)
            out[tall:, :] = jnp.concatenate([*sizes, fill], axis=0)

    outs = [shaped((tall + 16 * (k > 0), plan.block), jnp.float32) for k in range(len(mine))]
    return call(kernel, outs, (*mine, *theirs))


def scaled_sum(own, *scaled):
    tall = own.shape[0]
    pieces = []
    for n, at in enumerate(range(0, tall, HEAD_DIM)):
        piece = own[at : at + HEAD_DIM, :]
        for ref in scaled:
            size = ref[tall + n : tall + n + 1, :]
            piece = piece + ref[at : at + HEAD_DIM, :] * jnp.exp2(size - HALF_SIZE)
        pieces.append(piece)
    return jnp.concatenate(pieces, axis=0)


def reduce_mix(plan, parts):
    c, hs = plan.cols, plan.heads

    def kernel(*refs):
        *ins, out = refs
        total = scaled_sum(*ins)
        half = total[:c].astype(jnp.bfloat16)
        out[:c, :] = half
        product = half.astype(jnp.float32) * total[c:]
        sums = [
            jnp.sum(product[h * HEAD_DIM : (h + 1) * HEAD_DIM], axis=0, keepdims=True) for h in range(hs)
        ]
        fill = jnp.zeros((16 - 3 * hs, plan.block), jnp.float32)
        stack = jnp.concatenate([*split3(jnp.concatenate(sums, axis=0)), fill], axis=0)
        out[c:, :] = stack.astype(jnp.bfloat16)

    outs = [shaped((plan.ct_rows, plan.block), jnp.bfloat16)]
    return call(kernel, outs, parts)[0]


def encoder_pass(plan, lats, pts, kept, mixes, before):
    places = [(part, at) for part, (heads, _) in enumerate(before) for at in range(len(heads))]
    n_lat, n_pts, n_mix = len(lats), len(pts), len(mixes)
    c, m, hs = plan.cols, plan.latents, plan.heads

    def kernel(*refs):
        refs = list(refs)

        def take(n):
            got = refs[:n]
            del refs[:n]
            return got

        lat_refs, pts_refs = take(n_lat), take(n_pts)
        kept_refs = take(len(kept))
        mix_refs = take(n_mix)
        parts_in = [take(2) for _ in before]
        pts_outs, lat_outs = take(n_pts), take(n_lat)
        query, mix, keys_t, values, ds, encs = refs
        for k, ref in enumerate(lat_refs):
            query[:, k * plan.block : (k + 1) * plan.block] = ref[:c, :]
        for k, ref in enumerate(mix_refs):
            mix[:, k * plan.block : (k + 1) * plan.block] = ref[...]
        for j, ref in enumerate(pts_refs):
            rows = slice(j * plan.rows, (j + 1) * plan.rows)
            keys_t[:, rows] = turned(ref[: plan.rows, :c])
            across = [ref[plan.rows :, h * plan.rows : (h + 1) * plan.rows] for h in range(hs)]
            values[rows, :] = turned(jnp.concatenate(across, axis=0))
        tail = mix[c:, :].astype(jnp.float32)
        columns = (tail[:hs] + tail[hs : 2 * hs]) + tail[2 * hs : 3 * hs]
        tiles = lane_tiles(plan)
        sums = {}

        def weigh(h, t, slot):
            mine, lanes = slice(h * HEAD_DIM, (h + 1) * HEAD_DIM), tiles[t]
            enc = jnp.concatenate([ref[h, :, lanes] for ref in kept_refs], axis=0)
            grad = nn(values[:, mine], mix[mine, lanes])
            encs[slot] = enc.astype(jnp.bfloat16)
            ds[slot] = (enc * (grad - columns[h : h + 1, lanes])).astype(jnp.bfloat16)

        def gather(h, t, slot):
            mine, lanes = slice(h * HEAD_DIM, (h + 1) * HEAD_DIM), tiles[t]
            part, at = places[h]
            key_in, lat_in = parts_in[part]
            put = slice(at * HEAD_DIM, (at + 1) * HEAD_DIM)
            lat = (lat_in[put, lanes] + nn(keys_t[mine, :], ds[slot])) * HEAD_DIM**-0.5
            store_blocks(plan, lat_outs, mine, lanes, lat)
            key, value = nt(query[mine, lanes], ds[slot]), nt(mix[mine, lanes], encs[slot])
            key = key + (sums[h][0] if t else key_in[put, :])
            sums[h] = (key, value + sums[h][1] if t else value)
            if t < len(tiles) - 1:
                return
            key, value = sums.pop(h)
            key = (key * HEAD_DIM**-0.5).T.astype(jnp.bfloat16)
            value = value.T.astype(jnp.bfloat16)
            for j, out in enumerate(pts_outs):
                rows = slice(j * plan.rows, (j + 1) * plan.rows)
                out[:, mine] = key[rows]
                out[:, c + h * HEAD_DIM : c + (h + 1) * HEAD_DIM] = value[rows]

        work = [(h, t) for h in range(hs) for t in range(len(tiles))]
        for n, place in enumerate(work):
            weigh(*place, n % SLOTS)
            if n >= LAG:
                gather(*work[n - LAG], (n - LAG) % SLOTS)
        for n in range(len(work) - LAG, len(work)):
            gather(*work[n], n % SLOTS)

    outs = [shaped((plan.rows, 2 * c), jnp.bfloat16)] * n_pts
    outs += [shaped((c, plan.block), jnp.float32)] * n_lat
    scratch = [
        pltpu.VMEM((c, m), jnp.bfloat16),
        pltpu.VMEM((plan.ct_rows, m), jnp.bfloat16),
        pltpu.VMEM((c, plan.points), jnp.bfloat16),
        pltpu.VMEM((plan.points, c), jnp.bfloat16),
        pltpu.VMEM((SLOTS, plan.points, 2 * plan.block), jnp.bfloat16),
        pltpu.VMEM((SLOTS, plan.points, 2 * plan.block), jnp.bfloat16),
    ]
    flops = 10 * plan.points * m * c
    args = (*lats, *pts, *kept, *mixes, *(a for _, part in before for a in part))
    got = call(kernel, outs, args, scratch, flops)
    return got[:n_pts], got[n_pts:]


def reduce_latents(plan, parts):
    def kernel(*refs):
        ins, outs = refs[: len(parts)], refs[len(parts) :]
        total = scaled_sum(*ins).T
        for j, out in enumerate(outs):
            rows = total[j * plan.lat_rows : (j + 1) * plan.lat_rows]
            n, half = plan.lat_rows, plan.lat_rows // 2
            out[:n, :] = rows[:, :LANES]
            out[n:, :] = jnp.concatenate([rows[:half, LANES:], rows[half:, LANES:]], axis=1)

    outs = [shaped((3 * plan.lat_rows // 2, LANES), jnp.float32)] * GROUPS
    return call(kernel, outs, parts)


def place_points(plan, slots):
    def kernel(*refs):
        ins, (key_out, value_out) = refs[:GROUPS], refs[GROUPS:]
        z = group_index(plan)
        c = plan.cols
        pieces = by_group([r[...].astype(jnp.float32) for r in ins], z)
        for g, piece in enumerate(pieces):
            key_out[:, g * c : (g + 1) * c] = piece[:, :c].astype(jnp.bfloat16)
            value_out[:, g * c : (g + 1) * c] = piece[:, c:].astype(jnp.bfloat16)

    outs = [shaped((plan.rows, plan.width), jnp.bfloat16)] * 2
    return call(kernel, outs, slots)


def place_latents(plan, slots):
    def kernel(*refs):
        *ins, out = refs
        n, at = plan.lat_rows, plan.cols - LANES
        for g, piece in enumerate(by_group([r[...] for r in ins], group_index(plan))):
            rest = jnp.concatenate([piece[n:, :at], piece[n:, at:]], axis=0)
            out[:, g * plan.cols : (g + 1) * plan.cols] = jnp.concatenate([piece[:n], rest], axis=1)

    outs = [shaped((plan.lat_rows, plan.width), jnp.float32)]
    return call(kernel, outs, slots)[0]


def grouped(
    plan, point_keys, point_values, out_grad, decoder_norm, latent_query, latent_out, encoder_norm
):
    def over_group(slots):
        got = [slots[0]]
        for j in range(1, GROUPS):
            got.append(plan.exchange(slots[j], True, j))
        return got

    def chip_steps():
        return [k for k in range(plan.plane) if not k & plan.fast]

    def from_chips(blocks):
        got = []
        for k, block in zip(chip_steps(), blocks, strict=True):
            got.append(plan.exchange(block, False, k) if k else block)
        return got

    def sum_cores(blocks):
        near = chip_steps()
        theirs = [plan.exchange(blocks[k | plan.fast], False, plan.fast) for k in near]
        return add_and_scale(plan, [blocks[k] for k in near], theirs)

    def sum_chips(blocks):
        halves = [blocks[0], *(block.astype(jnp.float16) for block in blocks[1:])]
        return [block.astype(jnp.float32) for block in from_chips(halves)]

    def to_plane(block):
        got = dict(zip(chip_steps(), from_chips([block] * len(chip_steps())), strict=True))
        for k in chip_steps():
            got[k | plan.fast] = plan.exchange(got[k], False, plan.fast)
        return tuple(got[k] for k in range(plan.plane))

    lat_slots, pts = pack(
        plan, latent_query, latent_out, decoder_norm, point_keys, out_grad, point_values
    )
    lat_slots = over_group(lat_slots)
    pts = over_group(pts)
    norm = order_norm(plan, encoder_norm)
    block, dec_norm = turn_latents(plan, lat_slots)
    lats = to_plane(block)
    half = GROUPS // 2
    sums, kept = first_pass(plan, lats, pts[:half], 0, dec_norm, norm)
    sums, more = first_pass(plan, lats, pts[half:], half, dec_norm, norm, sums)
    kept = (kept, more)
    cores = sum_cores(sums)
    early, late = tuple(range(plan.heads))[:1], tuple(range(plan.heads))[1:]
    before = [(early, decoder_pass(plan, lats, pts, dec_norm, early))]
    sums = sum_chips(cores)
    before.append((late, decoder_pass(plan, lats, pts, dec_norm, late)))
    mixes = to_plane(reduce_mix(plan, sums))
    pts_out, lat_out = encoder_pass(plan, lats, pts, kept, mixes, before)
    lat_out = sum_chips(sum_cores(lat_out))
    pts_out = over_group(pts_out)
    lat_rows = over_group(reduce_latents(plan, lat_out))
    keys_grad, values_grad = place_points(plan, pts_out)
    return keys_grad, values_grad, place_latents(plan, lat_rows)


def column(block, current):
    return lax.dynamic_slice_in_dim(block, current * HEAD_DIM, HEAD_DIM, 1)


def put_head(total, piece, current):
    return lax.dynamic_update_slice_in_dim(total, piece, current * HEAD_DIM, 1)


def add_head(total, piece, current):
    return put_head(total, column(total, current) + piece, current)


def across(left, right):
    return lax.dot_general(
        left, right, (((1,), (1,)), ((), ())), preferred_element_type=jnp.float32
    )


def down_rows(left, right):
    return lax.dot_general(
        left, right, (((0,), (0,)), ((), ())), preferred_element_type=jnp.float32
    )


def gathered(
    point_keys, point_values, out_grad, decoder_norm, latent_query, latent_out, encoder_norm
):
    scale_factor = HEAD_DIM ** (-0.5)
    lat_all, out_all = (
        lax.all_gather(latent_query, ("pa", "pb"), axis=0, tiled=True),
        lax.all_gather(latent_out, ("pa", "pb"), axis=0, tiled=True),
    )
    point_rows = point_keys.shape[0]
    latent_rows = lat_all.shape[0]
    width = point_keys.shape[1]

    def encoder_row(current):
        return lax.dynamic_slice_in_dim(encoder_norm, current, 1, 0)

    def pass_one(current, state):
        mix_acc, query_acc, key_acc, weighted_acc = state
        key_head = column(point_keys, current)
        grad_head = column(out_grad, current)
        lat_head = column(lat_all, current)
        scores = across(key_head, lat_head) * scale_factor
        decoder_weights = jnp.exp(scores - lax.dynamic_slice_in_dim(decoder_norm, current, 1, 0).T)
        decoder_gradient = across(grad_head, column(out_all, current))
        row_total = jnp.sum(decoder_weights * decoder_gradient, axis=1, keepdims=True)
        decoder_scores_grad = (decoder_weights * (decoder_gradient - row_total)).astype(
            jnp.bfloat16
        )
        mix_acc = put_head(
            mix_acc, down_rows(decoder_weights.astype(jnp.bfloat16), grad_head), current
        )
        query_acc = put_head(
            query_acc, down_rows(decoder_scores_grad, key_head) * scale_factor, current
        )
        key_acc = put_head(
            key_acc,
            jnp.dot(decoder_scores_grad, lat_head, preferred_element_type=jnp.float32)
            * scale_factor,
            current,
        )
        return (mix_acc, query_acc, key_acc, weighted_acc)

    weighted_blank = jnp.zeros((1, 1), jnp.float32)
    latent_blank = jnp.zeros((latent_rows, width), jnp.float32)
    begin = (
        latent_blank,
        latent_blank,
        jnp.zeros((point_rows, width), jnp.float32),
        weighted_blank,
    )
    mix_acc, query_acc, key_acc, _ = lax.fori_loop(0, HEADS, pass_one, begin)
    mix_grad = lax.psum(mix_acc, ("pa", "pb"))
    mixing_portion = mix_grad.astype(jnp.bfloat16)

    def pass_two(current, state):
        partial_rows, value_acc = state
        scores = across(column(point_keys, current), column(lat_all, current)) * scale_factor
        encoder_portion = jnp.exp(scores - encoder_row(current)).astype(jnp.bfloat16)
        mix_head = column(mixing_portion, current)
        encoder_gradient = across(column(point_values, current), mix_head)
        sums = jnp.sum(encoder_portion.astype(jnp.float32) * encoder_gradient, axis=0)[None, :]
        partial_rows = lax.dynamic_update_slice_in_dim(partial_rows, sums, current, 0)
        value_acc = put_head(
            value_acc,
            jnp.dot(encoder_portion, mix_head, preferred_element_type=jnp.float32),
            current,
        )
        return (partial_rows, value_acc)

    partial_rows, value_acc = lax.fori_loop(
        0,
        HEADS,
        pass_two,
        (jnp.zeros((HEADS, latent_rows), jnp.float32), jnp.zeros((point_rows, width), jnp.float32)),
    )
    column_total = lax.psum(partial_rows, ("pa", "pb"))

    def pass_three(current, state):
        query_acc, key_acc, value_acc = state
        key_head = column(point_keys, current)
        lat_head = column(lat_all, current)
        mix_head = column(mixing_portion, current)
        scores = across(key_head, lat_head) * scale_factor
        encoder = jnp.exp(scores - encoder_row(current))
        encoder_gradient = across(column(point_values, current), mix_head)
        encoder_scores_grad = (
            encoder * (encoder_gradient - lax.dynamic_slice_in_dim(column_total, current, 1, 0))
        ).astype(jnp.bfloat16)
        query_acc = add_head(
            query_acc, down_rows(encoder_scores_grad, key_head) * scale_factor, current
        )
        key_acc = add_head(
            key_acc,
            jnp.dot(encoder_scores_grad, lat_head, preferred_element_type=jnp.float32)
            * scale_factor,
            current,
        )
        return (query_acc, key_acc, value_acc)

    query_acc, key_acc, value_acc = lax.fori_loop(
        0, HEADS, pass_three, (query_acc, key_acc, value_acc)
    )
    latent_grad = lax.psum_scatter(query_acc, ("pa", "pb"), scatter_dimension=0, tiled=True)
    return (key_acc.astype(jnp.bfloat16), value_acc.astype(jnp.bfloat16), latent_grad)


def solution(mesh):
    in_specs = (
        P(("pa", "pb"), None),
        P(("pa", "pb"), None),
        P(("pa", "pb"), None),
        P(None, ("pa", "pb")),
        P(("pa", "pb"), None),
        P(("pa", "pb"), None),
        P(),
    )
    out_specs = (P(("pa", "pb"), None), P(("pa", "pb"), None), P(("pa", "pb"), None))
    npa, npb = mesh.shape["pa"], mesh.shape["pb"]

    def shards(*args):
        plan_of = (npa, npb, args[0].shape[0], args[4].shape[0], args[0].shape[1])
        if Plan.fits(*plan_of):
            return grouped(Plan(*plan_of), *args)
        return gathered(*args)

    return jax.shard_map(shards, mesh=mesh, in_specs=in_specs, out_specs=out_specs, check_vma=False)
```

```python
import math

import jax
import jax.numpy as jnp
from jax import lax
from jax.experimental import pallas as pl
from jax.experimental.pallas import tpu as pltpu
from jax.sharding import PartitionSpec as P


HEADS = 12
HEAD_DIM = 64
LANES = 128
AXES = ("pa", "pb")
MOST_IN_PLANE = 16
HALF_SIZE, SMALLEST = 14.0, 2.0**-100
LAG, SLOTS = 1, 3
GROUPS = 4
VMEM_BYTES = 20 * 2**20
LOG2E = math.log2(math.e)


class Plan:
    def __init__(self, npa, npb, rows, lat_rows, width):
        self.npa, self.npb = npa, npb
        self.fast = npb // GROUPS
        self.plane = npa * self.fast
        self.rows, self.lat_rows, self.width = rows, lat_rows, width
        self.heads = HEADS // GROUPS
        self.cols = self.heads * HEAD_DIM
        self.points = rows * GROUPS
        self.block = lat_rows * GROUPS
        self.latents = self.block * self.plane
        self.slot = lat_rows + 16
        self.ct_rows = self.cols + 16

    @staticmethod
    def fits(npa, npb, rows, lat_rows, width):
        def power(v):
            return v > 0 and v & (v - 1) == 0

        return (
            power(npa)
            and power(npb)
            and npb % GROUPS == 0
            and npa * npb // GROUPS <= MOST_IN_PLANE
            and lat_rows * GROUPS == LANES
            and rows == LANES
            and HEADS % GROUPS == 0
            and HEADS // GROUPS * rows == 2 * HEADS // GROUPS * HEAD_DIM
            and width == HEADS * HEAD_DIM
            and 2 * width // GROUPS == 3 * LANES
        )

    def chip_steps(self):
        return [k for k in range(self.plane) if not k & self.fast]

    def views(self, mine, away, tall):
        at = {k: slice(i * tall, (i + 1) * tall) for i, k in enumerate(self.chip_steps())}
        return [(away if k & self.fast else mine).at[at[k & ~self.fast]] for k in range(self.plane)]

    def stack(self, tall):
        return shaped((len(self.chip_steps()) * tall, self.block), jnp.float32)

    def exchange(self, value, over_group, step):
        pairs = []
        for a in range(self.npa):
            for b in range(self.npb):
                z, f = divmod(b, self.fast)
                if over_group:
                    a2, z2, f2 = a, z ^ step, f
                else:
                    a2, z2, f2 = a ^ (step // self.fast), z, f ^ (step % self.fast)
                pairs.append((a * self.npb + b, a2 * self.npb + z2 * self.fast + f2))
        return lax.ppermute(value, AXES, pairs)


def call(kernel, outs, args, scratch=(), flops=0, space=pltpu.VMEM):
    nbytes = sum(a.size * a.dtype.itemsize for a in args)
    nbytes += sum(math.prod(o.shape) * o.dtype.itemsize for o in outs)
    return pl.pallas_call(
        kernel,
        out_shape=tuple(outs),
        in_specs=[pl.BlockSpec(memory_space=space)] * len(args),
        out_specs=tuple(pl.BlockSpec(memory_space=pltpu.VMEM) for _ in outs),
        scratch_shapes=list(scratch),
        cost_estimate=pl.CostEstimate(flops=flops, bytes_accessed=nbytes, transcendentals=flops // 256),
        compiler_params=pltpu.CompilerParams(vmem_limit_bytes=VMEM_BYTES),
    )(*args)


def call_from_hbm(kernel, outs, args):
    n = len(args)

    def body(*refs):
        held, sems = refs[-n - 1 : -1], refs[-1]
        copies = [
            pltpu.make_async_copy(src, dst, sems.at[i])
            for i, (src, dst) in enumerate(zip(refs[:n], held, strict=True))
        ]
        for copy in copies:
            copy.start()
        for copy in copies:
            copy.wait()
        kernel(*held, *refs[n : -n - 1])

    scratch = [pltpu.VMEM(a.shape, a.dtype) for a in args] + [pltpu.SemaphoreType.DMA((n,))]
    args = [pltpu.with_memory_space_constraint(a, pltpu.HBM) for a in args]
    return call(body, outs, args, scratch, space=pltpu.HBM)


def shaped(shape, dtype):
    return jax.ShapeDtypeStruct(shape, dtype)


def by_group(pieces, z):
    out = list(pieces)
    bit = 1
    while bit < len(out):
        on = (z & bit) != 0
        out = [jnp.where(on, out[g ^ bit], out[g]) for g in range(len(out))]
        bit *= 2
    return out


def group_index(plan):
    return lax.axis_index("pb") // plan.fast


def split3(value):
    hi = value.astype(jnp.bfloat16).astype(jnp.float32)
    rest = value - hi
    mid = rest.astype(jnp.bfloat16).astype(jnp.float32)
    return hi, mid, rest - mid


def nn(a, b):
    return lax.dot_general(a, b, (((1,), (0,)), ((), ())), preferred_element_type=jnp.float32)


def nt(a, b):
    return lax.dot_general(a, b, (((1,), (1,)), ((), ())), preferred_element_type=jnp.float32)


def turned(block):
    return block.astype(jnp.float32).T.astype(block.dtype)


def pack(plan, query, out, norm, keys, grads, values):
    def kernel(q_ref, o_ref, n_ref, k_ref, g_ref, v_ref, *outs):
        z = group_index(plan)
        c, hs = plan.cols, plan.heads
        q, o = q_ref[...].astype(jnp.float32), o_ref[...].astype(jnp.float32)
        parts = split3(n_ref[...])
        fill = jnp.zeros((plan.slot - plan.lat_rows - 3, hs * plan.rows), jnp.float32)
        pieces = []
        for g in range(GROUPS):
            top = jnp.concatenate([q[:, g * c : (g + 1) * c], o[:, g * c : (g + 1) * c]], axis=1)
            lines = [
                jnp.concatenate([p[h : h + 1, :] for h in range(g * hs, (g + 1) * hs)], axis=1) for p in parts
            ]
            pieces.append(jnp.concatenate([top, *lines, fill], axis=0).astype(jnp.bfloat16))
        for ref, piece in zip(outs[:GROUPS], by_group(pieces, z), strict=True):
            ref[...] = piece
        outs = outs[GROUPS:]
        for first, ref in ((0, k_ref), (1, g_ref)):
            pieces = by_group([ref[:, g * c : (g + 1) * c] for g in range(GROUPS)], z)
            for out, piece in zip(outs, pieces, strict=True):
                out[: plan.rows, first * c : (first + 1) * c] = piece
        across = v_ref[...].T
        pieces = by_group([across[g * c : (g + 1) * c] for g in range(GROUPS)], z)
        for out, piece in zip(outs, pieces, strict=True):
            for h in range(hs):
                lanes = slice(h * plan.rows, (h + 1) * plan.rows)
                out[plan.rows :, lanes] = piece[h * HEAD_DIM : (h + 1) * HEAD_DIM]

    outs = [shaped((plan.slot, 2 * plan.cols), jnp.bfloat16)] * GROUPS
    outs += [shaped((plan.rows + HEAD_DIM, 2 * plan.cols), jnp.bfloat16)] * GROUPS
    got = call_from_hbm(kernel, outs, (query, out, norm, keys, grads, values))
    return got[:GROUPS], got[GROUPS:]


def order_norm(plan, norm):
    def kernel(n_ref, out_ref):
        z = group_index(plan)
        member = lax.axis_index("pa") * plan.npb + lax.axis_index("pb")
        hs, m = plan.heads, plan.latents
        rows = by_group([n_ref[g * hs : (g + 1) * hs, :] for g in range(GROUPS)], z)[0]
        fill = jnp.zeros((16 - 3 * hs, m), jnp.float32)
        stack = jnp.concatenate([*split3(rows), fill], axis=0).astype(jnp.bfloat16)
        lane = lax.broadcasted_iota(jnp.int32, (1, m), 1)
        inner, j, k = lane % plan.lat_rows, (lane // plan.lat_rows) % GROUPS, lane // plan.block
        owner = (k // plan.fast) * plan.npb + j * plan.fast + k % plan.fast
        source = (owner ^ member) * plan.lat_rows + inner
        total = jnp.zeros((16, m), jnp.float32)
        step = 256
        for start in range(0, m, step):
            row = lax.broadcasted_iota(jnp.int32, (step, m), 0) + start
            chosen = jnp.where(row == source, 1.0, 0.0).astype(jnp.bfloat16)
            total = total + nn(stack[:, start : start + step], chosen)
        out_ref[0:hs, :] = (total[:hs] + total[hs : 2 * hs]) + total[2 * hs : 3 * hs]

    outs = [shaped((plan.heads, plan.latents), jnp.float32)]
    return call_from_hbm(kernel, outs, (norm,))[0]


def turn_latents(plan, slots):
    def kernel(*refs):
        *slots, out, norm_out = refs
        n, rows = plan.lat_rows, plan.rows
        slots = [s[...] for s in slots]
        out[...] = turned(jnp.concatenate([s[:n] for s in slots], axis=0))
        for j, slot in enumerate(slots):
            parts = slot[n : n + 3].astype(jnp.float32)
            line = (parts[0:1] + parts[1:2]) + parts[2:3]
            lines = [line[:, h * rows : (h + 1) * rows] for h in range(plan.heads)]
            fill = jnp.zeros((LANES - plan.heads, rows), jnp.float32)
            norm_out[j * rows : (j + 1) * rows, :] = jnp.concatenate([*lines, fill], axis=0).T

    outs = [
        shaped((2 * plan.cols, plan.block), jnp.bfloat16),
        shaped((plan.points, LANES), jnp.float32),
    ]
    return call(kernel, outs, slots)


def lane_tiles(plan):
    width = min(2 * plan.block, plan.latents)
    return [slice(at, at + width) for at in range(0, plan.latents, width)]


def store_blocks(plan, outs, rows, lanes, value):
    for at in range(lanes.start, lanes.stop, plan.block):
        outs[at // plan.block][rows, :] = value[:, at - lanes.start : at - lanes.start + plan.block]


def load_blocks(plan, refs, rows, lanes):
    blocks = range(lanes.start // plan.block, lanes.stop // plan.block)
    return jnp.concatenate([refs[k][rows, :] for k in blocks], axis=1)


def first_pass(plan, lats, pts, at, dec_norm, enc_norm, before=()):
    n_lat, n_pts = len(lats), len(pts)
    c, m = plan.cols, plan.latents
    points = n_pts * plan.rows

    def kernel(*refs):
        lat_refs, pts_refs, rest = refs[:n_lat], refs[n_lat : n_lat + n_pts], refs[n_lat + n_pts :]
        dec_ref, enc_ref = rest[:2]
        earlier = plan.views(*rest[2:4], 2 * c) if before else ()
        outs, kept = plan.views(*refs[-6:-4], 2 * c), refs[-4]
        query, sides, keys = refs[-3:]
        for k, ref in enumerate(lat_refs):
            query[:, k * plan.block : (k + 1) * plan.block] = ref[:c, :]
        for j, ref in enumerate(pts_refs):
            rows = slice(j * plan.rows, (j + 1) * plan.rows)
            keys[rows, :] = ref[: plan.rows, :c]
            sides[:c, rows] = turned(ref[: plan.rows, c:])
            for h in range(plan.heads):
                below = slice(c + h * HEAD_DIM, c + (h + 1) * HEAD_DIM)
                sides[below, rows] = ref[plan.rows :, h * plan.rows : (h + 1) * plan.rows]
        for h in range(plan.heads):
            mine = slice(h * HEAD_DIM, (h + 1) * HEAD_DIM)
            below = slice(c + h * HEAD_DIM, c + (h + 1) * HEAD_DIM)
            key = keys[:, mine]
            row_norm = dec_ref[at * plan.rows : at * plan.rows + points, h : h + 1] * LOG2E
            for lanes in lane_tiles(plan):
                scores = nn(key, query[mine, lanes]) * (HEAD_DIM**-0.5 * LOG2E)
                dec = jnp.exp2(scores - row_norm).astype(jnp.bfloat16)
                enc = jnp.exp2(scores - enc_ref[h : h + 1, lanes] * LOG2E)
                kept[h, :, lanes] = enc
                for rows, half in ((mine, dec), (below, enc.astype(jnp.bfloat16))):
                    total = nn(sides[rows, :], half)
                    if earlier:
                        total = total + load_blocks(plan, earlier, rows, lanes)
                    store_blocks(plan, outs, rows, lanes, total)

    outs = [plan.stack(2 * c)] * 2 + [shaped((plan.heads, points, m), jnp.float32)]
    scratch = [
        pltpu.VMEM((c, m), jnp.bfloat16),
        pltpu.VMEM((2 * c, points), jnp.bfloat16),
        pltpu.VMEM((points, c), jnp.bfloat16),
    ]
    flops = 6 * points * m * c
    args = (*lats, *pts, dec_norm, enc_norm, *before)
    *sums, kept = call(kernel, outs, args, scratch, flops)
    return sums, kept


def decoder_pass(plan, lats, pts, dec_norm, heads):
    n_lat = len(lats)
    c, m = plan.cols, plan.latents

    def kernel(*refs):
        lat_refs, pts_refs, dec_ref = refs[:n_lat], refs[n_lat:-6], refs[-6]
        key_ref, lat_ref = refs[-5:-3]
        both, keys_t, ds = refs[-3:]
        for k, ref in enumerate(lat_refs):
            both[:, k * plan.block : (k + 1) * plan.block] = ref[...]
        for j, ref in enumerate(pts_refs):
            keys_t[:, j * plan.rows : (j + 1) * plan.rows] = turned(ref[: plan.rows, :c])
        for at, h in enumerate(heads):
            mine = slice(h * HEAD_DIM, (h + 1) * HEAD_DIM)
            put = slice(at * HEAD_DIM, (at + 1) * HEAD_DIM)
            other = slice(c + h * HEAD_DIM, c + (h + 1) * HEAD_DIM)
            for j, ref in enumerate(pts_refs):
                rows = slice(j * plan.rows, (j + 1) * plan.rows)
                scores = nn(ref[: plan.rows, mine], both[mine, :]) * (HEAD_DIM**-0.5 * LOG2E)
                dec = jnp.exp2(scores - dec_ref[rows, h : h + 1] * LOG2E)
                grad = nn(ref[: plan.rows, other], both[other, :])
                total = jnp.sum(dec * grad, axis=1, keepdims=True)
                tile = (dec * (grad - total)).astype(jnp.bfloat16)
                ds[rows, :] = tile
            key_ref[put, :] = nt(both[mine, :], ds[...])
            lat_ref[put, :] = nn(keys_t[mine, :], ds[...])

    width = len(heads) * HEAD_DIM
    outs = [shaped((width, plan.points), jnp.float32), shaped((width, m), jnp.float32)]
    scratch = [
        pltpu.VMEM((2 * c, m), jnp.bfloat16),
        pltpu.VMEM((c, plan.points), jnp.bfloat16),
        pltpu.VMEM((plan.points, m), jnp.bfloat16),
    ]
    flops = 8 * plan.points * m * width
    return call(kernel, outs, (*lats, *pts, dec_norm), scratch, flops)


def add_and_scale(plan, mine, theirs):
    n = len(plan.chip_steps())
    tall = mine.shape[0] // n

    def kernel(mine_ref, theirs_ref, *outs):
        for k, out in enumerate(outs):
            rows = slice(k * tall, (k + 1) * tall)
            total = mine_ref[rows, :] + theirs_ref[rows, :]
            if k == 0:
                out[...] = total
                continue
            sizes = []
            for at in range(0, tall, HEAD_DIM):
                part = total[at : at + HEAD_DIM]
                most = jnp.max(jnp.abs(part), axis=0, keepdims=True)
                size = jnp.ceil(jnp.log2(jnp.maximum(most, SMALLEST)))
                out[at : at + HEAD_DIM, :] = part * jnp.exp2(HALF_SIZE - size)
                sizes.append(size)
            fill = jnp.zeros((16 - len(sizes), plan.block), jnp.float32)
            out[tall:, :] = jnp.concatenate([*sizes, fill], axis=0)

    outs = [shaped((tall + 16 * (k > 0), plan.block), jnp.float32) for k in range(n)]
    return call(kernel, outs, (mine, theirs))


def scaled_sum(own, *scaled):
    tall = own.shape[0]
    pieces = []
    for n, at in enumerate(range(0, tall, HEAD_DIM)):
        piece = own[at : at + HEAD_DIM, :]
        for ref in scaled:
            size = ref[tall + n : tall + n + 1, :]
            piece = piece + ref[at : at + HEAD_DIM, :] * jnp.exp2(size - HALF_SIZE)
        pieces.append(piece)
    return jnp.concatenate(pieces, axis=0)


def reduce_mix(plan, parts):
    c, hs = plan.cols, plan.heads

    def kernel(*refs):
        *ins, out = refs
        total = scaled_sum(*ins)
        half = total[:c].astype(jnp.bfloat16)
        out[:c, :] = half
        product = half.astype(jnp.float32) * total[c:]
        sums = [
            jnp.sum(product[h * HEAD_DIM : (h + 1) * HEAD_DIM], axis=0, keepdims=True) for h in range(hs)
        ]
        fill = jnp.zeros((16 - 3 * hs, plan.block), jnp.float32)
        stack = jnp.concatenate([*split3(jnp.concatenate(sums, axis=0)), fill], axis=0)
        out[c:, :] = stack.astype(jnp.bfloat16)

    outs = [shaped((plan.ct_rows, plan.block), jnp.bfloat16)]
    return call(kernel, outs, parts)[0]


def encoder_pass(plan, lats, pts, kept, mixes, before):
    places = [(part, at) for part, (heads, _) in enumerate(before) for at in range(len(heads))]
    n_lat, n_pts, n_mix = len(lats), len(pts), len(mixes)
    c, m, hs = plan.cols, plan.latents, plan.heads

    def kernel(*refs):
        refs = list(refs)

        def take(n):
            got = refs[:n]
            del refs[:n]
            return got

        lat_refs, pts_refs = take(n_lat), take(n_pts)
        kept_refs = take(len(kept))
        mix_refs = take(n_mix)
        parts_in = [take(2) for _ in before]
        pts_outs, lat_outs = take(n_pts), plan.views(*take(2), c)
        query, mix, keys_t, values, ds, encs = refs
        for k, ref in enumerate(lat_refs):
            query[:, k * plan.block : (k + 1) * plan.block] = ref[:c, :]
        for k, ref in enumerate(mix_refs):
            mix[:, k * plan.block : (k + 1) * plan.block] = ref[...]
        for j, ref in enumerate(pts_refs):
            rows = slice(j * plan.rows, (j + 1) * plan.rows)
            keys_t[:, rows] = turned(ref[: plan.rows, :c])
            across = [ref[plan.rows :, h * plan.rows : (h + 1) * plan.rows] for h in range(hs)]
            values[rows, :] = turned(jnp.concatenate(across, axis=0))
        tail = mix[c:, :].astype(jnp.float32)
        columns = (tail[:hs] + tail[hs : 2 * hs]) + tail[2 * hs : 3 * hs]
        tiles = lane_tiles(plan)
        sums = {}

        def weigh(h, t, slot):
            mine, lanes = slice(h * HEAD_DIM, (h + 1) * HEAD_DIM), tiles[t]
            enc = jnp.concatenate([ref[h, :, lanes] for ref in kept_refs], axis=0)
            grad = nn(values[:, mine], mix[mine, lanes])
            encs[slot] = enc.astype(jnp.bfloat16)
            ds[slot] = (enc * (grad - columns[h : h + 1, lanes])).astype(jnp.bfloat16)

        def gather(h, t, slot):
            mine, lanes = slice(h * HEAD_DIM, (h + 1) * HEAD_DIM), tiles[t]
            part, at = places[h]
            key_in, lat_in = parts_in[part]
            put = slice(at * HEAD_DIM, (at + 1) * HEAD_DIM)
            lat = (lat_in[put, lanes] + nn(keys_t[mine, :], ds[slot])) * HEAD_DIM**-0.5
            store_blocks(plan, lat_outs, mine, lanes, lat)
            key, value = nt(query[mine, lanes], ds[slot]), nt(mix[mine, lanes], encs[slot])
            key = key + (sums[h][0] if t else key_in[put, :])
            sums[h] = (key, value + sums[h][1] if t else value)
            if t < len(tiles) - 1:
                return
            key, value = sums.pop(h)
            key = (key * HEAD_DIM**-0.5).T.astype(jnp.bfloat16)
            value = value.T.astype(jnp.bfloat16)
            for j, out in enumerate(pts_outs):
                rows = slice(j * plan.rows, (j + 1) * plan.rows)
                out[:, mine] = key[rows]
                out[:, c + h * HEAD_DIM : c + (h + 1) * HEAD_DIM] = value[rows]

        work = [(h, t) for h in range(hs) for t in range(len(tiles))]
        for n, place in enumerate(work):
            weigh(*place, n % SLOTS)
            if n >= LAG:
                gather(*work[n - LAG], (n - LAG) % SLOTS)
        for n in range(len(work) - LAG, len(work)):
            gather(*work[n], n % SLOTS)

    outs = [shaped((plan.rows, 2 * c), jnp.bfloat16)] * n_pts
    outs += [plan.stack(c)] * 2
    scratch = [
        pltpu.VMEM((c, m), jnp.bfloat16),
        pltpu.VMEM((plan.ct_rows, m), jnp.bfloat16),
        pltpu.VMEM((c, plan.points), jnp.bfloat16),
        pltpu.VMEM((plan.points, c), jnp.bfloat16),
        pltpu.VMEM((SLOTS, plan.points, 2 * plan.block), jnp.bfloat16),
        pltpu.VMEM((SLOTS, plan.points, 2 * plan.block), jnp.bfloat16),
    ]
    flops = 10 * plan.points * m * c
    args = (*lats, *pts, *kept, *mixes, *(a for _, part in before for a in part))
    got = call(kernel, outs, args, scratch, flops)
    return got[:n_pts], got[n_pts:]


def reduce_latents(plan, parts):
    def kernel(*refs):
        ins, outs = refs[: len(parts)], refs[len(parts) :]
        total = scaled_sum(*ins).T
        for j, out in enumerate(outs):
            rows = total[j * plan.lat_rows : (j + 1) * plan.lat_rows]
            n, half = plan.lat_rows, plan.lat_rows // 2
            out[:n, :] = rows[:, :LANES]
            out[n:, :] = jnp.concatenate([rows[:half, LANES:], rows[half:, LANES:]], axis=1)

    outs = [shaped((3 * plan.lat_rows // 2, LANES), jnp.float32)] * GROUPS
    return call(kernel, outs, parts)


def place_points(plan, slots):
    def kernel(*refs):
        ins, (key_out, value_out) = refs[:GROUPS], refs[GROUPS:]
        z = group_index(plan)
        c = plan.cols
        pieces = by_group([r[...].astype(jnp.float32) for r in ins], z)
        for g, piece in enumerate(pieces):
            key_out[:, g * c : (g + 1) * c] = piece[:, :c].astype(jnp.bfloat16)
            value_out[:, g * c : (g + 1) * c] = piece[:, c:].astype(jnp.bfloat16)

    outs = [shaped((plan.rows, plan.width), jnp.bfloat16)] * 2
    return call(kernel, outs, slots)


def place_latents(plan, slots):
    def kernel(*refs):
        *ins, out = refs
        n, at = plan.lat_rows, plan.cols - LANES
        for g, piece in enumerate(by_group([r[...] for r in ins], group_index(plan))):
            rest = jnp.concatenate([piece[n:, :at], piece[n:, at:]], axis=0)
            out[:, g * plan.cols : (g + 1) * plan.cols] = jnp.concatenate([piece[:n], rest], axis=1)

    outs = [shaped((plan.lat_rows, plan.width), jnp.float32)]
    return call(kernel, outs, slots)[0]


def grouped(
    plan, point_keys, point_values, out_grad, decoder_norm, latent_query, latent_out, encoder_norm
):
    def over_group(slots):
        got = [slots[0]]
        for j in range(1, GROUPS):
            got.append(plan.exchange(slots[j], True, j))
        return got

    def from_chips(blocks):
        got = []
        for k, block in zip(plan.chip_steps(), blocks, strict=True):
            got.append(plan.exchange(block, False, k) if k else block)
        return got

    def sum_cores(mine, away):
        theirs = plan.exchange(away, False, plan.fast)
        return add_and_scale(plan, mine, theirs)

    def sum_chips(blocks):
        halves = [blocks[0], *(block.astype(jnp.float16) for block in blocks[1:])]
        return [block.astype(jnp.float32) for block in from_chips(halves)]

    def to_plane(block):
        got = dict(zip(plan.chip_steps(), from_chips([block] * len(plan.chip_steps())), strict=True))
        for k in plan.chip_steps():
            got[k | plan.fast] = plan.exchange(got[k], False, plan.fast)
        return tuple(got[k] for k in range(plan.plane))

    lat_slots, pts = pack(
        plan, latent_query, latent_out, decoder_norm, point_keys, out_grad, point_values
    )
    lat_slots = over_group(lat_slots)
    pts = over_group(pts)
    norm = order_norm(plan, encoder_norm)
    block, dec_norm = turn_latents(plan, lat_slots)
    lats = to_plane(block)
    half = GROUPS // 2
    sums, kept = first_pass(plan, lats, pts[:half], 0, dec_norm, norm)
    sums, more = first_pass(plan, lats, pts[half:], half, dec_norm, norm, sums)
    kept = (kept, more)
    cores = sum_cores(*sums)
    sums = sum_chips(cores)
    every = tuple(range(plan.heads))
    before = [(every, decoder_pass(plan, lats, pts, dec_norm, every))]
    mixes = to_plane(reduce_mix(plan, sums))
    pts_out, lat_out = encoder_pass(plan, lats, pts, kept, mixes, before)
    lat_out = sum_chips(sum_cores(*lat_out))
    pts_out = over_group(pts_out)
    lat_rows = over_group(reduce_latents(plan, lat_out))
    keys_grad, values_grad = place_points(plan, pts_out)
    return keys_grad, values_grad, place_latents(plan, lat_rows)


def column(block, current):
    return lax.dynamic_slice_in_dim(block, current * HEAD_DIM, HEAD_DIM, 1)


def put_head(total, piece, current):
    return lax.dynamic_update_slice_in_dim(total, piece, current * HEAD_DIM, 1)


def add_head(total, piece, current):
    return put_head(total, column(total, current) + piece, current)


def across(left, right):
    return lax.dot_general(
        left, right, (((1,), (1,)), ((), ())), preferred_element_type=jnp.float32
    )


def down_rows(left, right):
    return lax.dot_general(
        left, right, (((0,), (0,)), ((), ())), preferred_element_type=jnp.float32
    )


def gathered(
    point_keys, point_values, out_grad, decoder_norm, latent_query, latent_out, encoder_norm
):
    scale_factor = HEAD_DIM ** (-0.5)
    lat_all, out_all = (
        lax.all_gather(latent_query, ("pa", "pb"), axis=0, tiled=True),
        lax.all_gather(latent_out, ("pa", "pb"), axis=0, tiled=True),
    )
    point_rows = point_keys.shape[0]
    latent_rows = lat_all.shape[0]
    width = point_keys.shape[1]

    def encoder_row(current):
        return lax.dynamic_slice_in_dim(encoder_norm, current, 1, 0)

    def pass_one(current, state):
        mix_acc, query_acc, key_acc, weighted_acc = state
        key_head = column(point_keys, current)
        grad_head = column(out_grad, current)
        lat_head = column(lat_all, current)
        scores = across(key_head, lat_head) * scale_factor
        decoder_weights = jnp.exp(scores - lax.dynamic_slice_in_dim(decoder_norm, current, 1, 0).T)
        decoder_gradient = across(grad_head, column(out_all, current))
        row_total = jnp.sum(decoder_weights * decoder_gradient, axis=1, keepdims=True)
        decoder_scores_grad = (decoder_weights * (decoder_gradient - row_total)).astype(
            jnp.bfloat16
        )
        mix_acc = put_head(
            mix_acc, down_rows(decoder_weights.astype(jnp.bfloat16), grad_head), current
        )
        query_acc = put_head(
            query_acc, down_rows(decoder_scores_grad, key_head) * scale_factor, current
        )
        key_acc = put_head(
            key_acc,
            jnp.dot(decoder_scores_grad, lat_head, preferred_element_type=jnp.float32)
            * scale_factor,
            current,
        )
        return (mix_acc, query_acc, key_acc, weighted_acc)

    weighted_blank = jnp.zeros((1, 1), jnp.float32)
    latent_blank = jnp.zeros((latent_rows, width), jnp.float32)
    begin = (
        latent_blank,
        latent_blank,
        jnp.zeros((point_rows, width), jnp.float32),
        weighted_blank,
    )
    mix_acc, query_acc, key_acc, _ = lax.fori_loop(0, HEADS, pass_one, begin)
    mix_grad = lax.psum(mix_acc, ("pa", "pb"))
    mixing_portion = mix_grad.astype(jnp.bfloat16)

    def pass_two(current, state):
        partial_rows, value_acc = state
        scores = across(column(point_keys, current), column(lat_all, current)) * scale_factor
        encoder_portion = jnp.exp(scores - encoder_row(current)).astype(jnp.bfloat16)
        mix_head = column(mixing_portion, current)
        encoder_gradient = across(column(point_values, current), mix_head)
        sums = jnp.sum(encoder_portion.astype(jnp.float32) * encoder_gradient, axis=0)[None, :]
        partial_rows = lax.dynamic_update_slice_in_dim(partial_rows, sums, current, 0)
        value_acc = put_head(
            value_acc,
            jnp.dot(encoder_portion, mix_head, preferred_element_type=jnp.float32),
            current,
        )
        return (partial_rows, value_acc)

    partial_rows, value_acc = lax.fori_loop(
        0,
        HEADS,
        pass_two,
        (jnp.zeros((HEADS, latent_rows), jnp.float32), jnp.zeros((point_rows, width), jnp.float32)),
    )
    column_total = lax.psum(partial_rows, ("pa", "pb"))

    def pass_three(current, state):
        query_acc, key_acc, value_acc = state
        key_head = column(point_keys, current)
        lat_head = column(lat_all, current)
        mix_head = column(mixing_portion, current)
        scores = across(key_head, lat_head) * scale_factor
        encoder = jnp.exp(scores - encoder_row(current))
        encoder_gradient = across(column(point_values, current), mix_head)
        encoder_scores_grad = (
            encoder * (encoder_gradient - lax.dynamic_slice_in_dim(column_total, current, 1, 0))
        ).astype(jnp.bfloat16)
        query_acc = add_head(
            query_acc, down_rows(encoder_scores_grad, key_head) * scale_factor, current
        )
        key_acc = add_head(
            key_acc,
            jnp.dot(encoder_scores_grad, lat_head, preferred_element_type=jnp.float32)
            * scale_factor,
            current,
        )
        return (query_acc, key_acc, value_acc)

    query_acc, key_acc, value_acc = lax.fori_loop(
        0, HEADS, pass_three, (query_acc, key_acc, value_acc)
    )
    latent_grad = lax.psum_scatter(query_acc, ("pa", "pb"), scatter_dimension=0, tiled=True)
    return (key_acc.astype(jnp.bfloat16), value_acc.astype(jnp.bfloat16), latent_grad)


def solution(mesh):
    in_specs = (
        P(("pa", "pb"), None),
        P(("pa", "pb"), None),
        P(("pa", "pb"), None),
        P(None, ("pa", "pb")),
        P(("pa", "pb"), None),
        P(("pa", "pb"), None),
        P(),
    )
    out_specs = (P(("pa", "pb"), None), P(("pa", "pb"), None), P(("pa", "pb"), None))
    npa, npb = mesh.shape["pa"], mesh.shape["pb"]

    def shards(*args):
        plan_of = (npa, npb, args[0].shape[0], args[4].shape[0], args[0].shape[1])
        if Plan.fits(*plan_of):
            return grouped(Plan(*plan_of), *args)
        return gathered(*args)

    return jax.shard_map(shards, mesh=mesh, in_specs=in_specs, out_specs=out_specs, check_vma=False)
```

```python
import math

import jax
import jax.numpy as jnp
from jax import lax
from jax.experimental import pallas as pl
from jax.experimental.pallas import tpu as pltpu
from jax.sharding import PartitionSpec as P


HEADS = 12
HEAD_DIM = 64
LANES = 128
AXES = ("pa", "pb")
MOST_IN_PLANE = 16
HALF_SIZE, SMALLEST = 14.0, 2.0**-100
LAG, SLOTS = 1, 3
GROUPS = 4
VMEM_BYTES = 20 * 2**20
LOG2E = math.log2(math.e)


class Plan:
    def __init__(self, npa, npb, rows, lat_rows, width):
        self.npa, self.npb = npa, npb
        self.fast = npb // GROUPS
        self.plane = npa * self.fast
        self.rows, self.lat_rows, self.width = rows, lat_rows, width
        self.heads = HEADS // GROUPS
        self.cols = self.heads * HEAD_DIM
        self.points = rows * GROUPS
        self.block = lat_rows * GROUPS
        self.latents = self.block * self.plane
        self.slot = lat_rows + 16
        self.ct_rows = self.cols + 16

    @staticmethod
    def fits(npa, npb, rows, lat_rows, width):
        def power(v):
            return v > 0 and v & (v - 1) == 0

        return (
            power(npa)
            and power(npb)
            and npb % (2 * GROUPS) == 0
            and npa * npb // GROUPS <= MOST_IN_PLANE
            and lat_rows * GROUPS == LANES
            and rows == LANES
            and HEADS % GROUPS == 0
            and HEADS // GROUPS * rows == 2 * HEADS // GROUPS * HEAD_DIM
            and width == HEADS * HEAD_DIM
            and 2 * width // GROUPS == 3 * LANES
        )

    def chip_steps(self):
        return [k for k in range(self.plane) if not k & self.fast]

    def views(self, mine, away, tall):
        at = {k: slice(i * tall, (i + 1) * tall) for i, k in enumerate(self.chip_steps())}
        return [(away if k & self.fast else mine).at[at[k & ~self.fast]] for k in range(self.plane)]

    def stack(self, tall):
        return shaped((len(self.chip_steps()) * tall, self.block), jnp.float32)

    def exchange(self, value, over_group, step):
        pairs = []
        for a in range(self.npa):
            for b in range(self.npb):
                z, f = divmod(b, self.fast)
                if over_group:
                    a2, z2, f2 = a, z ^ step, f
                else:
                    a2, z2, f2 = a ^ (step // self.fast), z, f ^ (step % self.fast)
                pairs.append((a * self.npb + b, a2 * self.npb + z2 * self.fast + f2))
        return lax.ppermute(value, AXES, pairs)


def call(kernel, outs, args, scratch=(), flops=0, space=pltpu.VMEM):
    nbytes = sum(a.size * a.dtype.itemsize for a in args)
    nbytes += sum(math.prod(o.shape) * o.dtype.itemsize for o in outs)
    return pl.pallas_call(
        kernel,
        out_shape=tuple(outs),
        in_specs=[pl.BlockSpec(memory_space=space)] * len(args),
        out_specs=tuple(pl.BlockSpec(memory_space=pltpu.VMEM) for _ in outs),
        scratch_shapes=list(scratch),
        cost_estimate=pl.CostEstimate(flops=flops, bytes_accessed=nbytes, transcendentals=flops // 256),
        compiler_params=pltpu.CompilerParams(vmem_limit_bytes=VMEM_BYTES),
    )(*args)


def call_from_hbm(kernel, outs, args):
    n = len(args)

    def body(*refs):
        held, sems = refs[-n - 1 : -1], refs[-1]
        copies = [
            pltpu.make_async_copy(src, dst, sems.at[i])
            for i, (src, dst) in enumerate(zip(refs[:n], held, strict=True))
        ]
        for copy in copies:
            copy.start()
        for copy in copies:
            copy.wait()
        kernel(*held, *refs[n : -n - 1])

    scratch = [pltpu.VMEM(a.shape, a.dtype) for a in args] + [pltpu.SemaphoreType.DMA((n,))]
    args = [pltpu.with_memory_space_constraint(a, pltpu.HBM) for a in args]
    return call(body, outs, args, scratch, space=pltpu.HBM)


def shaped(shape, dtype):
    return jax.ShapeDtypeStruct(shape, dtype)


def by_group(pieces, z):
    out = list(pieces)
    bit = 1
    while bit < len(out):
        on = (z & bit) != 0
        out = [jnp.where(on, out[g ^ bit], out[g]) for g in range(len(out))]
        bit *= 2
    return out


def group_index(plan):
    return lax.axis_index("pb") // plan.fast


def split3(value):
    hi = value.astype(jnp.bfloat16).astype(jnp.float32)
    rest = value - hi
    mid = rest.astype(jnp.bfloat16).astype(jnp.float32)
    return hi, mid, rest - mid


def nn(a, b):
    return lax.dot_general(a, b, (((1,), (0,)), ((), ())), preferred_element_type=jnp.float32)


def nt(a, b):
    return lax.dot_general(a, b, (((1,), (1,)), ((), ())), preferred_element_type=jnp.float32)


def turned(block):
    return block.astype(jnp.float32).T.astype(block.dtype)


def pack(plan, query, out, norm, keys, grads, values):
    def kernel(q_ref, o_ref, n_ref, k_ref, g_ref, v_ref, *outs):
        z = group_index(plan)
        c, hs = plan.cols, plan.heads
        q, o = q_ref[...].astype(jnp.float32), o_ref[...].astype(jnp.float32)
        parts = split3(n_ref[...])
        fill = jnp.zeros((plan.slot - plan.lat_rows - 3, hs * plan.rows), jnp.float32)
        pieces = []
        for g in range(GROUPS):
            top = jnp.concatenate([q[:, g * c : (g + 1) * c], o[:, g * c : (g + 1) * c]], axis=1)
            lines = [
                jnp.concatenate([p[h : h + 1, :] for h in range(g * hs, (g + 1) * hs)], axis=1) for p in parts
            ]
            pieces.append(jnp.concatenate([top, *lines, fill], axis=0).astype(jnp.bfloat16))
        for ref, piece in zip(outs[:GROUPS], by_group(pieces, z), strict=True):
            ref[...] = piece
        outs = outs[GROUPS:]
        for first, ref in ((0, k_ref), (1, g_ref)):
            pieces = by_group([ref[:, g * c : (g + 1) * c] for g in range(GROUPS)], z)
            for out, piece in zip(outs, pieces, strict=True):
                out[: plan.rows, first * c : (first + 1) * c] = piece
        across = v_ref[...].T
        pieces = by_group([across[g * c : (g + 1) * c] for g in range(GROUPS)], z)
        for out, piece in zip(outs, pieces, strict=True):
            for h in range(hs):
                lanes = slice(h * plan.rows, (h + 1) * plan.rows)
                out[plan.rows :, lanes] = piece[h * HEAD_DIM : (h + 1) * HEAD_DIM]

    outs = [shaped((plan.slot, 2 * plan.cols), jnp.bfloat16)] * GROUPS
    outs += [shaped((plan.rows + HEAD_DIM, 2 * plan.cols), jnp.bfloat16)] * GROUPS
    got = call_from_hbm(kernel, outs, (query, out, norm, keys, grads, values))
    return got[:GROUPS], got[GROUPS:]


def order_norm(plan, norm):
    def kernel(n_ref, out_ref):
        z = group_index(plan)
        member = lax.axis_index("pa") * plan.npb + lax.axis_index("pb")
        hs, m = plan.heads, plan.latents
        rows = by_group([n_ref[g * hs : (g + 1) * hs, :] for g in range(GROUPS)], z)[0]
        fill = jnp.zeros((16 - 3 * hs, m), jnp.float32)
        stack = jnp.concatenate([*split3(rows), fill], axis=0).astype(jnp.bfloat16)
        lane = lax.broadcasted_iota(jnp.int32, (1, m), 1)
        inner, j, k = lane % plan.lat_rows, (lane // plan.lat_rows) % GROUPS, lane // plan.block
        owner = (k // plan.fast) * plan.npb + j * plan.fast + k % plan.fast
        source = (owner ^ member) * plan.lat_rows + inner
        total = jnp.zeros((16, m), jnp.float32)
        step = 256
        for start in range(0, m, step):
            row = lax.broadcasted_iota(jnp.int32, (step, m), 0) + start
            chosen = jnp.where(row == source, 1.0, 0.0).astype(jnp.bfloat16)
            total = total + nn(stack[:, start : start + step], chosen)
        out_ref[0:hs, :] = (total[:hs] + total[hs : 2 * hs]) + total[2 * hs : 3 * hs]

    outs = [shaped((plan.heads, plan.latents), jnp.float32)]
    return call_from_hbm(kernel, outs, (norm,))[0]


def turn_latents(plan, slots):
    def kernel(*refs):
        *slots, out, norm_out = refs
        n, rows = plan.lat_rows, plan.rows
        slots = [s[...] for s in slots]
        out[...] = turned(jnp.concatenate([s[:n] for s in slots], axis=0))
        for j, slot in enumerate(slots):
            parts = slot[n : n + 3].astype(jnp.float32)
            line = (parts[0:1] + parts[1:2]) + parts[2:3]
            lines = [line[:, h * rows : (h + 1) * rows] for h in range(plan.heads)]
            fill = jnp.zeros((LANES - plan.heads, rows), jnp.float32)
            norm_out[j * rows : (j + 1) * rows, :] = jnp.concatenate([*lines, fill], axis=0).T

    outs = [
        shaped((2 * plan.cols, plan.block), jnp.bfloat16),
        shaped((plan.points, LANES), jnp.float32),
    ]
    return call(kernel, outs, slots)


def lane_tiles(plan):
    width = min(2 * plan.block, plan.latents)
    return [slice(at, at + width) for at in range(0, plan.latents, width)]


def store_blocks(plan, outs, rows, lanes, value):
    for at in range(lanes.start, lanes.stop, plan.block):
        outs[at // plan.block][rows, :] = value[:, at - lanes.start : at - lanes.start + plan.block]


def load_blocks(plan, refs, rows, lanes):
    blocks = range(lanes.start // plan.block, lanes.stop // plan.block)
    return jnp.concatenate([refs[k][rows, :] for k in blocks], axis=1)


def first_pass(plan, lats, pts, at, dec_norm, enc_norm, before=()):
    n_lat, n_pts = len(lats), len(pts)
    c, m = plan.cols, plan.latents
    points = n_pts * plan.rows

    def kernel(*refs):
        lat_refs, pts_refs, rest = refs[:n_lat], refs[n_lat : n_lat + n_pts], refs[n_lat + n_pts :]
        dec_ref, enc_ref = rest[:2]
        earlier = plan.views(*rest[2:4], 2 * c) if before else ()
        outs, kept = plan.views(*refs[-6:-4], 2 * c), refs[-4]
        query, sides, keys = refs[-3:]
        for k, ref in enumerate(lat_refs):
            query[:, k * plan.block : (k + 1) * plan.block] = ref[:c, :]
        for j, ref in enumerate(pts_refs):
            rows = slice(j * plan.rows, (j + 1) * plan.rows)
            keys[rows, :] = ref[: plan.rows, :c]
            sides[:c, rows] = turned(ref[: plan.rows, c:])
            for h in range(plan.heads):
                below = slice(c + h * HEAD_DIM, c + (h + 1) * HEAD_DIM)
                sides[below, rows] = ref[plan.rows :, h * plan.rows : (h + 1) * plan.rows]
        for h in range(plan.heads):
            mine = slice(h * HEAD_DIM, (h + 1) * HEAD_DIM)
            below = slice(c + h * HEAD_DIM, c + (h + 1) * HEAD_DIM)
            key = keys[:, mine]
            row_norm = dec_ref[at * plan.rows : at * plan.rows + points, h : h + 1] * LOG2E
            for lanes in lane_tiles(plan):
                scores = nn(key, query[mine, lanes]) * (HEAD_DIM**-0.5 * LOG2E)
                dec = jnp.exp2(scores - row_norm).astype(jnp.bfloat16)
                enc = jnp.exp2(scores - enc_ref[h : h + 1, lanes] * LOG2E)
                kept[h, :, lanes] = enc
                for rows, half in ((mine, dec), (below, enc.astype(jnp.bfloat16))):
                    total = nn(sides[rows, :], half)
                    if earlier:
                        total = total + load_blocks(plan, earlier, rows, lanes)
                    store_blocks(plan, outs, rows, lanes, total)

    outs = [plan.stack(2 * c)] * 2 + [shaped((plan.heads, points, m), jnp.float32)]
    scratch = [
        pltpu.VMEM((c, m), jnp.bfloat16),
        pltpu.VMEM((2 * c, points), jnp.bfloat16),
        pltpu.VMEM((points, c), jnp.bfloat16),
    ]
    flops = 6 * points * m * c
    args = (*lats, *pts, dec_norm, enc_norm, *before)
    *sums, kept = call(kernel, outs, args, scratch, flops)
    return sums, kept


def decoder_pass(plan, lats, pts, dec_norm, heads):
    n_lat = len(lats)
    c, m = plan.cols, plan.latents

    def kernel(*refs):
        lat_refs, pts_refs, dec_ref = refs[:n_lat], refs[n_lat:-6], refs[-6]
        key_ref, lat_ref = refs[-5:-3]
        both, keys_t, ds = refs[-3:]
        for k, ref in enumerate(lat_refs):
            both[:, k * plan.block : (k + 1) * plan.block] = ref[...]
        for j, ref in enumerate(pts_refs):
            keys_t[:, j * plan.rows : (j + 1) * plan.rows] = turned(ref[: plan.rows, :c])
        for at, h in enumerate(heads):
            mine = slice(h * HEAD_DIM, (h + 1) * HEAD_DIM)
            put = slice(at * HEAD_DIM, (at + 1) * HEAD_DIM)
            other = slice(c + h * HEAD_DIM, c + (h + 1) * HEAD_DIM)
            for j, ref in enumerate(pts_refs):
                rows = slice(j * plan.rows, (j + 1) * plan.rows)
                scores = nn(ref[: plan.rows, mine], both[mine, :]) * (HEAD_DIM**-0.5 * LOG2E)
                dec = jnp.exp2(scores - dec_ref[rows, h : h + 1] * LOG2E)
                grad = nn(ref[: plan.rows, other], both[other, :])
                total = jnp.sum(dec * grad, axis=1, keepdims=True)
                tile = (dec * (grad - total)).astype(jnp.bfloat16)
                ds[rows, :] = tile
            key_ref[put, :] = nt(both[mine, :], ds[...])
            lat_ref[put, :] = nn(keys_t[mine, :], ds[...])

    width = len(heads) * HEAD_DIM
    outs = [shaped((width, plan.points), jnp.float32), shaped((width, m), jnp.float32)]
    scratch = [
        pltpu.VMEM((2 * c, m), jnp.bfloat16),
        pltpu.VMEM((c, plan.points), jnp.bfloat16),
        pltpu.VMEM((plan.points, m), jnp.bfloat16),
    ]
    flops = 8 * plan.points * m * width
    return call(kernel, outs, (*lats, *pts, dec_norm), scratch, flops)


def add_and_scale(plan, mine, theirs):
    n = len(plan.chip_steps())
    tall = mine.shape[0] // n

    def kernel(mine_ref, theirs_ref, *outs):
        for k, out in enumerate(outs):
            rows = slice(k * tall, (k + 1) * tall)
            total = mine_ref[rows, :] + theirs_ref[rows, :]
            if k == 0:
                out[...] = total
                continue
            sizes = []
            for at in range(0, tall, HEAD_DIM):
                part = total[at : at + HEAD_DIM]
                most = jnp.max(jnp.abs(part), axis=0, keepdims=True)
                size = jnp.ceil(jnp.log2(jnp.maximum(most, SMALLEST)))
                out[at : at + HEAD_DIM, :] = part * jnp.exp2(HALF_SIZE - size)
                sizes.append(size)
            fill = jnp.zeros((16 - len(sizes), plan.block), jnp.float32)
            out[tall:, :] = jnp.concatenate([*sizes, fill], axis=0)

    outs = [shaped((tall + 16 * (k > 0), plan.block), jnp.float32) for k in range(n)]
    return call(kernel, outs, (mine, theirs))


def scaled_sum(own, *scaled):
    tall = own.shape[0]
    pieces = []
    for n, at in enumerate(range(0, tall, HEAD_DIM)):
        piece = own[at : at + HEAD_DIM, :]
        for ref in scaled:
            size = ref[tall + n : tall + n + 1, :]
            piece = piece + ref[at : at + HEAD_DIM, :] * jnp.exp2(size - HALF_SIZE)
        pieces.append(piece)
    return jnp.concatenate(pieces, axis=0)


def reduce_mix(plan, parts):
    c, hs = plan.cols, plan.heads

    def kernel(*refs):
        *ins, out = refs
        total = scaled_sum(*ins)
        half = total[:c].astype(jnp.bfloat16)
        out[:c, :] = half
        product = half.astype(jnp.float32) * total[c:]
        sums = [
            jnp.sum(product[h * HEAD_DIM : (h + 1) * HEAD_DIM], axis=0, keepdims=True) for h in range(hs)
        ]
        fill = jnp.zeros((16 - 3 * hs, plan.block), jnp.float32)
        stack = jnp.concatenate([*split3(jnp.concatenate(sums, axis=0)), fill], axis=0)
        out[c:, :] = stack.astype(jnp.bfloat16)

    outs = [shaped((plan.ct_rows, plan.block), jnp.bfloat16)]
    return call(kernel, outs, parts)[0]


def encoder_pass(plan, lats, pts, kept, mixes, before, carried=None):
    places = [(part, at) for part, (heads, _) in enumerate(before) for at in range(len(heads))]
    n_lat, n_pts, n_mix = len(lats), len(pts), len(mixes)
    c, m, hs = plan.cols, plan.latents, plan.heads

    held = [k for k in range(plan.plane) if bool(k & plan.fast) == bool(carried)]
    mixes = [mixes[k] for k in held]
    n_mix = len(mixes)

    def kernel(*refs):
        refs = list(refs)

        def take(n):
            got = refs[:n]
            del refs[:n]
            return got

        lat_refs, pts_refs = take(n_lat), take(n_pts)
        kept_refs = take(len(kept))
        mix_refs = take(n_mix)
        parts_in = [take(2) for _ in before]
        so_far = take(2) if carried else None
        pts_outs = take(n_pts if carried else 2)
        (stack,) = take(1)
        lat_outs = plan.views(stack, stack, c)
        query, mix, keys_t, values, ds, encs = refs
        for k, ref in enumerate(lat_refs):
            query[:, k * plan.block : (k + 1) * plan.block] = ref[:c, :]
        for k, ref in zip(held, mix_refs, strict=True):
            mix[:, k * plan.block : (k + 1) * plan.block] = ref[...]
        for j, ref in enumerate(pts_refs):
            rows = slice(j * plan.rows, (j + 1) * plan.rows)
            keys_t[:, rows] = turned(ref[: plan.rows, :c])
            across = [ref[plan.rows :, h * plan.rows : (h + 1) * plan.rows] for h in range(hs)]
            values[rows, :] = turned(jnp.concatenate(across, axis=0))
        tiles = lane_tiles(plan)
        sums = {}
        chosen = [t for t, s in enumerate(tiles) if bool(s.start // plan.block & plan.fast) == bool(carried)]

        def weigh(h, t, slot):
            mine, lanes = slice(h * HEAD_DIM, (h + 1) * HEAD_DIM), tiles[t]
            enc = jnp.concatenate([ref[h, :, lanes] for ref in kept_refs], axis=0)
            grad = nn(values[:, mine], mix[mine, lanes])
            tail = [mix[c : c + 16, lanes].astype(jnp.float32)[n * hs + h : n * hs + h + 1] for n in range(3)]
            column = (tail[0] + tail[1]) + tail[2]
            encs[slot] = enc.astype(jnp.bfloat16)
            ds[slot] = (enc * (grad - column)).astype(jnp.bfloat16)

        def gather(h, t, slot):
            mine, lanes = slice(h * HEAD_DIM, (h + 1) * HEAD_DIM), tiles[t]
            part, at = places[h]
            key_in, lat_in = parts_in[part]
            put = slice(at * HEAD_DIM, (at + 1) * HEAD_DIM)
            lat = (lat_in[put, lanes] + nn(keys_t[mine, :], ds[slot])) * HEAD_DIM**-0.5
            store_blocks(plan, lat_outs, mine, lanes, lat)
            key, value = nt(query[mine, lanes], ds[slot]), nt(mix[mine, lanes], encs[slot])
            if t != chosen[0]:
                key, value = key + sums[h][0], value + sums[h][1]
            elif carried:
                key, value = key + so_far[0][mine, :], value + so_far[1][mine, :]
            else:
                key = key + key_in[put, :]
            sums[h] = key, value
            if t != chosen[-1]:
                return
            key, value = sums.pop(h)
            if not carried:
                pts_outs[0][mine, :] = key
                pts_outs[1][mine, :] = value
                return
            key = (key * HEAD_DIM**-0.5).T.astype(jnp.bfloat16)
            value = value.T.astype(jnp.bfloat16)
            for j, out in enumerate(pts_outs):
                rows = slice(j * plan.rows, (j + 1) * plan.rows)
                out[:, mine] = key[rows]
                out[:, c + h * HEAD_DIM : c + (h + 1) * HEAD_DIM] = value[rows]

        work = [(h, t) for h in range(hs) for t in chosen]
        for n, place in enumerate(work):
            weigh(*place, n % SLOTS)
            if n >= LAG:
                gather(*work[n - LAG], (n - LAG) % SLOTS)
        for n in range(len(work) - LAG, len(work)):
            gather(*work[n], n % SLOTS)

    outs = [shaped((c, plan.points), jnp.float32)] * 2
    if carried:
        outs = [shaped((plan.rows, 2 * c), jnp.bfloat16)] * n_pts
    outs += [plan.stack(c)]
    scratch = [
        pltpu.VMEM((c, m), jnp.bfloat16),
        pltpu.VMEM((plan.ct_rows, m), jnp.bfloat16),
        pltpu.VMEM((c, plan.points), jnp.bfloat16),
        pltpu.VMEM((plan.points, c), jnp.bfloat16),
        pltpu.VMEM((SLOTS, plan.points, 2 * plan.block), jnp.bfloat16),
        pltpu.VMEM((SLOTS, plan.points, 2 * plan.block), jnp.bfloat16),
    ]
    flops = 5 * plan.points * m * c
    args = (*lats, *pts, *kept, *mixes, *(a for _, part in before for a in part), *(carried or ()))
    got = call(kernel, outs, args, scratch, flops)
    return got[:-1], got[-1]


def reduce_latents(plan, parts):
    def kernel(*refs):
        ins, outs = refs[: len(parts)], refs[len(parts) :]
        total = scaled_sum(*ins).T
        for j, out in enumerate(outs):
            rows = total[j * plan.lat_rows : (j + 1) * plan.lat_rows]
            n, half = plan.lat_rows, plan.lat_rows // 2
            out[:n, :] = rows[:, :LANES]
            out[n:, :] = jnp.concatenate([rows[:half, LANES:], rows[half:, LANES:]], axis=1)

    outs = [shaped((3 * plan.lat_rows // 2, LANES), jnp.float32)] * GROUPS
    return call(kernel, outs, parts)


def place_points(plan, slots):
    def kernel(*refs):
        ins, (key_out, value_out) = refs[:GROUPS], refs[GROUPS:]
        z = group_index(plan)
        c = plan.cols
        pieces = by_group([r[...].astype(jnp.float32) for r in ins], z)
        for g, piece in enumerate(pieces):
            key_out[:, g * c : (g + 1) * c] = piece[:, :c].astype(jnp.bfloat16)
            value_out[:, g * c : (g + 1) * c] = piece[:, c:].astype(jnp.bfloat16)

    outs = [shaped((plan.rows, plan.width), jnp.bfloat16)] * 2
    return call(kernel, outs, slots)


def place_latents(plan, slots):
    def kernel(*refs):
        *ins, out = refs
        n, at = plan.lat_rows, plan.cols - LANES
        for g, piece in enumerate(by_group([r[...] for r in ins], group_index(plan))):
            rest = jnp.concatenate([piece[n:, :at], piece[n:, at:]], axis=0)
            out[:, g * plan.cols : (g + 1) * plan.cols] = jnp.concatenate([piece[:n], rest], axis=1)

    outs = [shaped((plan.lat_rows, plan.width), jnp.float32)]
    return call(kernel, outs, slots)[0]


def grouped(
    plan, point_keys, point_values, out_grad, decoder_norm, latent_query, latent_out, encoder_norm
):
    def over_group(slots):
        got = [slots[0]]
        for j in range(1, GROUPS):
            got.append(plan.exchange(slots[j], True, j))
        return got

    def from_chips(blocks):
        got = []
        for k, block in zip(plan.chip_steps(), blocks, strict=True):
            got.append(plan.exchange(block, False, k) if k else block)
        return got

    def sum_cores(mine, away):
        theirs = plan.exchange(away, False, plan.fast)
        return add_and_scale(plan, mine, theirs)

    def sum_chips(blocks):
        halves = [blocks[0], *(block.astype(jnp.float16) for block in blocks[1:])]
        return [block.astype(jnp.float32) for block in from_chips(halves)]

    def to_plane(block):
        got = dict(zip(plan.chip_steps(), from_chips([block] * len(plan.chip_steps())), strict=True))
        for k in plan.chip_steps():
            got[k | plan.fast] = plan.exchange(got[k], False, plan.fast)
        return tuple(got[k] for k in range(plan.plane))

    lat_slots, pts = pack(
        plan, latent_query, latent_out, decoder_norm, point_keys, out_grad, point_values
    )
    lat_slots = over_group(lat_slots)
    pts = over_group(pts)
    norm = order_norm(plan, encoder_norm)
    block, dec_norm = turn_latents(plan, lat_slots)
    lats = to_plane(block)
    half = GROUPS // 2
    sums, kept = first_pass(plan, lats, pts[:half], 0, dec_norm, norm)
    sums, more = first_pass(plan, lats, pts[half:], half, dec_norm, norm, sums)
    kept = (kept, more)
    cores = sum_cores(*sums)
    sums = sum_chips(cores)
    every = tuple(range(plan.heads))
    before = [(every, decoder_pass(plan, lats, pts, dec_norm, every))]
    mixes = to_plane(reduce_mix(plan, sums))
    carried, lat_mine = encoder_pass(plan, lats, pts, kept, mixes, before)
    pts_out, lat_away = encoder_pass(plan, lats, pts, kept, mixes, before, carried)
    lat_out = sum_chips(sum_cores(lat_mine, lat_away))
    pts_out = over_group(pts_out)
    lat_rows = over_group(reduce_latents(plan, lat_out))
    keys_grad, values_grad = place_points(plan, pts_out)
    return keys_grad, values_grad, place_latents(plan, lat_rows)


def column(block, current):
    return lax.dynamic_slice_in_dim(block, current * HEAD_DIM, HEAD_DIM, 1)


def put_head(total, piece, current):
    return lax.dynamic_update_slice_in_dim(total, piece, current * HEAD_DIM, 1)


def add_head(total, piece, current):
    return put_head(total, column(total, current) + piece, current)


def across(left, right):
    return lax.dot_general(
        left, right, (((1,), (1,)), ((), ())), preferred_element_type=jnp.float32
    )


def down_rows(left, right):
    return lax.dot_general(
        left, right, (((0,), (0,)), ((), ())), preferred_element_type=jnp.float32
    )


def gathered(
    point_keys, point_values, out_grad, decoder_norm, latent_query, latent_out, encoder_norm
):
    scale_factor = HEAD_DIM ** (-0.5)
    lat_all, out_all = (
        lax.all_gather(latent_query, ("pa", "pb"), axis=0, tiled=True),
        lax.all_gather(latent_out, ("pa", "pb"), axis=0, tiled=True),
    )
    point_rows = point_keys.shape[0]
    latent_rows = lat_all.shape[0]
    width = point_keys.shape[1]

    def encoder_row(current):
        return lax.dynamic_slice_in_dim(encoder_norm, current, 1, 0)

    def pass_one(current, state):
        mix_acc, query_acc, key_acc, weighted_acc = state
        key_head = column(point_keys, current)
        grad_head = column(out_grad, current)
        lat_head = column(lat_all, current)
        scores = across(key_head, lat_head) * scale_factor
        decoder_weights = jnp.exp(scores - lax.dynamic_slice_in_dim(decoder_norm, current, 1, 0).T)
        decoder_gradient = across(grad_head, column(out_all, current))
        row_total = jnp.sum(decoder_weights * decoder_gradient, axis=1, keepdims=True)
        decoder_scores_grad = (decoder_weights * (decoder_gradient - row_total)).astype(
            jnp.bfloat16
        )
        mix_acc = put_head(
            mix_acc, down_rows(decoder_weights.astype(jnp.bfloat16), grad_head), current
        )
        query_acc = put_head(
            query_acc, down_rows(decoder_scores_grad, key_head) * scale_factor, current
        )
        key_acc = put_head(
            key_acc,
            jnp.dot(decoder_scores_grad, lat_head, preferred_element_type=jnp.float32)
            * scale_factor,
            current,
        )
        return (mix_acc, query_acc, key_acc, weighted_acc)

    weighted_blank = jnp.zeros((1, 1), jnp.float32)
    latent_blank = jnp.zeros((latent_rows, width), jnp.float32)
    begin = (
        latent_blank,
        latent_blank,
        jnp.zeros((point_rows, width), jnp.float32),
        weighted_blank,
    )
    mix_acc, query_acc, key_acc, _ = lax.fori_loop(0, HEADS, pass_one, begin)
    mix_grad = lax.psum(mix_acc, ("pa", "pb"))
    mixing_portion = mix_grad.astype(jnp.bfloat16)

    def pass_two(current, state):
        partial_rows, value_acc = state
        scores = across(column(point_keys, current), column(lat_all, current)) * scale_factor
        encoder_portion = jnp.exp(scores - encoder_row(current)).astype(jnp.bfloat16)
        mix_head = column(mixing_portion, current)
        encoder_gradient = across(column(point_values, current), mix_head)
        sums = jnp.sum(encoder_portion.astype(jnp.float32) * encoder_gradient, axis=0)[None, :]
        partial_rows = lax.dynamic_update_slice_in_dim(partial_rows, sums, current, 0)
        value_acc = put_head(
            value_acc,
            jnp.dot(encoder_portion, mix_head, preferred_element_type=jnp.float32),
            current,
        )
        return (partial_rows, value_acc)

    partial_rows, value_acc = lax.fori_loop(
        0,
        HEADS,
        pass_two,
        (jnp.zeros((HEADS, latent_rows), jnp.float32), jnp.zeros((point_rows, width), jnp.float32)),
    )
    column_total = lax.psum(partial_rows, ("pa", "pb"))

    def pass_three(current, state):
        query_acc, key_acc, value_acc = state
        key_head = column(point_keys, current)
        lat_head = column(lat_all, current)
        mix_head = column(mixing_portion, current)
        scores = across(key_head, lat_head) * scale_factor
        encoder = jnp.exp(scores - encoder_row(current))
        encoder_gradient = across(column(point_values, current), mix_head)
        encoder_scores_grad = (
            encoder * (encoder_gradient - lax.dynamic_slice_in_dim(column_total, current, 1, 0))
        ).astype(jnp.bfloat16)
        query_acc = add_head(
            query_acc, down_rows(encoder_scores_grad, key_head) * scale_factor, current
        )
        key_acc = add_head(
            key_acc,
            jnp.dot(encoder_scores_grad, lat_head, preferred_element_type=jnp.float32)
            * scale_factor,
            current,
        )
        return (query_acc, key_acc, value_acc)

    query_acc, key_acc, value_acc = lax.fori_loop(
        0, HEADS, pass_three, (query_acc, key_acc, value_acc)
    )
    latent_grad = lax.psum_scatter(query_acc, ("pa", "pb"), scatter_dimension=0, tiled=True)
    return (key_acc.astype(jnp.bfloat16), value_acc.astype(jnp.bfloat16), latent_grad)


def solution(mesh):
    in_specs = (
        P(("pa", "pb"), None),
        P(("pa", "pb"), None),
        P(("pa", "pb"), None),
        P(None, ("pa", "pb")),
        P(("pa", "pb"), None),
        P(("pa", "pb"), None),
        P(),
    )
    out_specs = (P(("pa", "pb"), None), P(("pa", "pb"), None), P(("pa", "pb"), None))
    npa, npb = mesh.shape["pa"], mesh.shape["pb"]

    def shards(*args):
        plan_of = (npa, npb, args[0].shape[0], args[4].shape[0], args[0].shape[1])
        if Plan.fits(*plan_of):
            return grouped(Plan(*plan_of), *args)
        return gathered(*args)

    return jax.shard_map(shards, mesh=mesh, in_specs=in_specs, out_specs=out_specs, check_vma=False)
```
